32 devices in a mesh: group: 2 (over y), ctx: 4 (over z), smp: 2 (over x), head: 2 (over core).
Axes of the slice: x: 2, y: 2, z: 4, core: 2. Of those that a mesh axis runs over, the one named last changes fastest.
Arguments:
- queries: bfloat16 [512, 2, 4096], P(('group', 'smp'), 'head'), parts along dimension 0, may hold values from -8 to 8
- prefix_cache: bfloat16 [2, 8192, 2, 512], P(None, ('group', 'ctx'), 'head'), parts along dimension 1, may hold values from -8 to 8
- suffix_cache: bfloat16 [2, 512, 128, 2, 512], P(None, ('group', 'ctx', 'smp'), None, 'head'), parts along dimension 1, may hold values from -8 to 8
- suffix_length: int32 [512], P(('group', 'smp')), parts along dimension 0, may hold values from 1 to 128, as said below
- cache_sample: int32 [512], P('group'), parts along dimension 0, may hold values from 0 to 255, as said below
- residual: bfloat16 [512, 8192], P(('group', 'ctx', 'head'), 'smp'), parts along dimension 0, may hold values from -6 to 6
- w_out: bfloat16 [2, 4096, 8192], P('head', 'ctx', 'smp'), may hold values from -0.75 to 0.75
- norm_gain: float32 [8192], P('smp'), may hold values from 0.1 to 1.9
- gate_matrix: bfloat16 [8192, 16384], P('smp', ('ctx', 'head')), may hold values from -0.0625 to 0.0625
- w_up: bfloat16 [8192, 16384], P('smp', ('ctx', 'head')), may hold values from -0.0625 to 0.0625
- w_down: bfloat16 [16384, 8192], P(('ctx', 'head'), 'smp'), may hold values from -0.046875 to 0.046875
Outputs:
- mixed: bfloat16 [512, 8192], P(('group', 'ctx', 'head'), 'smp'), parts along dimension 0
The draws below stay inside these ranges and needn't reach their ends.
There are 2 independent parts, one for each index of `group`. The reference program is written for one: setup_inputs(seed, part) draws one part's arguments, and reference() takes and returns one part's arrays. A program takes and returns all parts, laid end to end along the dimension named above; an argument that names none is the same for every part. Nothing has to cross between parts.
Inputs may be any that keep to these rules, and one draw needn't show every extreme that they name: `suffix_length`: the longest is exactly 128 in every draw. A permutation; cache row r and sample cache_sample[r] lie in the same group, the group of row r being (r // 32) % (2) and that of sample i being i // 128.
All inputs are finite; a program needn't handle non-finite values.
Results may differ from the reference program's by a relative error of at most 0.012.
Values may be sent and summed in bfloat16 or wider, within the bound.
A program may use at most 192 MiB of HBM per device.

```python
import jax
import jax.numpy as jnp
from jax import lax

D = 8192
QUERY_HEADS = 64
KEY_VALUE_HEADS = 8
HD = 128
FF = 16384
SAMP_GRP = 128
PRE_DEV = 1024
SUFFIX = 128
HEAD_GROUP_COUNT = 2
QW = 4096
KVW = 512
PREFIX = 4096
SAMPLES = 256
ROWS_DEV = 32
N_CTX = 4


def drawn_draw(key):
    query_key = jax.random.fold_in(key, 11)
    cache_key = jax.random.fold_in(key, 12)
    value_key = jax.random.fold_in(key, 13)
    query_shape = (SAMPLES, HEAD_GROUP_COUNT, QW)
    cache_shape = (PREFIX, HEAD_GROUP_COUNT, KVW)
    queries = jnp.clip(jax.random.normal(query_key, query_shape, jnp.float32), -6.0, 6.0)
    prefix_keys = jnp.clip(1.5 * jax.random.normal(cache_key, cache_shape, jnp.float32), -8.0, 8.0)
    prefix_values = jnp.clip(jax.random.normal(value_key, cache_shape, jnp.float32), -6.0, 6.0)
    return (queries, jnp.stack([prefix_keys, prefix_values]))


def draw_queries(key, part):
    return drawn_draw(key)[0].astype(jnp.bfloat16)


def draw_prefix_cache(key, part):
    return drawn_draw(key)[1].astype(jnp.bfloat16)


def draw_suffix_length(key, part):
    lengths = jax.random.randint(jax.random.fold_in(key, 21), (SAMPLES,), 1, SUFFIX + 1)
    longest = jax.random.randint(jax.random.fold_in(key, 22), (), 0, SAMPLES)
    return lengths.at[longest].set(SUFFIX).astype(jnp.int32)


def draw_cache_sample(key, part):
    groups = SAMPLES // SAMP_GRP
    row_ids = jnp.arange(SAMPLES, dtype=jnp.int32)
    group_of_row = row_ids // ROWS_DEV % groups
    rank = row_ids // (ROWS_DEV * groups) * ROWS_DEV + row_ids % ROWS_DEV
    orders = jnp.stack([jax.random.permutation(jax.random.fold_in(key, 31 + number), SAMP_GRP) for number in range(groups)])
    return (group_of_row * SAMP_GRP + orders[group_of_row, rank]).astype(jnp.int32)


def draw_suffix_cache(key, part):
    cache_shape = (2, SAMPLES, SUFFIX, HEAD_GROUP_COUNT, KVW)
    cache_key = jax.random.fold_in(key, 41)
    cache = jnp.clip(3.0 * jax.random.normal(cache_key, cache_shape, jnp.float32), -5.0, 5.0)
    return cache.astype(jnp.bfloat16)


def levels(stream_key, dims, cuts, smallest, top_value):
    factor_of = 1.0
    for axis_at, blocks in cuts:
        draws = jax.random.uniform(jax.random.fold_in(jax.random.fold_in(stream_key, 6), axis_at), (blocks,), jnp.float32, smallest / len(cuts), top_value / len(cuts))
        factor_of = factor_of * jnp.repeat(jnp.exp(draws), dims[axis_at] // blocks).reshape((-1,) + (1,) * (len(dims) - 1 - axis_at))
    return factor_of


def normal_values(own_key, extent, spread, limit, pieces=(), kind=jnp.bfloat16):
    entries = spread * jax.random.normal(own_key, extent, jnp.float32)
    if pieces:
        entries = entries * levels(own_key, extent, pieces, -0.22, 0.18)
    return jnp.clip(entries, -limit, limit).astype(kind)


def setup_inputs(seed: int = 0, part: int = 0) -> dict:
    arg_keys = jax.random.split(jax.random.key(seed), 12)
    part_splits = jax.random.split(jax.random.fold_in(arg_keys[11], part), 12)
    return {
        "queries": draw_queries(jax.random.fold_in(jax.random.fold_in(arg_keys[11], part), 71), part),
        "prefix_cache": draw_prefix_cache(jax.random.fold_in(jax.random.fold_in(arg_keys[11], part), 71), part),
        "suffix_cache": draw_suffix_cache(jax.random.fold_in(jax.random.fold_in(arg_keys[11], part), 71), part),
        "suffix_length": draw_suffix_length(jax.random.fold_in(jax.random.fold_in(arg_keys[11], part), 71), part),
        "cache_sample": draw_cache_sample(jax.random.fold_in(jax.random.fold_in(arg_keys[11], part), 71), part),
        "residual": normal_values(part_splits[5], (SAMPLES, D), 1.0, 6.0, ((0, 8), (1, 2))),
        "w_out": normal_values(arg_keys[6], (HEAD_GROUP_COUNT, QW, D), (QUERY_HEADS * HD // 128) ** -0.5, 0.75, ((0, 2), (1, 4), (2, 2))),
        "norm_gain": jnp.clip(1.0 + 0.18 * jax.random.normal(arg_keys[7], (D,), jnp.float32), 0.1, 1.9),
        "gate_matrix": normal_values(arg_keys[8], (D, FF), D ** -0.5, 0.0625, ((0, 2), (1, 8))),
        "w_up": normal_values(arg_keys[9], (D, FF), D ** -0.5, 0.0625, ((0, 2), (1, 8))),
        "w_down": normal_values(arg_keys[10], (FF, D), FF ** -0.5, 0.046875, ((0, 8), (1, 2))),
    }


EPSILON = 1e-05

def finish_piece(scores, values, form):
    highest = lax.optimization_barrier(jnp.max(scores, axis=-1))
    weights = jnp.exp(scores - highest[..., None])
    totals = lax.optimization_barrier(jnp.sum(weights, axis=-1))
    rounded = lax.optimization_barrier(weights.astype(jnp.bfloat16)).astype(jnp.float32)
    summed = jnp.einsum(form, rounded, values)
    piece_out = (summed / totals[..., None]).astype(jnp.bfloat16)
    return (piece_out, highest + jnp.log(totals))

def reference(queries, prefix_cache, suffix_cache, suffix_length, cache_sample, residual, w_out, norm_gain, gate_matrix, w_up, w_down):
    key_value_heads_here = KEY_VALUE_HEADS // HEAD_GROUP_COUNT
    queries_per_key_value = QUERY_HEADS // KEY_VALUE_HEADS
    score_scale = HD ** (-0.5)
    query_rows = queries.astype(jnp.float32).reshape(SAMPLES, HEAD_GROUP_COUNT, key_value_heads_here, queries_per_key_value, HD)
    prefix_keys = prefix_cache[0].astype(jnp.float32).reshape(PREFIX, HEAD_GROUP_COUNT, key_value_heads_here, HD)
    prefix_values = prefix_cache[1].astype(jnp.float32).reshape(PREFIX, HEAD_GROUP_COUNT, key_value_heads_here, HD)

    def block_piece(block):
        start_pos = (block * PRE_DEV).astype(jnp.int32)
        block_keys = lax.dynamic_slice_in_dim(prefix_keys, start_pos, PRE_DEV, 0)
        block_values = lax.dynamic_slice_in_dim(prefix_values, start_pos, PRE_DEV, 0)
        scores = jnp.einsum('shjgd,phjd->shjgp', query_rows, block_keys) * score_scale
        return finish_piece(scores, block_values, 'shjgp,phjd->shjgd')
    block_out, block_lse = lax.map(block_piece, jnp.arange(N_CTX, dtype=jnp.int32))
    row_of = jnp.zeros((SAMPLES,), jnp.int32).at[cache_sample].set(jnp.arange(SAMPLES, dtype=jnp.int32))
    own_cache = jnp.take(suffix_cache, row_of, axis=1)
    suffix_keys = own_cache[0].astype(jnp.float32).reshape(SAMPLES, SUFFIX, HEAD_GROUP_COUNT, key_value_heads_here, HD)
    suffix_values = own_cache[1].astype(jnp.float32).reshape(SAMPLES, SUFFIX, HEAD_GROUP_COUNT, key_value_heads_here, HD)
    suffix_scores = jnp.einsum('shjgd,sthjd->shjgt', query_rows, suffix_keys) * score_scale
    positions = lax.broadcasted_iota(jnp.int32, suffix_scores.shape, 4)
    live = positions < suffix_length.astype(jnp.int32)[:, None, None, None, None]
    suffix_scores = jnp.where(live, suffix_scores, -jnp.inf)
    suffix_out, suffix_lse = finish_piece(suffix_scores, suffix_values, 'shjgt,sthjd->shjgd')
    all_out = jnp.concatenate([block_out, suffix_out[None]], axis=0)
    all_out = lax.optimization_barrier(all_out).astype(jnp.float32)
    all_lse = jnp.concatenate([block_lse, suffix_lse[None]], axis=0)
    top = lax.optimization_barrier(jnp.max(all_lse, axis=0))
    piece_weights = jnp.exp(all_lse - top[None])
    numer = lax.optimization_barrier(jnp.sum(piece_weights[..., None] * all_out, axis=0))
    denom = lax.optimization_barrier(jnp.sum(piece_weights, axis=0))
    attention = (numer / denom[..., None]).astype(jnp.bfloat16).reshape(SAMPLES, HEAD_GROUP_COUNT * QW)
    projected = jnp.dot(attention, w_out.reshape(HEAD_GROUP_COUNT * QW, D), preferred_element_type=jnp.float32)
    state = (residual.astype(jnp.float32) + projected).astype(jnp.bfloat16)
    state_wide = lax.optimization_barrier(state).astype(jnp.float32)
    inverse_rms = lax.rsqrt(lax.optimization_barrier(jnp.mean(state_wide * state_wide, axis=1)) + EPSILON)
    scaled = (state_wide * norm_gain).astype(jnp.bfloat16)
    gate = inverse_rms[:, None] * jnp.dot(scaled, gate_matrix, preferred_element_type=jnp.float32)
    up_part = inverse_rms[:, None] * jnp.dot(scaled, w_up, preferred_element_type=jnp.float32)
    hidden = (jax.nn.silu(gate) * up_part).astype(jnp.bfloat16)
    return (state_wide + jnp.dot(hidden, w_down, preferred_element_type=jnp.float32)).astype(jnp.bfloat16)
```

```python
import functools

import jax
import jax.numpy as jnp
from jax import lax
from jax.experimental import pallas as pl
from jax.experimental.pallas import tpu as pltpu
from jax.sharding import PartitionSpec as P

D = 8192
QUERY_HEADS = 64
KEY_VALUE_HEADS = 8
HD = 128


EPSILON = 1e-05


def suffix_kernel(lengths_ref, queries_ref, cache_ref, out_ref, lse_ref):
    block, heads, _ = queries_ref.shape
    positions_here, width = cache_ref.shape[2:]
    per_key = heads // (width // HD)
    first = pl.program_id(0) * block
    same = (
        lax.broadcasted_iota(jnp.int32, (heads, width), 0) // per_key
        == lax.broadcasted_iota(jnp.int32, (heads, width), 1) // HD
    )
    positions = lax.broadcasted_iota(jnp.int32, (heads, positions_here), 1)
    for r in range(block):
        q = queries_ref[r].astype(jnp.float32)
        spread = jnp.concatenate([q] * (width // HD), axis=1)
        spread = jnp.where(same, spread, 0.0).astype(jnp.bfloat16)
        scores = lax.dot_general(
            spread, cache_ref[0, r], (((1,), (1,)), ((), ())), preferred_element_type=jnp.float32
        )
        scores = jnp.where(positions < lengths_ref[first + r], scores * HD ** (-0.5), -jnp.inf)
        high = jnp.max(scores, axis=1, keepdims=True)
        weights = jnp.exp(scores - high)
        total = jnp.sum(weights, axis=1, keepdims=True)
        summed = jnp.dot(
            weights.astype(jnp.bfloat16), cache_ref[1, r], preferred_element_type=jnp.float32
        )
        own = jnp.concatenate(
            [
                summed[j * per_key : (j + 1) * per_key, j * HD : (j + 1) * HD]
                for j in range(width // HD)
            ],
            axis=0,
        )
        out_ref[r] = (own / total).astype(jnp.bfloat16)
        lse_ref[r] = high + jnp.log(total)


def suffix_piece(row_queries, suffix_cache, row_lengths):
    rows, heads, _ = row_queries.shape
    block = min(8, rows)
    _, _, positions_here, width = suffix_cache.shape
    return pl.pallas_call(
        suffix_kernel,
        grid=(rows // block,),
        out_shape=(
            jax.ShapeDtypeStruct((rows, heads, HD), jnp.bfloat16),
            jax.ShapeDtypeStruct((rows, heads, 1), jnp.float32),
        ),
        in_specs=[
            pl.BlockSpec(memory_space=pltpu.SMEM),
            pl.BlockSpec((block, heads, HD), lambda i: (i, 0, 0)),
            pl.BlockSpec((2, block, positions_here, width), lambda i: (0, i, 0, 0)),
        ],
        out_specs=(
            pl.BlockSpec((block, heads, HD), lambda i: (i, 0, 0)),
            pl.BlockSpec((block, heads, 1), lambda i: (i, 0, 0)),
        ),
        compiler_params=pltpu.CompilerParams(vmem_limit_bytes=57 * 1024 * 1024),
    )(row_lengths, row_queries, suffix_cache)


MESH = pl.DeviceIdType.MESH
TILE = 512
VMEM_BYTES = 62 * 1024 * 1024


def remote(src, dst, send_sem, recv_sem, where):
    return pltpu.make_async_remote_copy(
        src_ref=src,
        dst_ref=dst,
        send_sem=send_sem,
        recv_sem=recv_sem,
        device_id=where,
        device_id_type=MESH,
    )


def greet(n, n_smp, c, s, h):
    barrier = pltpu.get_barrier_semaphore()
    for k in range(1, n):
        pl.semaphore_signal(barrier, inc=1, device_id={"ctx": lax.rem(c + k, n)}, device_id_type=MESH)
    for k in range(1, n_smp):
        pl.semaphore_signal(
            barrier, inc=1, device_id={"smp": lax.rem(s + k, n_smp)}, device_id_type=MESH
        )
    pl.semaphore_signal(barrier, inc=1, device_id={"head": 1 - h}, device_id_type=MESH)
    pl.semaphore_wait(barrier, (n - 1) + (n_smp - 1) + 1)


class Line:
    def __init__(self, n, c, h, buf_a, recv_a, buf_b, from_left, from_right, sa, ra, ss, rl, rr):
        self.n, self.c, self.h = n, c, h
        self.buf_a, self.recv_a, self.buf_b = buf_a, recv_a, buf_b
        self.from_left, self.from_right = from_left, from_right
        self.sa, self.ra, self.ss, self.rl, self.rr = sa, ra, ss, rl, rr
        self.tiles = buf_a.shape[0]

        @pl.when(c == 0)
        def _():
            from_left[:, 0] = jnp.zeros(from_left.shape[:1] + from_left.shape[2:], from_left.dtype)

        @pl.when(c == n - 1)
        def _():
            from_right[:, n - 1] = jnp.zeros(
                from_right.shape[:1] + from_right.shape[2:], from_right.dtype
            )

    def pair_copy(self, t):
        return remote(
            self.buf_a.at[t, 1 - self.h],
            self.recv_a.at[t],
            self.sa.at[t],
            self.ra.at[t],
            {"head": 1 - self.h},
        )

    def to_right(self, t, d):
        return remote(
            self.buf_b.at[t, d],
            self.from_left.at[t, d],
            self.ss.at[t, d],
            self.rl.at[t, d],
            {"ctx": lax.rem(self.c + 1, self.n)},
        )

    def to_left(self, t, d):
        return remote(
            self.buf_b.at[t, d],
            self.from_right.at[t, d],
            self.ss.at[t, d],
            self.rr.at[t, d],
            {"ctx": lax.rem(self.c + self.n - 1, self.n)},
        )

    def give(self, t, value):
        _, _, n, rows, width = self.buf_a.shape
        parts = value.reshape(n, 2, rows, width).astype(jnp.bfloat16)
        self.buf_a[t, 0] = parts[:, 0]
        self.buf_a[t, 1] = parts[:, 1]
        self.pair_copy(t).start()

    def middle(self, t):
        self.pair_copy(t).wait()
        both = self.buf_a[t, self.h].astype(jnp.float32) + self.recv_a[t].astype(jnp.float32)
        self.buf_b[t] = both.astype(jnp.bfloat16)

    def hop(self, t, inside, d, copy_of, arrived, first):
        @pl.when(inside & (t >= 0) & (t < self.tiles))
        def _():
            @pl.when(jnp.logical_not(first))
            def _():
                copy_of(t, d).wait_recv()
                both = self.buf_b[t, d].astype(jnp.float32) + arrived[t, d].astype(jnp.float32)
                self.buf_b[t, d] = both.astype(jnp.bfloat16)

            copy_of(t, d).start()

    def step(self, i):
        n, c = self.n, self.c

        @pl.when((i >= 1) & (i <= self.tiles))
        def _():
            self.middle(i - 1)

        for e in range(n - 1):
            right, left = n - 1 - e, e
            self.hop(i - 1 - c, right > c, right, self.to_right, self.from_left, c == 0)
            self.hop(i - n + c, left < c, left, self.to_left, self.from_right, c == n - 1)

    def finish(self, t):
        n, c = self.n, self.c

        @pl.when(c > 0)
        def _():
            self.to_right(t, c).wait_recv()

        @pl.when(c < n - 1)
        def _():
            self.to_left(t, c).wait_recv()

        return (
            self.buf_b[t, c].astype(jnp.float32)
            + self.from_left[t, c].astype(jnp.float32)
            + self.from_right[t, c].astype(jnp.float32)
        )

    def drain(self, t):
        for d in range(self.n):

            @pl.when(d > self.c)
            def _():
                self.to_right(t, d).wait_send()

            @pl.when(d < self.c)
            def _():
                self.to_left(t, d).wait_send()


class Scatter:
    def __init__(self, n, c, h, buf_a, recv_a, buf_b, recv_b, sa, ra, sb, rb):
        self.n, self.c, self.h = n, c, h
        self.buf_a, self.recv_a, self.buf_b, self.recv_b = buf_a, recv_a, buf_b, recv_b
        self.sa, self.ra, self.sb, self.rb = sa, ra, sb, rb

    def pair_copy(self, t):
        return remote(
            self.buf_a.at[t, 1 - self.h],
            self.recv_a.at[t],
            self.sa.at[t],
            self.ra.at[t],
            {"head": 1 - self.h},
        )

    def row_copy(self, t, k):
        d = lax.rem(self.c + k, self.n)
        return remote(
            self.buf_b.at[t, d],
            self.recv_b.at[t, k - 1],
            self.sb.at[t, k - 1],
            self.rb.at[t, k - 1],
            {"ctx": d},
        )

    def give(self, t, value):
        _, _, n, rows, width = self.buf_a.shape
        parts = value.reshape(n, 2, rows, width).astype(jnp.bfloat16)
        self.buf_a[t, 0] = parts[:, 0]
        self.buf_a[t, 1] = parts[:, 1]
        self.pair_copy(t).start()

    def middle(self, t):
        self.pair_copy(t).wait()
        both = self.buf_a[t, self.h].astype(jnp.float32) + self.recv_a[t].astype(jnp.float32)
        self.buf_b[t] = both.astype(jnp.bfloat16)
        for k in range(1, self.n):
            self.row_copy(t, k).start()

    def finish(self, t):
        total = self.buf_b[t, self.c].astype(jnp.float32)
        for k in range(1, self.n):
            self.row_copy(t, k).wait()
            total = total + self.recv_b[t, k - 1].astype(jnp.float32)
        return total


def columns(t, width):
    return pl.ds(pl.multiple_of(t * width, width), width)


def proj_kernel(
    n,
    n_smp,
    q_ref,
    kv_ref,
    suf_ref,
    suf_lse_ref,
    w_ref,
    res_ref,
    state_ref,
    out_mine,
    lse_mine,
    out_in,
    lse_in,
    attn,
    w_buf,
    buf_a,
    recv_a,
    buf_b,
    from_left,
    from_right,
    w_sem,
    os,
    orr,
    ls,
    lr,
    xs,
    xr,
    sa,
    ra,
    ss,
    rl,
    rr,
    gsr,
    gsl,
    gr,
    fs,
    fr,
):
    c, s, h = lax.axis_index("ctx"), lax.axis_index("smp"), lax.axis_index("head")
    tiles = w_buf.shape[0]
    keys, samples, per_key = suf_lse_ref.shape
    per_dest = out_mine.shape[2] // HD
    dests = per_key // per_dest
    together = 4

    greet(n, n_smp, c, s, h)

    def piece_copies(at, d):
        return (
            remote(out_mine.at[d], out_in.at[at], os.at[d], orr.at[at], {"ctx": d}),
            remote(lse_mine.at[d], lse_in.at[at], ls.at[d], lr.at[at], {"ctx": d}),
        )

    def w_copy(t):
        return pltpu.make_async_copy(w_ref.at[:, columns(t, TILE)], w_buf.at[t], w_sem.at[t])

    @pl.loop(0, tiles)
    def _(t):
        w_copy(t).start()

    lanes_at = lax.broadcasted_iota(jnp.int32, (samples, 128), 1)

    @pl.loop(0, keys)
    def _(i):
        j = lax.rem(lax.div(c, dests) + 1 + i, keys)
        key = kv_ref[0, :, columns(j, HD)]
        value = kv_ref[1, :, columns(j, HD)]
        own = q_ref[:, columns(j, per_key * HD)]
        placed = suf_ref[:, columns(j, per_key * HD)]
        placed_lse = suf_lse_ref[j]
        tables = [jnp.zeros((samples, 128), jnp.float32) for _ in range(dests)]
        for g0 in range(0, per_key, together):
            rows = jnp.concatenate(
                [own[:, g * HD : (g + 1) * HD] for g in range(g0, g0 + together)], axis=0
            )
            scores = lax.dot_general(
                rows, key, (((1,), (1,)), ((), ())), preferred_element_type=jnp.float32
            ) * HD ** (-0.5)
            high = jnp.max(scores, axis=1, keepdims=True)
            weights = jnp.exp(scores - high)
            total = jnp.sum(weights, axis=1, keepdims=True)
            summed = (
                jnp.dot(weights.astype(jnp.bfloat16), value, preferred_element_type=jnp.float32)
                / total
            )
            lse = high + jnp.log(total)
            for g in range(g0, g0 + together):
                part = slice((g - g0) * samples, (g - g0 + 1) * samples)
                own_lse, other_lse = lse[part], placed_lse[:, g : g + 1]
                top = jnp.maximum(own_lse, other_lse)
                own_weight = jnp.exp(own_lse - top)
                other_weight = jnp.exp(other_lse - top)
                both = own_weight + other_weight
                merged = (
                    own_weight * summed[part]
                    + other_weight * placed[:, g * HD : (g + 1) * HD].astype(jnp.float32)
                ) / both
                at = g % per_dest
                out_mine[j * dests + g // per_dest, :, at * HD : (at + 1) * HD] = merged.astype(
                    jnp.bfloat16
                )
                q = g // per_dest
                tables[q] = jnp.where(lanes_at == at, top + jnp.log(both), tables[q])
        for q in range(dests):
            d = j * dests + q
            lse_mine[d] = tables[q].T[:8]

            @pl.when(d != c)
            def _():
                for copy in piece_copies(c, d):
                    copy.start()

    for k in range(1, n):
        d = lax.rem(c + k, n)
        for copy in piece_copies(d, d):
            copy.wait_recv()
    for k in range(1, n):
        d = lax.rem(c + k, n)
        for copy in piece_copies(c, d):
            copy.wait_send()

    lses = [lse_mine[c]] + [lse_in[lax.rem(c + k, n)] for k in range(1, n)]
    peak = functools.reduce(jnp.maximum, lses)
    scales = [jnp.exp(value - peak) for value in lses]
    denom = functools.reduce(jnp.add, scales)
    blank = jnp.zeros((120, samples), jnp.float32)
    scales = [jnp.concatenate([value / denom, blank], axis=0).T for value in scales]
    for j in range(per_dest):
        lanes = slice(j * HD, (j + 1) * HD)
        total = scales[0][:, j : j + 1] * out_mine[c, :, lanes].astype(jnp.float32)
        for k in range(1, n):
            piece = out_in[lax.rem(c + k, n), :, lanes].astype(jnp.float32)
            total = total + scales[k][:, j : j + 1] * piece
        attn[s, :, lanes] = total.astype(jnp.bfloat16)

    def attn_copy(k):
        return remote(
            attn.at[s], attn.at[s], xs.at[k - 1], xr.at[k - 1], {"smp": lax.rem(s + k, n_smp)}
        )

    for k in range(1, n_smp):
        attn_copy(k).start()
    for k in range(1, n_smp):
        attn_copy(k).wait()

    line = Line(n, c, h, buf_a, recv_a, buf_b, from_left, from_right, sa, ra, ss, rl, rr)

    def gather_copy(t, q, way, sems):
        block = state_ref.at[q, h, :, columns(t, TILE)]
        return remote(
            block, block, sems.at[t, q], gr.at[t, q], {"ctx": lax.rem(c + way, n)}
        )

    def pass_copy(t, q):
        block = state_ref.at[q, h, :, columns(t, TILE)]
        return remote(block, block, fs.at[t, q], fr.at[t, q], {"head": 1 - h})

    def spread(t, q, right, left):
        @pl.when(right & (c < n - 1))
        def _():
            gather_copy(t, q, 1, gsr).start()

        @pl.when(left & (c > 0))
        def _():
            gather_copy(t, q, n - 1, gsl).start()

        pass_copy(t, q).start()

    @pl.loop(0, tiles + 2 * n - 1)
    def _(i):
        @pl.when(i < tiles)
        def _():
            w_copy(i).wait()
            rows = attn[...].reshape(-1, attn.shape[2])
            line.give(i, jnp.dot(rows, w_buf[i], preferred_element_type=jnp.float32))

        line.step(i)

        @pl.when((i >= n) & (i < tiles + n))
        def _():
            t = i - n
            own = line.finish(t) + res_ref[:, columns(t, TILE)].astype(jnp.float32)
            state_ref[c, h, :, columns(t, TILE)] = own.astype(jnp.bfloat16)
            spread(t, c, c >= 0, c >= 0)

        for q in range(n):
            t = i - n - lax.max(c - q, q - c)

            @pl.when((q != c) & (t >= 0) & (t < tiles))
            def _():
                gather_copy(t, q, 1, gsr).wait_recv()
                spread(t, q, q < c, q > c)

    @pl.loop(0, tiles)
    def _(t):
        line.drain(t)
        for q in range(n):

            @pl.when((q <= c) & (c < n - 1))
            def _():
                gather_copy(t, q, 1, gsr).wait_send()

            @pl.when((q >= c) & (c > 0))
            def _():
                gather_copy(t, q, n - 1, gsl).wait_send()

            pass_copy(t, q).wait()


def project(n, n_smp, queries, prefix_cache, suffix_out, suffix_lse, w, residual):
    keys, samples, per_key = suffix_lse.shape
    features = queries.shape[1] // n
    rows, width = residual.shape
    tiles = width // TILE
    vmem = pl.BlockSpec(memory_space=pltpu.VMEM)
    dma = pltpu.SemaphoreType.DMA
    bf16 = jnp.bfloat16
    return pl.pallas_call(
        functools.partial(proj_kernel, n, n_smp),
        out_shape=jax.ShapeDtypeStruct((n, 2, rows, width), bf16),
        in_specs=[vmem, vmem, vmem, vmem, pl.BlockSpec(memory_space=pl.ANY), vmem],
        out_specs=vmem,
        scratch_shapes=[
            pltpu.VMEM((n, samples, features), bf16),
            pltpu.VMEM((n, 8, samples), jnp.float32),
            pltpu.VMEM((n, samples, features), bf16),
            pltpu.VMEM((n, 8, samples), jnp.float32),
            pltpu.VMEM((n_smp, samples, features), bf16),
            pltpu.VMEM((tiles, w.shape[0], TILE), bf16),
            pltpu.VMEM((tiles, 2, n, rows, TILE), bf16),
            pltpu.VMEM((tiles, n, rows, TILE), bf16),
            pltpu.VMEM((tiles, n, rows, TILE), bf16),
            pltpu.VMEM((tiles, n, rows, TILE), bf16),
            pltpu.VMEM((tiles, n, rows, TILE), bf16),
            dma((tiles,)),
            dma((n,)),
            dma((n,)),
            dma((n,)),
            dma((n,)),
            dma((n_smp - 1,)),
            dma((n_smp - 1,)),
            dma((tiles,)),
            dma((tiles,)),
            dma((tiles, n)),
            dma((tiles, n)),
            dma((tiles, n)),
            dma((tiles, n)),
            dma((tiles, n)),
            dma((tiles, n)),
            dma((tiles, n)),
            dma((tiles, n)),
        ],
        compiler_params=pltpu.CompilerParams(
            collective_id=0, has_side_effects=True, vmem_limit_bytes=VMEM_BYTES
        ),
    )(queries, prefix_cache, suffix_out, suffix_lse, w, residual)


UNITS = 256
SLOTS = 4
DOWN_TILE = 1024
SUB = 16


def ffn_kernel(
    n,
    n_smp,
    state_ref,
    gain_ref,
    gate_ref,
    up_ref,
    down_ref,
    mixed_ref,
    scaled,
    squares,
    squares_in,
    gate_buf,
    up_buf,
    down_buf,
    part,
    part_in,
    hidden,
    buf_a,
    recv_a,
    buf_b,
    from_left,
    from_right,
    g_sem,
    u_sem,
    d_sem,
    qs,
    qr,
    ps,
    pr,
    hs,
    hr,
    sa,
    ra,
    ss,
    rl,
    rr,
):
    c, s, h = lax.axis_index("ctx"), lax.axis_index("smp"), lax.axis_index("head")
    slots, width, _ = gate_buf.shape
    tiles, units, down_tile = down_buf.shape
    subsets, sub_rows, _ = scaled.shape
    sub = state_ref.shape[2] // subsets
    smp_rows = sub_rows // n_smp
    steps = units // UNITS
    all_steps, all_tiles = subsets * steps, subsets * tiles
    ratio = max(1, steps // tiles)

    def weight_copies(i):
        slot, t = lax.rem(i, slots), lax.rem(i, steps)
        return (
            pltpu.make_async_copy(
                gate_ref.at[:, columns(t, UNITS)], gate_buf.at[slot], g_sem.at[slot]
            ),
            pltpu.make_async_copy(up_ref.at[:, columns(t, UNITS)], up_buf.at[slot], u_sem.at[slot]),
        )

    def down_copy(t):
        return pltpu.make_async_copy(
            down_ref.at[:, columns(t, down_tile)], down_buf.at[t], d_sem.at[t]
        )

    @pl.loop(0, min(slots, all_steps))
    def _(t):
        for copy in weight_copies(t):
            copy.start()

    greet(n, n_smp, c, s, h)

    def smp_rows_of(p):
        return pl.ds(pl.multiple_of(p * smp_rows, smp_rows), smp_rows)

    def square_copy(k, m):
        p = lax.rem(s + m, n_smp)
        return remote(
            squares.at[k, smp_rows_of(p)],
            squares_in.at[k, m - 1],
            qs.at[k, m - 1],
            qr.at[k, m - 1],
            {"smp": p},
        )

    def prepare(k):
        own = pl.ds(pl.multiple_of(k * sub, sub), sub)
        for block in range(n):
            for core in range(2):
                wide = state_ref[block, core, own].astype(jnp.float32)
                first = (2 * block + core) * sub
                rows = slice(first, first + sub)
                scaled[k, rows] = (wide * gain_ref[...]).astype(jnp.bfloat16)
                sums = jnp.sum(wide * wide, axis=1, keepdims=True)
                squares[k, rows] = jnp.broadcast_to(sums, (sub, 128))
        for m in range(1, n_smp):
            square_copy(k, m).start()

    def part_copy(i, m):
        p = lax.rem(s + m, n_smp)
        return remote(
            part.at[i, smp_rows_of(p)],
            part_in.at[i, m - 1],
            ps.at[i, m - 1],
            pr.at[i, m - 1],
            {"smp": p},
        )

    def hidden_copy(i, m):
        k, t = lax.div(i, steps), lax.rem(i, steps)
        block = hidden.at[k, smp_rows_of(s), columns(t, UNITS)]
        return remote(
            block, block, hs.at[i, m - 1], hr.at[i, m - 1], {"smp": lax.rem(s + m, n_smp)}
        )

    def act(i):
        k, t = lax.div(i, steps), lax.rem(i, steps)

        @pl.when(t == 0)
        def _():
            for m in range(1, n_smp):
                square_copy(k, m).wait()

        both = part[i, smp_rows_of(s)].astype(jnp.float32)
        for m in range(1, n_smp):
            part_copy(i, m).wait()
            both = both + part_in[i, m - 1].astype(jnp.float32)
        total = squares[k, smp_rows_of(s)]
        for m in range(1, n_smp):
            total = total + squares_in[k, m - 1]
        factor = lax.rsqrt(total / (width * n_smp) + EPSILON)[:, :1]
        gate = factor * both[:, :UNITS]
        up = factor * both[:, UNITS:]
        value = gate / (1.0 + jnp.exp(-gate)) * up
        hidden[k, smp_rows_of(s), columns(t, UNITS)] = value.astype(jnp.bfloat16)
        for m in range(1, n_smp):
            hidden_copy(i, m).start()

    def gate_up(i):
        k, t = lax.div(i, steps), lax.rem(i, steps)

        @pl.when(t == 0)
        def _():
            prepare(k)

        for copy in weight_copies(i):
            copy.wait()
        slot = lax.rem(i, slots)
        part[i, :, :UNITS] = jnp.dot(
            scaled[k], gate_buf[slot], preferred_element_type=jnp.float32
        ).astype(jnp.bfloat16)
        part[i, :, UNITS:] = jnp.dot(
            scaled[k], up_buf[slot], preferred_element_type=jnp.float32
        ).astype(jnp.bfloat16)
        for m in range(1, n_smp):
            part_copy(i, m).start()

        @pl.when(i + slots < all_steps)
        def _():
            for copy in weight_copies(i + slots):
                copy.start()

        @pl.when(i < tiles)
        def _():
            down_copy(i).start()

    line = Line(n, c, h, buf_a, recv_a, buf_b, from_left, from_right, sa, ra, ss, rl, rr)

    def down(j):
        k, t = lax.div(j, tiles), lax.rem(j, tiles)

        @pl.when(t == 0)
        def _():
            @pl.loop(0, steps)
            def _(u):
                for m in range(1, n_smp):
                    hidden_copy(k * steps + u, m).wait()

        @pl.when(k == 0)
        def _():
            down_copy(t).wait()

        line.give(j, jnp.dot(hidden[k], down_buf[t], preferred_element_type=jnp.float32))

    def emit(j):
        k, t = lax.div(j, tiles), lax.rem(j, tiles)
        own = pl.ds(pl.multiple_of(k * sub, sub), sub)
        value = line.finish(j) + state_ref[c, h, own, columns(t, down_tile)].astype(jnp.float32)
        mixed_ref[own, columns(t, down_tile)] = value.astype(jnp.bfloat16)

    lag = min(2, all_steps)
    first = steps + lag + 1

    @pl.loop(0, first + (all_tiles + n) * ratio)
    def _(i):
        @pl.when(i < all_steps)
        def _():
            gate_up(i)

        @pl.when((i >= lag) & (i < all_steps + lag))
        def _():
            act(i - lag)

        j = lax.div(i - first, ratio)

        @pl.when((i >= first) & (lax.rem(i - first, ratio) == 0))
        def _():
            @pl.when(j < all_tiles)
            def _():
                down(j)

            line.step(j)

            @pl.when(j >= n)
            def _():
                emit(j - n)

    @pl.loop(0, all_tiles)
    def _(t):
        line.drain(t)


def feed_forward(n, n_smp, state, gain, gate, up, down):
    _, _, rows, width = state.shape
    sub = SUB if rows % SUB == 0 else rows
    subsets = rows // sub
    sub_rows = n * 2 * sub
    smp_rows = sub_rows // n_smp
    units = gate.shape[1]
    steps = units // UNITS
    down_tile = max(DOWN_TILE, width // steps)
    tiles = width // down_tile
    all_steps, all_tiles = subsets * steps, subsets * tiles
    slots = min(SLOTS, all_steps)
    vmem = pl.BlockSpec(memory_space=pltpu.VMEM)
    hbm = pl.BlockSpec(memory_space=pl.ANY)
    dma = pltpu.SemaphoreType.DMA
    bf16 = jnp.bfloat16
    return pl.pallas_call(
        functools.partial(ffn_kernel, n, n_smp),
        out_shape=jax.ShapeDtypeStruct((rows, width), bf16),
        in_specs=[vmem, vmem, hbm, hbm, hbm],
        out_specs=vmem,
        scratch_shapes=[
            pltpu.VMEM((subsets, sub_rows, width), bf16),
            pltpu.VMEM((subsets, sub_rows, 128), jnp.float32),
            pltpu.VMEM((subsets, n_smp - 1, smp_rows, 128), jnp.float32),
            pltpu.VMEM((slots, width, UNITS), bf16),
            pltpu.VMEM((slots, width, UNITS), bf16),
            pltpu.VMEM((tiles, units, down_tile), bf16),
            pltpu.VMEM((all_steps, sub_rows, 2 * UNITS), bf16),
            pltpu.VMEM((all_steps, n_smp - 1, smp_rows, 2 * UNITS), bf16),
            pltpu.VMEM((subsets, sub_rows, units), bf16),
            pltpu.VMEM((all_tiles, 2, n, sub, down_tile), bf16),
            pltpu.VMEM((all_tiles, n, sub, down_tile), bf16),
            pltpu.VMEM((all_tiles, n, sub, down_tile), bf16),
            pltpu.VMEM((all_tiles, n, sub, down_tile), bf16),
            pltpu.VMEM((all_tiles, n, sub, down_tile), bf16),
            dma((slots,)),
            dma((slots,)),
            dma((tiles,)),
            dma((subsets, n_smp - 1)),
            dma((subsets, n_smp - 1)),
            dma((all_steps, n_smp - 1)),
            dma((all_steps, n_smp - 1)),
            dma((all_steps, n_smp - 1)),
            dma((all_steps, n_smp - 1)),
            dma((all_tiles,)),
            dma((all_tiles,)),
            dma((all_tiles, n)),
            dma((all_tiles, n)),
            dma((all_tiles, n)),
        ],
        compiler_params=pltpu.CompilerParams(
            collective_id=1, has_side_effects=True, vmem_limit_bytes=VMEM_BYTES
        ),
    )(state, gain, gate, up, down)


def on_device(
    queries,
    prefix_cache,
    suffix_cache,
    suffix_length,
    cache_sample,
    residual,
    w_out,
    norm_gain,
    gate_matrix,
    w_up,
    w_down,
):
    group_rows = queries.shape[0]
    keys_here = prefix_cache.shape[3] // HD
    heads_local = queries.shape[2] // HD
    n, n_smp = lax.axis_size("ctx"), lax.axis_size("smp")
    own_queries = queries[:, 0]
    rows_here = suffix_cache.shape[1]
    flat_index = lax.axis_index("ctx") * n_smp + lax.axis_index("smp")
    row_ids = lax.dynamic_slice_in_dim(cache_sample, flat_index * rows_here, rows_here, 0)
    local_ids = row_ids % group_rows
    row_queries = jnp.take(own_queries, local_ids, axis=0).reshape(rows_here, heads_local, HD)
    row_lengths = jnp.take(suffix_length, local_ids, axis=0)
    suffix_out, suffix_lse = suffix_piece(row_queries, suffix_cache[:, :, :, 0], row_lengths)
    chosen = local_ids[None, :] == jnp.arange(group_rows, dtype=jnp.int32)[:, None]
    placed_out = jnp.dot(
        chosen.astype(jnp.bfloat16),
        suffix_out.reshape(rows_here, -1),
        preferred_element_type=jnp.float32,
    ).astype(jnp.bfloat16)
    placed_lse = jnp.dot(
        chosen.astype(jnp.float32), suffix_lse[:, :, 0], precision=lax.Precision.HIGHEST
    )
    placed_lse = jnp.where(jnp.any(chosen, axis=1)[:, None], placed_lse, -1e30)
    placed_lse = placed_lse.reshape(group_rows, keys_here, -1).transpose(1, 0, 2)
    state = project(
        n,
        n_smp,
        own_queries,
        prefix_cache[:, :, 0],
        placed_out,
        placed_lse,
        w_out[0],
        residual,
    )
    return feed_forward(n, n_smp, state, norm_gain[None, :], gate_matrix, w_up, w_down)


def solution(mesh):
    in_specs = (
        P(("group", "smp"), "head", None),
        P(None, ("group", "ctx"), "head", None),
        P(None, ("group", "ctx", "smp"), None, "head", None),
        P(("group", "smp")),
        P("group"),
        P(("group", "ctx", "head"), "smp"),
        P("head", "ctx", "smp"),
        P("smp"),
        P("smp", ("ctx", "head")),
        P("smp", ("ctx", "head")),
        P(("ctx", "head"), "smp"),
    )
    out_specs = P(("group", "ctx", "head"), "smp")
    return jax.shard_map(
        on_device, mesh=mesh, in_specs=in_specs, out_specs=out_specs, check_vma=False
    )
```

```python
import functools

import jax
import jax.numpy as jnp
from jax import lax
from jax.experimental import pallas as pl
from jax.experimental.pallas import tpu as pltpu
from jax.sharding import PartitionSpec as P

D = 8192
QUERY_HEADS = 64
KEY_VALUE_HEADS = 8
HD = 128


EPSILON = 1e-05


MESH = pl.DeviceIdType.MESH
TILE = 512
VMEM_BYTES = 62 * 1024 * 1024


def remote(src, dst, send_sem, recv_sem, where):
    return pltpu.make_async_remote_copy(
        src_ref=src,
        dst_ref=dst,
        send_sem=send_sem,
        recv_sem=recv_sem,
        device_id=where,
        device_id_type=MESH,
    )


def announce(n, n_smp, c, s, h):
    barrier = pltpu.get_barrier_semaphore()
    for k in range(1, n):
        pl.semaphore_signal(barrier, inc=1, device_id={"ctx": lax.rem(c + k, n)}, device_id_type=MESH)
    for k in range(1, n_smp):
        pl.semaphore_signal(
            barrier, inc=1, device_id={"smp": lax.rem(s + k, n_smp)}, device_id_type=MESH
        )
    pl.semaphore_signal(barrier, inc=1, device_id={"head": 1 - h}, device_id_type=MESH)


def gather_round(n, n_smp):
    pl.semaphore_wait(pltpu.get_barrier_semaphore(), (n - 1) + (n_smp - 1) + 1)


def greet(n, n_smp, c, s, h):
    announce(n, n_smp, c, s, h)
    gather_round(n, n_smp)


class Line:
    def __init__(self, n, c, h, buf_a, recv_a, buf_b, from_left, from_right, sa, ra, ss, rl, rr):
        self.n, self.c, self.h = n, c, h
        self.buf_a, self.recv_a, self.buf_b = buf_a, recv_a, buf_b
        self.from_left, self.from_right = from_left, from_right
        self.sa, self.ra, self.ss, self.rl, self.rr = sa, ra, ss, rl, rr
        self.tiles = buf_a.shape[0]

        @pl.when(c == 0)
        def _():
            from_left[:, 0] = jnp.zeros(from_left.shape[:1] + from_left.shape[2:], from_left.dtype)

        @pl.when(c == n - 1)
        def _():
            from_right[:, n - 1] = jnp.zeros(
                from_right.shape[:1] + from_right.shape[2:], from_right.dtype
            )

    def pair_copy(self, t):
        return remote(
            self.buf_a.at[t, 1 - self.h],
            self.recv_a.at[t],
            self.sa.at[t],
            self.ra.at[t],
            {"head": 1 - self.h},
        )

    def to_right(self, t, d):
        return remote(
            self.buf_b.at[t, d],
            self.from_left.at[t, d],
            self.ss.at[t, d],
            self.rl.at[t, d],
            {"ctx": lax.rem(self.c + 1, self.n)},
        )

    def to_left(self, t, d):
        return remote(
            self.buf_b.at[t, d],
            self.from_right.at[t, d],
            self.ss.at[t, d],
            self.rr.at[t, d],
            {"ctx": lax.rem(self.c + self.n - 1, self.n)},
        )

    def give(self, t, value):
        _, _, n, rows, width = self.buf_a.shape
        parts = value.reshape(n, 2, rows, width).astype(jnp.bfloat16)
        self.buf_a[t, 0] = parts[:, 0]
        self.buf_a[t, 1] = parts[:, 1]
        self.pair_copy(t).start()

    def middle(self, t):
        self.pair_copy(t).wait()
        both = self.buf_a[t, self.h].astype(jnp.float32) + self.recv_a[t].astype(jnp.float32)
        self.buf_b[t] = both.astype(jnp.bfloat16)

    def hop(self, t, inside, d, copy_of, arrived, first):
        @pl.when(inside & (t >= 0) & (t < self.tiles))
        def _():
            @pl.when(jnp.logical_not(first))
            def _():
                copy_of(t, d).wait_recv()
                both = self.buf_b[t, d].astype(jnp.float32) + arrived[t, d].astype(jnp.float32)
                self.buf_b[t, d] = both.astype(jnp.bfloat16)

            copy_of(t, d).start()

    def step(self, i):
        n, c = self.n, self.c

        @pl.when((i >= 1) & (i <= self.tiles))
        def _():
            self.middle(i - 1)

        for e in range(n - 1):
            right, left = n - 1 - e, e
            self.hop(i - 1 - c, right > c, right, self.to_right, self.from_left, c == 0)
            self.hop(i - n + c, left < c, left, self.to_left, self.from_right, c == n - 1)

    def finish(self, t):
        n, c = self.n, self.c

        @pl.when(c > 0)
        def _():
            self.to_right(t, c).wait_recv()

        @pl.when(c < n - 1)
        def _():
            self.to_left(t, c).wait_recv()

        return (
            self.buf_b[t, c].astype(jnp.float32)
            + self.from_left[t, c].astype(jnp.float32)
            + self.from_right[t, c].astype(jnp.float32)
        )

    def drain(self, t):
        for d in range(self.n):

            @pl.when(d > self.c)
            def _():
                self.to_right(t, d).wait_send()

            @pl.when(d < self.c)
            def _():
                self.to_left(t, d).wait_send()


class Scatter:
    def __init__(self, n, c, h, buf_a, recv_a, buf_b, recv_b, sa, ra, sb, rb):
        self.n, self.c, self.h = n, c, h
        self.buf_a, self.recv_a, self.buf_b, self.recv_b = buf_a, recv_a, buf_b, recv_b
        self.sa, self.ra, self.sb, self.rb = sa, ra, sb, rb

    def pair_copy(self, t):
        return remote(
            self.buf_a.at[t, 1 - self.h],
            self.recv_a.at[t],
            self.sa.at[t],
            self.ra.at[t],
            {"head": 1 - self.h},
        )

    def row_copy(self, t, k):
        d = lax.rem(self.c + k, self.n)
        return remote(
            self.buf_b.at[t, d],
            self.recv_b.at[t, k - 1],
            self.sb.at[t, k - 1],
            self.rb.at[t, k - 1],
            {"ctx": d},
        )

    def give(self, t, value):
        _, _, n, rows, width = self.buf_a.shape
        parts = value.reshape(n, 2, rows, width).astype(jnp.bfloat16)
        self.buf_a[t, 0] = parts[:, 0]
        self.buf_a[t, 1] = parts[:, 1]
        self.pair_copy(t).start()

    def middle(self, t):
        self.pair_copy(t).wait()
        both = self.buf_a[t, self.h].astype(jnp.float32) + self.recv_a[t].astype(jnp.float32)
        self.buf_b[t] = both.astype(jnp.bfloat16)
        for k in range(1, self.n):
            self.row_copy(t, k).start()

    def finish(self, t):
        total = self.buf_b[t, self.c].astype(jnp.float32)
        for k in range(1, self.n):
            self.row_copy(t, k).wait()
            total = total + self.recv_b[t, k - 1].astype(jnp.float32)
        return total


def columns(t, width):
    return pl.ds(pl.multiple_of(t * width, width), width)


def suffix_pieces(
    ids_ref, lengths_ref, q_ref, block_copy, cache, row_q, row_out, row_piece, placed, placed_lse
):
    _, rows, positions_here, width = cache.shape
    samples, features = q_ref.shape
    keys, _, per_key = placed_lse.shape
    heads = features // HD
    block = min(8, rows)
    ids = ids_ref[...]
    chosen = (
        lax.broadcasted_iota(jnp.int32, (samples, ids.shape[1]), 0) == ids
    ).astype(jnp.float32)
    picked = chosen.T[:rows]
    lengths = jnp.sum(picked * lengths_ref[...].astype(jnp.float32), axis=1, keepdims=True)
    lengths = lengths.astype(jnp.int32)
    for j in range(keys):
        lanes = slice(j * per_key * HD, (j + 1) * per_key * HD)
        own = jnp.dot(
            picked.astype(jnp.bfloat16), q_ref[:, lanes], preferred_element_type=jnp.float32
        )
        for g in range(per_key):
            row_q[pl.ds(j * per_key + g, rows, stride=heads), :] = own[:, g * HD : (g + 1) * HD]

    same = (
        lax.broadcasted_iota(jnp.int32, (heads, width), 0) // per_key
        == lax.broadcasted_iota(jnp.int32, (heads, width), 1) // HD
    )
    positions = lax.broadcasted_iota(jnp.int32, (heads, positions_here), 1)
    lanes_at = lax.broadcasted_iota(jnp.int32, (heads, ids.shape[1]), 1)
    table = jnp.zeros((heads, ids.shape[1]), jnp.float32)
    for r0 in range(0, rows, block):
        block_copy(r0 // block).wait()
        scores = []
        for r in range(r0, r0 + block):
            q = row_q[r * heads : (r + 1) * heads]
            spread = jnp.concatenate([q] * keys, axis=1)
            spread = jnp.where(same, spread, 0.0).astype(jnp.bfloat16)
            one = lax.dot_general(
                spread, cache[0, r], (((1,), (1,)), ((), ())), preferred_element_type=jnp.float32
            )
            live = positions < lengths[r : r + 1]
            scores.append(jnp.where(live, one * HD ** (-0.5), -jnp.inf))
        scores = jnp.concatenate(scores, axis=0)
        high = jnp.max(scores, axis=1, keepdims=True)
        weights = jnp.exp(scores - high)
        total = jnp.sum(weights, axis=1, keepdims=True)
        lse = high + jnp.log(total)
        weights = weights.astype(jnp.bfloat16)
        for r in range(r0, r0 + block):
            part = slice((r - r0) * heads, (r - r0 + 1) * heads)
            summed = jnp.dot(weights[part], cache[1, r], preferred_element_type=jnp.float32)
            own = jnp.concatenate(
                [
                    summed[j * per_key : (j + 1) * per_key, j * HD : (j + 1) * HD]
                    for j in range(keys)
                ],
                axis=0,
            )
            piece = (own / total[part]).astype(jnp.bfloat16)
            row_out[r * heads : (r + 1) * heads] = piece.astype(jnp.float32)
            table = jnp.where(lanes_at == r, lse[part], table)

    found = jnp.sum(chosen, axis=1, keepdims=True) > 0.0
    for k in range(heads):
        row_piece[:, k * HD : (k + 1) * HD] = row_out[pl.ds(k, rows, stride=heads), :].astype(
            jnp.bfloat16
        )
    to_sample = chosen[:, :rows].astype(jnp.bfloat16)
    for j in range(keys):
        lanes = slice(j * per_key * HD, (j + 1) * per_key * HD)
        placed[:, lanes] = jnp.dot(
            to_sample, row_piece[:, lanes], preferred_element_type=jnp.float32
        ).astype(jnp.bfloat16)
        one = lax.dot_general(
            chosen,
            table[j * per_key : (j + 1) * per_key],
            (((1,), (1,)), ((), ())),
            precision=lax.Precision.HIGHEST,
            preferred_element_type=jnp.float32,
        )
        placed_lse[j] = jnp.where(found, one, -1e30)


def proj_kernel(
    n,
    n_smp,
    ids_ref,
    lengths_ref,
    q_ref,
    kv_hbm,
    cache_hbm,
    w_ref,
    res_ref,
    state_ref,
    kv_ref,
    cache,
    row_q,
    row_out,
    row_piece,
    suf_ref,
    suf_lse_ref,
    out_mine,
    lse_mine,
    out_in,
    lse_in,
    attn,
    w_buf,
    buf_a,
    recv_a,
    buf_b,
    from_left,
    from_right,
    w_sem,
    os,
    orr,
    ls,
    lr,
    xs,
    xr,
    sa,
    ra,
    ss,
    rl,
    rr,
    gsr,
    gsl,
    gr,
    fs,
    fr,
    kv_sem,
    cache_sem,
):
    c, s, h = lax.axis_index("ctx"), lax.axis_index("smp"), lax.axis_index("head")
    tiles = w_buf.shape[0]
    keys, samples, per_key = suf_lse_ref.shape
    per_dest = out_mine.shape[2] // HD
    dests = per_key // per_dest
    together = 4
    block = min(8, cache.shape[1])

    def block_copy(i):
        rows_at = pl.ds(i * block, block)
        return pltpu.make_async_copy(
            cache_hbm.at[:, rows_at], cache.at[:, rows_at], cache_sem.at[i]
        )

    for i in range(cache.shape[1] // block):
        block_copy(i).start()
    kv_copy = pltpu.make_async_copy(kv_hbm, kv_ref, kv_sem)
    kv_copy.start()
    announce(n, n_smp, c, s, h)

    def piece_copies(at, d):
        return (
            remote(out_mine.at[d], out_in.at[at], os.at[d], orr.at[at], {"ctx": d}),
            remote(lse_mine.at[d], lse_in.at[at], ls.at[d], lr.at[at], {"ctx": d}),
        )

    def w_copy(t):
        return pltpu.make_async_copy(w_ref.at[:, columns(t, TILE)], w_buf.at[t], w_sem.at[t])

    @pl.loop(0, tiles)
    def _(t):
        w_copy(t).start()

    suffix_pieces(
        ids_ref,
        lengths_ref,
        q_ref,
        block_copy,
        cache,
        row_q,
        row_out,
        row_piece,
        suf_ref,
        suf_lse_ref,
    )
    kv_copy.wait()
    gather_round(n, n_smp)

    lanes_at = lax.broadcasted_iota(jnp.int32, (samples, 128), 1)

    @pl.loop(0, keys)
    def _(i):
        j = lax.rem(lax.div(c, dests) + 1 + i, keys)
        key = kv_ref[0, :, columns(j, HD)]
        value = kv_ref[1, :, columns(j, HD)]
        own = q_ref[:, columns(j, per_key * HD)]
        placed = suf_ref[:, columns(j, per_key * HD)]
        placed_lse = suf_lse_ref[j]
        tables = [jnp.zeros((samples, 128), jnp.float32) for _ in range(dests)]
        for g0 in range(0, per_key, together):
            rows = jnp.concatenate(
                [own[:, g * HD : (g + 1) * HD] for g in range(g0, g0 + together)], axis=0
            )
            scores = lax.dot_general(
                rows, key, (((1,), (1,)), ((), ())), preferred_element_type=jnp.float32
            ) * HD ** (-0.5)
            high = jnp.max(scores, axis=1, keepdims=True)
            weights = jnp.exp(scores - high)
            total = jnp.sum(weights, axis=1, keepdims=True)
            summed = (
                jnp.dot(weights.astype(jnp.bfloat16), value, preferred_element_type=jnp.float32)
                / total
            )
            lse = high + jnp.log(total)
            for g in range(g0, g0 + together):
                part = slice((g - g0) * samples, (g - g0 + 1) * samples)
                own_lse, other_lse = lse[part], placed_lse[:, g : g + 1]
                top = jnp.maximum(own_lse, other_lse)
                own_weight = jnp.exp(own_lse - top)
                other_weight = jnp.exp(other_lse - top)
                both = own_weight + other_weight
                merged = (
                    own_weight * summed[part]
                    + other_weight * placed[:, g * HD : (g + 1) * HD].astype(jnp.float32)
                ) / both
                at = g % per_dest
                out_mine[j * dests + g // per_dest, :, at * HD : (at + 1) * HD] = merged.astype(
                    jnp.bfloat16
                )
                q = g // per_dest
                tables[q] = jnp.where(lanes_at == at, top + jnp.log(both), tables[q])
        for q in range(dests):
            d = j * dests + q
            lse_mine[d] = tables[q].T[:8]

            @pl.when(d != c)
            def _():
                for copy in piece_copies(c, d):
                    copy.start()

    for k in range(1, n):
        d = lax.rem(c + k, n)
        for copy in piece_copies(d, d):
            copy.wait_recv()
    for k in range(1, n):
        d = lax.rem(c + k, n)
        for copy in piece_copies(c, d):
            copy.wait_send()

    lses = [lse_mine[c]] + [lse_in[lax.rem(c + k, n)] for k in range(1, n)]
    peak = functools.reduce(jnp.maximum, lses)
    scales = [jnp.exp(value - peak) for value in lses]
    denom = functools.reduce(jnp.add, scales)
    blank = jnp.zeros((120, samples), jnp.float32)
    scales = [jnp.concatenate([value / denom, blank], axis=0).T for value in scales]
    for j in range(per_dest):
        lanes = slice(j * HD, (j + 1) * HD)
        total = scales[0][:, j : j + 1] * out_mine[c, :, lanes].astype(jnp.float32)
        for k in range(1, n):
            piece = out_in[lax.rem(c + k, n), :, lanes].astype(jnp.float32)
            total = total + scales[k][:, j : j + 1] * piece
        attn[s, :, lanes] = total.astype(jnp.bfloat16)

    def attn_copy(k):
        return remote(
            attn.at[s], attn.at[s], xs.at[k - 1], xr.at[k - 1], {"smp": lax.rem(s + k, n_smp)}
        )

    for k in range(1, n_smp):
        attn_copy(k).start()
    for k in range(1, n_smp):
        attn_copy(k).wait()

    line = Line(n, c, h, buf_a, recv_a, buf_b, from_left, from_right, sa, ra, ss, rl, rr)

    def gather_copy(t, q, way, sems):
        block = state_ref.at[q, h, :, columns(t, TILE)]
        return remote(
            block, block, sems.at[t, q], gr.at[t, q], {"ctx": lax.rem(c + way, n)}
        )

    def pass_copy(t, q):
        block = state_ref.at[q, h, :, columns(t, TILE)]
        return remote(block, block, fs.at[t, q], fr.at[t, q], {"head": 1 - h})

    def spread(t, q, right, left):
        @pl.when(right & (c < n - 1))
        def _():
            gather_copy(t, q, 1, gsr).start()

        @pl.when(left & (c > 0))
        def _():
            gather_copy(t, q, n - 1, gsl).start()

        pass_copy(t, q).start()

    @pl.loop(0, tiles + 2 * n - 1)
    def _(i):
        @pl.when(i < tiles)
        def _():
            w_copy(i).wait()
            rows = attn[...].reshape(-1, attn.shape[2])
            line.give(i, jnp.dot(rows, w_buf[i], preferred_element_type=jnp.float32))

        line.step(i)

        @pl.when((i >= n) & (i < tiles + n))
        def _():
            t = i - n
            own = line.finish(t) + res_ref[:, columns(t, TILE)].astype(jnp.float32)
            state_ref[c, h, :, columns(t, TILE)] = own.astype(jnp.bfloat16)
            spread(t, c, c >= 0, c >= 0)

        for q in range(n):
            t = i - n - lax.max(c - q, q - c)

            @pl.when((q != c) & (t >= 0) & (t < tiles))
            def _():
                gather_copy(t, q, 1, gsr).wait_recv()
                spread(t, q, q < c, q > c)

    @pl.loop(0, tiles)
    def _(t):
        line.drain(t)
        for q in range(n):

            @pl.when((q <= c) & (c < n - 1))
            def _():
                gather_copy(t, q, 1, gsr).wait_send()

            @pl.when((q >= c) & (c > 0))
            def _():
                gather_copy(t, q, n - 1, gsl).wait_send()

            pass_copy(t, q).wait()


def project(n, n_smp, ids, lengths, queries, prefix_cache, suffix_cache, w, residual):
    samples, heads = queries.shape[0], queries.shape[1] // HD
    keys = prefix_cache.shape[2] // HD
    suffix_rows = suffix_cache.shape[1]
    features = queries.shape[1] // n
    rows, width = residual.shape
    tiles = width // TILE
    vmem = pl.BlockSpec(memory_space=pltpu.VMEM)
    hbm = pl.BlockSpec(memory_space=pl.ANY)
    dma = pltpu.SemaphoreType.DMA
    bf16 = jnp.bfloat16
    return pl.pallas_call(
        functools.partial(proj_kernel, n, n_smp),
        out_shape=jax.ShapeDtypeStruct((n, 2, rows, width), bf16),
        in_specs=[vmem, vmem, vmem, hbm, hbm, hbm, vmem],
        out_specs=vmem,
        scratch_shapes=[
            pltpu.VMEM(prefix_cache.shape, bf16),
            pltpu.VMEM(suffix_cache.shape, bf16),
            pltpu.VMEM((suffix_rows * heads, HD), jnp.float32),
            pltpu.VMEM((suffix_rows * heads, HD), jnp.float32),
            pltpu.VMEM((suffix_rows, heads * HD), bf16),
            pltpu.VMEM((samples, heads * HD), bf16),
            pltpu.VMEM((keys, samples, heads // keys), jnp.float32),
            pltpu.VMEM((n, samples, features), bf16),
            pltpu.VMEM((n, 8, samples), jnp.float32),
            pltpu.VMEM((n, samples, features), bf16),
            pltpu.VMEM((n, 8, samples), jnp.float32),
            pltpu.VMEM((n_smp, samples, features), bf16),
            pltpu.VMEM((tiles, w.shape[0], TILE), bf16),
            pltpu.VMEM((tiles, 2, n, rows, TILE), bf16),
            pltpu.VMEM((tiles, n, rows, TILE), bf16),
            pltpu.VMEM((tiles, n, rows, TILE), bf16),
            pltpu.VMEM((tiles, n, rows, TILE), bf16),
            pltpu.VMEM((tiles, n, rows, TILE), bf16),
            dma((tiles,)),
            dma((n,)),
            dma((n,)),
            dma((n,)),
            dma((n,)),
            dma((n_smp - 1,)),
            dma((n_smp - 1,)),
            dma((tiles,)),
            dma((tiles,)),
            dma((tiles, n)),
            dma((tiles, n)),
            dma((tiles, n)),
            dma((tiles, n)),
            dma((tiles, n)),
            dma((tiles, n)),
            dma((tiles, n)),
            dma((tiles, n)),
            dma,
            dma((suffix_rows // min(8, suffix_rows),)),
        ],
        compiler_params=pltpu.CompilerParams(
            collective_id=0, has_side_effects=True, vmem_limit_bytes=VMEM_BYTES
        ),
    )(ids, lengths, queries, prefix_cache, suffix_cache, w, residual)


UNITS = 256
SLOTS = 4
DOWN_TILE = 1024
SUB = 16


def ffn_kernel(
    n,
    n_smp,
    state_ref,
    gain_ref,
    gate_ref,
    up_ref,
    down_ref,
    mixed_ref,
    scaled,
    squares,
    squares_in,
    gate_buf,
    up_buf,
    down_buf,
    part,
    part_in,
    hidden,
    buf_a,
    recv_a,
    buf_b,
    from_left,
    from_right,
    g_sem,
    u_sem,
    d_sem,
    qs,
    qr,
    ps,
    pr,
    hs,
    hr,
    sa,
    ra,
    ss,
    rl,
    rr,
):
    c, s, h = lax.axis_index("ctx"), lax.axis_index("smp"), lax.axis_index("head")
    slots, width, _ = gate_buf.shape
    tiles, units, down_tile = down_buf.shape
    subsets, sub_rows, _ = scaled.shape
    sub = state_ref.shape[2] // subsets
    smp_rows = sub_rows // n_smp
    steps = units // UNITS
    all_steps, all_tiles = subsets * steps, subsets * tiles
    ratio = max(1, steps // tiles)

    def weight_copies(i):
        slot, t = lax.rem(i, slots), lax.rem(i, steps)
        return (
            pltpu.make_async_copy(
                gate_ref.at[:, columns(t, UNITS)], gate_buf.at[slot], g_sem.at[slot]
            ),
            pltpu.make_async_copy(up_ref.at[:, columns(t, UNITS)], up_buf.at[slot], u_sem.at[slot]),
        )

    def down_copy(t):
        return pltpu.make_async_copy(
            down_ref.at[:, columns(t, down_tile)], down_buf.at[t], d_sem.at[t]
        )

    @pl.loop(0, min(slots, all_steps))
    def _(t):
        for copy in weight_copies(t):
            copy.start()

    greet(n, n_smp, c, s, h)

    def smp_rows_of(p):
        return pl.ds(pl.multiple_of(p * smp_rows, smp_rows), smp_rows)

    def square_copy(k, m):
        p = lax.rem(s + m, n_smp)
        return remote(
            squares.at[k, smp_rows_of(p)],
            squares_in.at[k, m - 1],
            qs.at[k, m - 1],
            qr.at[k, m - 1],
            {"smp": p},
        )

    def prepare(k):
        own = pl.ds(pl.multiple_of(k * sub, sub), sub)
        for block in range(n):
            for core in range(2):
                wide = state_ref[block, core, own].astype(jnp.float32)
                first = (2 * block + core) * sub
                rows = slice(first, first + sub)
                scaled[k, rows] = (wide * gain_ref[...]).astype(jnp.bfloat16)
                sums = jnp.sum(wide * wide, axis=1, keepdims=True)
                squares[k, rows] = jnp.broadcast_to(sums, (sub, 128))
        for m in range(1, n_smp):
            square_copy(k, m).start()

    def part_copy(i, m):
        p = lax.rem(s + m, n_smp)
        return remote(
            part.at[i, smp_rows_of(p)],
            part_in.at[i, m - 1],
            ps.at[i, m - 1],
            pr.at[i, m - 1],
            {"smp": p},
        )

    def hidden_copy(i, m):
        k, t = lax.div(i, steps), lax.rem(i, steps)
        block = hidden.at[k, smp_rows_of(s), columns(t, UNITS)]
        return remote(
            block, block, hs.at[i, m - 1], hr.at[i, m - 1], {"smp": lax.rem(s + m, n_smp)}
        )

    def act(i):
        k, t = lax.div(i, steps), lax.rem(i, steps)

        @pl.when(t == 0)
        def _():
            for m in range(1, n_smp):
                square_copy(k, m).wait()

        both = part[i, smp_rows_of(s)].astype(jnp.float32)
        for m in range(1, n_smp):
            part_copy(i, m).wait()
            both = both + part_in[i, m - 1].astype(jnp.float32)
        total = squares[k, smp_rows_of(s)]
        for m in range(1, n_smp):
            total = total + squares_in[k, m - 1]
        factor = lax.rsqrt(total / (width * n_smp) + EPSILON)[:, :1]
        gate = factor * both[:, :UNITS]
        up = factor * both[:, UNITS:]
        value = gate / (1.0 + jnp.exp(-gate)) * up
        hidden[k, smp_rows_of(s), columns(t, UNITS)] = value.astype(jnp.bfloat16)
        for m in range(1, n_smp):
            hidden_copy(i, m).start()

    def gate_up(i):
        k, t = lax.div(i, steps), lax.rem(i, steps)

        @pl.when(t == 0)
        def _():
            prepare(k)

        for copy in weight_copies(i):
            copy.wait()
        slot = lax.rem(i, slots)
        part[i, :, :UNITS] = jnp.dot(
            scaled[k], gate_buf[slot], preferred_element_type=jnp.float32
        ).astype(jnp.bfloat16)
        part[i, :, UNITS:] = jnp.dot(
            scaled[k], up_buf[slot], preferred_element_type=jnp.float32
        ).astype(jnp.bfloat16)
        for m in range(1, n_smp):
            part_copy(i, m).start()

        @pl.when(i + slots < all_steps)
        def _():
            for copy in weight_copies(i + slots):
                copy.start()

        @pl.when(i < tiles)
        def _():
            down_copy(i).start()

    line = Line(n, c, h, buf_a, recv_a, buf_b, from_left, from_right, sa, ra, ss, rl, rr)

    def down(j):
        k, t = lax.div(j, tiles), lax.rem(j, tiles)

        @pl.when(t == 0)
        def _():
            @pl.loop(0, steps)
            def _(u):
                for m in range(1, n_smp):
                    hidden_copy(k * steps + u, m).wait()

        @pl.when(k == 0)
        def _():
            down_copy(t).wait()

        line.give(j, jnp.dot(hidden[k], down_buf[t], preferred_element_type=jnp.float32))

    def emit(j):
        k, t = lax.div(j, tiles), lax.rem(j, tiles)
        own = pl.ds(pl.multiple_of(k * sub, sub), sub)
        value = line.finish(j) + state_ref[c, h, own, columns(t, down_tile)].astype(jnp.float32)
        mixed_ref[own, columns(t, down_tile)] = value.astype(jnp.bfloat16)

    lag = min(2, all_steps)
    first = steps + lag + 1

    @pl.loop(0, first + (all_tiles + n) * ratio)
    def _(i):
        @pl.when(i < all_steps)
        def _():
            gate_up(i)

        @pl.when((i >= lag) & (i < all_steps + lag))
        def _():
            act(i - lag)

        j = lax.div(i - first, ratio)

        @pl.when((i >= first) & (lax.rem(i - first, ratio) == 0))
        def _():
            @pl.when(j < all_tiles)
            def _():
                down(j)

            line.step(j)

            @pl.when(j >= n)
            def _():
                emit(j - n)

    @pl.loop(0, all_tiles)
    def _(t):
        line.drain(t)


def feed_forward(n, n_smp, state, gain, gate, up, down):
    _, _, rows, width = state.shape
    sub = SUB if rows % SUB == 0 else rows
    subsets = rows // sub
    sub_rows = n * 2 * sub
    smp_rows = sub_rows // n_smp
    units = gate.shape[1]
    steps = units // UNITS
    down_tile = max(DOWN_TILE, width // steps)
    tiles = width // down_tile
    all_steps, all_tiles = subsets * steps, subsets * tiles
    slots = min(SLOTS, all_steps)
    vmem = pl.BlockSpec(memory_space=pltpu.VMEM)
    hbm = pl.BlockSpec(memory_space=pl.ANY)
    dma = pltpu.SemaphoreType.DMA
    bf16 = jnp.bfloat16
    return pl.pallas_call(
        functools.partial(ffn_kernel, n, n_smp),
        out_shape=jax.ShapeDtypeStruct((rows, width), bf16),
        in_specs=[vmem, vmem, hbm, hbm, hbm],
        out_specs=vmem,
        scratch_shapes=[
            pltpu.VMEM((subsets, sub_rows, width), bf16),
            pltpu.VMEM((subsets, sub_rows, 128), jnp.float32),
            pltpu.VMEM((subsets, n_smp - 1, smp_rows, 128), jnp.float32),
            pltpu.VMEM((slots, width, UNITS), bf16),
            pltpu.VMEM((slots, width, UNITS), bf16),
            pltpu.VMEM((tiles, units, down_tile), bf16),
            pltpu.VMEM((all_steps, sub_rows, 2 * UNITS), bf16),
            pltpu.VMEM((all_steps, n_smp - 1, smp_rows, 2 * UNITS), bf16),
            pltpu.VMEM((subsets, sub_rows, units), bf16),
            pltpu.VMEM((all_tiles, 2, n, sub, down_tile), bf16),
            pltpu.VMEM((all_tiles, n, sub, down_tile), bf16),
            pltpu.VMEM((all_tiles, n, sub, down_tile), bf16),
            pltpu.VMEM((all_tiles, n, sub, down_tile), bf16),
            pltpu.VMEM((all_tiles, n, sub, down_tile), bf16),
            dma((slots,)),
            dma((slots,)),
            dma((tiles,)),
            dma((subsets, n_smp - 1)),
            dma((subsets, n_smp - 1)),
            dma((all_steps, n_smp - 1)),
            dma((all_steps, n_smp - 1)),
            dma((all_steps, n_smp - 1)),
            dma((all_steps, n_smp - 1)),
            dma((all_tiles,)),
            dma((all_tiles,)),
            dma((all_tiles, n)),
            dma((all_tiles, n)),
            dma((all_tiles, n)),
        ],
        compiler_params=pltpu.CompilerParams(
            collective_id=1, has_side_effects=True, vmem_limit_bytes=VMEM_BYTES
        ),
    )(state, gain, gate, up, down)


def on_device(
    queries,
    prefix_cache,
    suffix_cache,
    suffix_length,
    cache_sample,
    residual,
    w_out,
    norm_gain,
    gate_matrix,
    w_up,
    w_down,
):
    group_rows = queries.shape[0]
    n, n_smp = lax.axis_size("ctx"), lax.axis_size("smp")
    rows_here = suffix_cache.shape[1]
    flat_index = lax.axis_index("ctx") * n_smp + lax.axis_index("smp")
    row_ids = lax.dynamic_slice_in_dim(cache_sample, flat_index * rows_here, rows_here, 0)
    local_ids = row_ids - lax.axis_index("smp") * group_rows
    local_ids = jnp.pad(local_ids, (0, 128 - rows_here), constant_values=-1)
    state = project(
        n,
        n_smp,
        local_ids[None, :],
        suffix_length[None, :],
        queries[:, 0],
        prefix_cache[:, :, 0],
        suffix_cache[:, :, :, 0],
        w_out[0],
        residual,
    )
    return feed_forward(n, n_smp, state, norm_gain[None, :], gate_matrix, w_up, w_down)


def solution(mesh):
    in_specs = (
        P(("group", "smp"), "head", None),
        P(None, ("group", "ctx"), "head", None),
        P(None, ("group", "ctx", "smp"), None, "head", None),
        P(("group", "smp")),
        P("group"),
        P(("group", "ctx", "head"), "smp"),
        P("head", "ctx", "smp"),
        P("smp"),
        P("smp", ("ctx", "head")),
        P("smp", ("ctx", "head")),
        P(("ctx", "head"), "smp"),
    )
    out_specs = P(("group", "ctx", "head"), "smp")
    return jax.shard_map(
        on_device, mesh=mesh, in_specs=in_specs, out_specs=out_specs, check_vma=False
    )
```

```python
import functools
import types

import jax
import jax.numpy as jnp
from jax import lax
from jax.experimental import pallas as pl
from jax.experimental.pallas import tpu as pltpu
from jax.sharding import PartitionSpec as P

D = 8192
QUERY_HEADS = 64
KEY_VALUE_HEADS = 8
HD = 128


EPSILON = 1e-05


MESH = pl.DeviceIdType.MESH
TILE = 1024
UNITS = 256
SLOTS = 3
SUB = 16
VMEM_BYTES = 67043328


def remote(src, dst, send_sem, recv_sem, where):
    return pltpu.make_async_remote_copy(
        src_ref=src,
        dst_ref=dst,
        send_sem=send_sem,
        recv_sem=recv_sem,
        device_id=where,
        device_id_type=MESH,
    )


def announce(n, n_smp, c, s, h):
    barrier = pltpu.get_barrier_semaphore()
    for k in range(1, n):
        pl.semaphore_signal(barrier, inc=1, device_id={"ctx": lax.rem(c + k, n)}, device_id_type=MESH)
    for k in range(1, n_smp):
        pl.semaphore_signal(
            barrier, inc=1, device_id={"smp": lax.rem(s + k, n_smp)}, device_id_type=MESH
        )
    pl.semaphore_signal(barrier, inc=1, device_id={"head": 1 - h}, device_id_type=MESH)


def gather_round(n, n_smp):
    pl.semaphore_wait(pltpu.get_barrier_semaphore(), (n - 1) + (n_smp - 1) + 1)


class Line:
    def __init__(self, n, c, h, buf_a, recv_a, buf_b, from_left, from_right, sa, ra, ss, rl, rr):
        self.n, self.c, self.h = n, c, h
        self.buf_a, self.recv_a, self.buf_b = buf_a, recv_a, buf_b
        self.from_left, self.from_right = from_left, from_right
        self.sa, self.ra, self.ss, self.rl, self.rr = sa, ra, ss, rl, rr
        self.tiles = buf_a.shape[0]

        @pl.when(c == 0)
        def _():
            from_left[:, 0] = jnp.zeros(from_left.shape[:1] + from_left.shape[2:], from_left.dtype)

        @pl.when(c == n - 1)
        def _():
            from_right[:, n - 1] = jnp.zeros(
                from_right.shape[:1] + from_right.shape[2:], from_right.dtype
            )

    def pair_copy(self, t):
        return remote(
            self.buf_a.at[t, 1 - self.h],
            self.recv_a.at[t],
            self.sa.at[t],
            self.ra.at[t],
            {"head": 1 - self.h},
        )

    def to_right(self, t, d):
        return remote(
            self.buf_b.at[t, d],
            self.from_left.at[t, d],
            self.ss.at[t, d],
            self.rl.at[t, d],
            {"ctx": lax.rem(self.c + 1, self.n)},
        )

    def to_left(self, t, d):
        return remote(
            self.buf_b.at[t, d],
            self.from_right.at[t, d],
            self.ss.at[t, d],
            self.rr.at[t, d],
            {"ctx": lax.rem(self.c + self.n - 1, self.n)},
        )

    def give(self, t, value):
        _, _, n, rows, width = self.buf_a.shape
        parts = value.reshape(n, 2, rows, width).astype(jnp.bfloat16)
        self.buf_a[t, 0] = parts[:, 0]
        self.buf_a[t, 1] = parts[:, 1]
        self.pair_copy(t).start()

    def middle(self, t):
        self.pair_copy(t).wait()
        both = self.buf_a[t, self.h].astype(jnp.float32) + self.recv_a[t].astype(jnp.float32)
        self.buf_b[t] = both.astype(jnp.bfloat16)

    def hop(self, t, inside, d, copy_of, arrived, first):
        @pl.when(inside & (t >= 0) & (t < self.tiles))
        def _():
            @pl.when(jnp.logical_not(first))
            def _():
                copy_of(t, d).wait_recv()
                both = self.buf_b[t, d].astype(jnp.float32) + arrived[t, d].astype(jnp.float32)
                self.buf_b[t, d] = both.astype(jnp.bfloat16)

            copy_of(t, d).start()

    def step(self, i):
        n, c = self.n, self.c

        @pl.when((i >= 1) & (i <= self.tiles))
        def _():
            self.middle(i - 1)

        for e in range(n - 1):
            right, left = n - 1 - e, e
            self.hop(i - 1 - c, right > c, right, self.to_right, self.from_left, c == 0)
            self.hop(i - n + c, left < c, left, self.to_left, self.from_right, c == n - 1)

    def finish(self, t):
        n, c = self.n, self.c

        @pl.when(c > 0)
        def _():
            self.to_right(t, c).wait_recv()

        @pl.when(c < n - 1)
        def _():
            self.to_left(t, c).wait_recv()

        return (
            self.buf_b[t, c].astype(jnp.float32)
            + self.from_left[t, c].astype(jnp.float32)
            + self.from_right[t, c].astype(jnp.float32)
        )

    def drain(self, t):
        for d in range(self.n):

            @pl.when(d > self.c)
            def _():
                self.to_right(t, d).wait_send()

            @pl.when(d < self.c)
            def _():
                self.to_left(t, d).wait_send()


def columns(t, width):
    return pl.ds(pl.multiple_of(t * width, width), width)


def suffix_pieces(
    ids_ref, lengths_ref, q_ref, block_copy, cache, row_q, row_out, row_piece, placed, placed_lse
):
    _, rows, positions_here, width = cache.shape
    samples, features = q_ref.shape
    keys, _, per_key = placed_lse.shape
    heads = features // HD
    block = min(8, rows)
    ids = ids_ref[...]
    chosen = (
        lax.broadcasted_iota(jnp.int32, (samples, ids.shape[1]), 0) == ids
    ).astype(jnp.float32)
    picked = chosen.T[:rows]
    lengths = jnp.sum(picked * lengths_ref[...].astype(jnp.float32), axis=1, keepdims=True)
    lengths = lengths.astype(jnp.int32)
    for j in range(keys):
        lanes = slice(j * per_key * HD, (j + 1) * per_key * HD)
        own = jnp.dot(
            picked.astype(jnp.bfloat16), q_ref[:, lanes], preferred_element_type=jnp.float32
        )
        for g in range(per_key):
            row_q[pl.ds(j * per_key + g, rows, stride=heads), :] = own[:, g * HD : (g + 1) * HD]

    same = (
        lax.broadcasted_iota(jnp.int32, (heads, width), 0) // per_key
        == lax.broadcasted_iota(jnp.int32, (heads, width), 1) // HD
    )
    positions = lax.broadcasted_iota(jnp.int32, (heads, positions_here), 1)
    lanes_at = lax.broadcasted_iota(jnp.int32, (heads, ids.shape[1]), 1)
    table = jnp.zeros((heads, ids.shape[1]), jnp.float32)
    for r0 in range(0, rows, block):
        block_copy(r0 // block).wait()
        scores = []
        for r in range(r0, r0 + block):
            q = row_q[r * heads : (r + 1) * heads]
            spread = jnp.concatenate([q] * keys, axis=1)
            spread = jnp.where(same, spread, 0.0).astype(jnp.bfloat16)
            one = lax.dot_general(
                spread, cache[0, r], (((1,), (1,)), ((), ())), preferred_element_type=jnp.float32
            )
            live = positions < lengths[r : r + 1]
            scores.append(jnp.where(live, one * HD ** (-0.5), -jnp.inf))
        scores = jnp.concatenate(scores, axis=0)
        high = jnp.max(scores, axis=1, keepdims=True)
        weights = jnp.exp(scores - high)
        total = jnp.sum(weights, axis=1, keepdims=True)
        lse = high + jnp.log(total)
        weights = weights.astype(jnp.bfloat16)
        for r in range(r0, r0 + block):
            part = slice((r - r0) * heads, (r - r0 + 1) * heads)
            summed = jnp.dot(weights[part], cache[1, r], preferred_element_type=jnp.float32)
            own = jnp.concatenate(
                [
                    summed[j * per_key : (j + 1) * per_key, j * HD : (j + 1) * HD]
                    for j in range(keys)
                ],
                axis=0,
            )
            piece = (own / total[part]).astype(jnp.bfloat16)
            row_out[r * heads : (r + 1) * heads] = piece.astype(jnp.float32)
            table = jnp.where(lanes_at == r, lse[part], table)

    found = jnp.sum(chosen, axis=1, keepdims=True) > 0.0
    for k in range(heads):
        row_piece[:, k * HD : (k + 1) * HD] = row_out[pl.ds(k, rows, stride=heads), :].astype(
            jnp.bfloat16
        )
    to_sample = chosen[:, :rows].astype(jnp.bfloat16)
    for j in range(keys):
        lanes = slice(j * per_key * HD, (j + 1) * per_key * HD)
        placed[:, lanes] = jnp.dot(
            to_sample, row_piece[:, lanes], preferred_element_type=jnp.float32
        ).astype(jnp.bfloat16)
        one = lax.dot_general(
            chosen,
            table[j * per_key : (j + 1) * per_key],
            (((1,), (1,)), ((), ())),
            precision=lax.Precision.HIGHEST,
            preferred_element_type=jnp.float32,
        )
        placed_lse[j] = jnp.where(found, one, -1e30)


def layer_kernel(n, n_smp, names, *refs):
    r = types.SimpleNamespace(**dict(zip(names, refs, strict=True)))
    c, s, h = lax.axis_index("ctx"), lax.axis_index("smp"), lax.axis_index("head")
    q_ref, kv_ref, suf_ref, suf_lse_ref = r.q, r.kv, r.placed, r.placed_lse
    out_mine, lse_mine, out_in, lse_in, attn = r.out_mine, r.lse_mine, r.out_in, r.lse_in, r.attn
    os, orr, ls, lr, xs, xr = r.os, r.orr, r.ls, r.lr, r.xs, r.xr
    state = r.state
    keys, samples, per_key = suf_lse_ref.shape
    per_dest = out_mine.shape[2] // HD
    dests = per_key // per_dest
    together = 4
    slots, width, _ = r.gate_buf.shape
    tiles, units, tile = r.down_buf.shape
    subsets, sub_rows, _ = r.scaled.shape
    sub = state.shape[2] // subsets
    smp_rows = sub_rows // n_smp
    steps = units // UNITS
    all_steps, all_tiles = subsets * steps, subsets * tiles
    ratio = max(1, steps // tiles)
    w_rows = r.w_hbm.shape[0]
    per_slot = units // w_rows
    w_slots = -(-tiles // per_slot)
    block = min(8, r.cache.shape[1])

    def block_copy(i):
        rows_at = pl.ds(i * block, block)
        return pltpu.make_async_copy(
            r.cache_hbm.at[:, rows_at], r.cache.at[:, rows_at], r.cache_sem.at[i]
        )

    def w_block(t):
        first_row = pl.multiple_of(lax.rem(t, per_slot) * w_rows, w_rows)
        return r.down_buf.at[lax.div(t, per_slot), pl.ds(first_row, w_rows)]

    def w_copy(t):
        return pltpu.make_async_copy(r.w_hbm.at[:, columns(t, tile)], w_block(t), r.w_sem.at[t])

    def weight_copies(i):
        slot, t = lax.rem(i, slots), lax.rem(i, steps)
        return (
            pltpu.make_async_copy(
                r.gate_hbm.at[:, columns(t, UNITS)], r.gate_buf.at[slot], r.g_sem.at[slot]
            ),
            pltpu.make_async_copy(
                r.up_hbm.at[:, columns(t, UNITS)], r.up_buf.at[slot], r.u_sem.at[slot]
            ),
        )

    def down_copy(t):
        return pltpu.make_async_copy(
            r.down_hbm.at[:, columns(t, tile)], r.down_buf.at[t], r.d_sem.at[t]
        )

    for i in range(r.cache.shape[1] // block):
        block_copy(i).start()
    kv_copy = pltpu.make_async_copy(r.kv_hbm, kv_ref, r.kv_sem)
    kv_copy.start()
    announce(n, n_smp, c, s, h)

    def piece_copies(at, d):
        return (
            remote(out_mine.at[d], out_in.at[at], os.at[d], orr.at[at], {"ctx": d}),
            remote(lse_mine.at[d], lse_in.at[at], ls.at[d], lr.at[at], {"ctx": d}),
        )

    suffix_pieces(
        r.ids,
        r.lengths,
        q_ref,
        block_copy,
        r.cache,
        r.row_q,
        r.row_out,
        r.row_piece,
        suf_ref,
        suf_lse_ref,
    )
    kv_copy.wait()

    @pl.loop(0, tiles)
    def _(t):
        w_copy(t).start()

    @pl.loop(0, min(slots, all_steps))
    def _(t):
        for copy in weight_copies(t):
            copy.start()

    for t in range(w_slots, tiles):
        down_copy(t).start()
    gather_round(n, n_smp)

    lanes_at = lax.broadcasted_iota(jnp.int32, (samples, 128), 1)

    @pl.loop(0, keys)
    def _(i):
        j = lax.rem(lax.div(c, dests) + 1 + i, keys)
        key = kv_ref[0, :, columns(j, HD)]
        value = kv_ref[1, :, columns(j, HD)]
        own = q_ref[:, columns(j, per_key * HD)]
        placed = suf_ref[:, columns(j, per_key * HD)]
        placed_lse = suf_lse_ref[j]
        tables = [jnp.zeros((samples, 128), jnp.float32) for _ in range(dests)]
        for g0 in range(0, per_key, together):
            rows = jnp.concatenate(
                [own[:, g * HD : (g + 1) * HD] for g in range(g0, g0 + together)], axis=0
            )
            scores = lax.dot_general(
                rows, key, (((1,), (1,)), ((), ())), preferred_element_type=jnp.float32
            ) * HD ** (-0.5)
            high = jnp.max(scores, axis=1, keepdims=True)
            weights = jnp.exp(scores - high)
            total = jnp.sum(weights, axis=1, keepdims=True)
            summed = (
                jnp.dot(weights.astype(jnp.bfloat16), value, preferred_element_type=jnp.float32)
                / total
            )
            lse = high + jnp.log(total)
            for g in range(g0, g0 + together):
                part = slice((g - g0) * samples, (g - g0 + 1) * samples)
                own_lse, other_lse = lse[part], placed_lse[:, g : g + 1]
                top = jnp.maximum(own_lse, other_lse)
                own_weight = jnp.exp(own_lse - top)
                other_weight = jnp.exp(other_lse - top)
                both = own_weight + other_weight
                merged = (
                    own_weight * summed[part]
                    + other_weight * placed[:, g * HD : (g + 1) * HD].astype(jnp.float32)
                ) / both
                at = g % per_dest
                out_mine[j * dests + g // per_dest, :, at * HD : (at + 1) * HD] = merged.astype(
                    jnp.bfloat16
                )
                q = g // per_dest
                tables[q] = jnp.where(lanes_at == at, top + jnp.log(both), tables[q])
        for q in range(dests):
            d = j * dests + q
            lse_mine[d] = tables[q].T[:8]

            @pl.when(d != c)
            def _():
                for copy in piece_copies(c, d):
                    copy.start()

    for k in range(1, n):
        d = lax.rem(c + k, n)
        for copy in piece_copies(d, d):
            copy.wait_recv()
    for k in range(1, n):
        d = lax.rem(c + k, n)
        for copy in piece_copies(c, d):
            copy.wait_send()

    lses = [lse_mine[c]] + [lse_in[lax.rem(c + k, n)] for k in range(1, n)]
    peak = functools.reduce(jnp.maximum, lses)
    scales = [jnp.exp(value - peak) for value in lses]
    denom = functools.reduce(jnp.add, scales)
    blank = jnp.zeros((120, samples), jnp.float32)
    scales = [jnp.concatenate([value / denom, blank], axis=0).T for value in scales]
    for j in range(per_dest):
        lanes = slice(j * HD, (j + 1) * HD)
        total = scales[0][:, j : j + 1] * out_mine[c, :, lanes].astype(jnp.float32)
        for k in range(1, n):
            piece = out_in[lax.rem(c + k, n), :, lanes].astype(jnp.float32)
            total = total + scales[k][:, j : j + 1] * piece
        attn[s, :, lanes] = total.astype(jnp.bfloat16)

    def attn_copy(k):
        return remote(
            attn.at[s], attn.at[s], xs.at[k - 1], xr.at[k - 1], {"smp": lax.rem(s + k, n_smp)}
        )

    for k in range(1, n_smp):
        attn_copy(k).start()
    for k in range(1, n_smp):
        attn_copy(k).wait()

    by_owner = attn[...].reshape(2 * n, subsets, sub, attn.shape[2])
    for k in range(subsets):
        r.attn_rows[k] = by_owner[:, k].reshape(sub_rows, attn.shape[2])

    line = Line(
        n,
        c,
        h,
        r.buf_a,
        r.recv_a,
        r.buf_b,
        r.from_left,
        r.from_right,
        r.sa,
        r.ra,
        r.ss,
        r.rl,
        r.rr,
    )

    def rows_of(k):
        return pl.ds(pl.multiple_of(k * sub, sub), sub)

    def gather_copy(j, q, way, sems):
        k, t = lax.div(j, tiles), lax.rem(j, tiles)
        at = state.at[q, h, rows_of(k), columns(t, tile)]
        return remote(at, at, sems.at[j, q], r.gr.at[j, q], {"ctx": lax.rem(c + way, n)})

    def pass_copy(j, q):
        k, t = lax.div(j, tiles), lax.rem(j, tiles)
        at = state.at[q, h, rows_of(k), columns(t, tile)]
        return remote(at, at, r.fs.at[j, q], r.fr.at[j, q], {"head": 1 - h})

    def spread(j, q, right, left):
        @pl.when(right & (c < n - 1))
        def _():
            gather_copy(j, q, 1, r.gsr).start()

        @pl.when(left & (c > 0))
        def _():
            gather_copy(j, q, n - 1, r.gsl).start()

        pass_copy(j, q).start()

    def project(i):
        @pl.when(i < all_tiles)
        def _():
            k, t = lax.div(i, tiles), lax.rem(i, tiles)

            @pl.when(k == 0)
            def _():
                w_copy(t).wait()

            line.give(
                i, jnp.dot(r.attn_rows[k], w_block(t)[...], preferred_element_type=jnp.float32)
            )

        line.step(i)

        @pl.when((i >= n) & (i < all_tiles + n))
        def _():
            j = i - n
            k, t = lax.div(j, tiles), lax.rem(j, tiles)
            own = line.finish(j) + r.res[rows_of(k), columns(t, tile)].astype(jnp.float32)
            state[c, h, rows_of(k), columns(t, tile)] = own.astype(jnp.bfloat16)
            spread(j, c, c >= 0, c >= 0)

        for q in range(n):
            j = i - n - lax.max(c - q, q - c)

            @pl.when((q != c) & (j >= 0) & (j < all_tiles))
            def _():
                gather_copy(j, q, 1, r.gsr).wait_recv()
                spread(j, q, q < c, q > c)

    def smp_rows_of(p):
        return pl.ds(pl.multiple_of(p * smp_rows, smp_rows), smp_rows)

    def square_copy(k, m):
        p = lax.rem(s + m, n_smp)
        return remote(
            r.squares.at[k, smp_rows_of(p)],
            r.squares_in.at[k, m - 1],
            r.qs.at[k, m - 1],
            r.qr.at[k, m - 1],
            {"smp": p},
        )

    def prepare(k):
        @pl.loop(k * tiles, (k + 1) * tiles)
        def _(j):
            for q in range(n):
                pass_copy(j, q).wait()

        for owner in range(n):
            for core in range(2):
                wide = state[owner, core, rows_of(k)].astype(jnp.float32)
                first_row = (2 * owner + core) * sub
                rows = slice(first_row, first_row + sub)
                r.scaled[k, rows] = (wide * r.gain[...]).astype(jnp.bfloat16)
                sums = jnp.sum(wide * wide, axis=1, keepdims=True)
                r.squares[k, rows] = jnp.broadcast_to(sums, (sub, 128))
        for m in range(1, n_smp):
            square_copy(k, m).start()

    def part_copy(i, m):
        p = lax.rem(s + m, n_smp)
        return remote(
            r.part.at[i, smp_rows_of(p)],
            r.part_in.at[i, m - 1],
            r.ps.at[i, m - 1],
            r.pr.at[i, m - 1],
            {"smp": p},
        )

    def hidden_copy(i, m):
        k, t = lax.div(i, steps), lax.rem(i, steps)
        at = r.hidden.at[k, smp_rows_of(s), columns(t, UNITS)]
        return remote(
            at, at, r.hs.at[i, m - 1], r.hr.at[i, m - 1], {"smp": lax.rem(s + m, n_smp)}
        )

    def act(i):
        k, t = lax.div(i, steps), lax.rem(i, steps)

        @pl.when(t == 0)
        def _():
            for m in range(1, n_smp):
                square_copy(k, m).wait()

        both = r.part[i, smp_rows_of(s)].astype(jnp.float32)
        for m in range(1, n_smp):
            part_copy(i, m).wait()
            both = both + r.part_in[i, m - 1].astype(jnp.float32)
        total = r.squares[k, smp_rows_of(s)]
        for m in range(1, n_smp):
            total = total + r.squares_in[k, m - 1]
        factor = lax.rsqrt(total / (width * n_smp) + EPSILON)[:, :1]
        gate = factor * both[:, :UNITS]
        up = factor * both[:, UNITS:]
        value = gate / (1.0 + jnp.exp(-gate)) * up
        r.hidden[k, smp_rows_of(s), columns(t, UNITS)] = value.astype(jnp.bfloat16)
        for m in range(1, n_smp):
            hidden_copy(i, m).start()

    def gate_up(i):
        k, t = lax.div(i, steps), lax.rem(i, steps)

        @pl.when(t == 0)
        def _():
            prepare(k)

        for copy in weight_copies(i):
            copy.wait()
        slot = lax.rem(i, slots)
        r.part[i, :, :UNITS] = jnp.dot(
            r.scaled[k], r.gate_buf[slot], preferred_element_type=jnp.float32
        ).astype(jnp.bfloat16)
        r.part[i, :, UNITS:] = jnp.dot(
            r.scaled[k], r.up_buf[slot], preferred_element_type=jnp.float32
        ).astype(jnp.bfloat16)
        for m in range(1, n_smp):
            part_copy(i, m).start()

        @pl.when(i + slots < all_steps)
        def _():
            for copy in weight_copies(i + slots):
                copy.start()

    def down(j):
        k, t = lax.div(j, tiles), lax.rem(j, tiles)

        @pl.when(t == 0)
        def _():
            @pl.loop(0, steps)
            def _(u):
                for m in range(1, n_smp):
                    hidden_copy(k * steps + u, m).wait()

        @pl.when(k == 0)
        def _():
            down_copy(t).wait()

        line.drain(j)
        line.give(j, jnp.dot(r.hidden[k], r.down_buf[t], preferred_element_type=jnp.float32))

    def emit(j):
        k, t = lax.div(j, tiles), lax.rem(j, tiles)
        value = line.finish(j) + state[c, h, rows_of(k), columns(t, tile)].astype(jnp.float32)
        r.mixed[rows_of(k), columns(t, tile)] = value.astype(jnp.bfloat16)

    ahead = max(tiles + 2 * n - 1, all_tiles)
    rest = all_tiles + 2 * n - 1 - ahead

    @pl.loop(0, ahead)
    def _(i):
        project(i)

    for t in range(w_slots):
        down_copy(t).start()

    lag = min(2, all_steps)
    first = max(steps + lag + 1, rest)

    @pl.loop(0, first + (all_tiles + n) * ratio)
    def _(i):
        @pl.when(i < all_steps)
        def _():
            gate_up(i)

        @pl.when(i < rest)
        def _():
            project(i + ahead)

        @pl.when((i >= lag) & (i < all_steps + lag))
        def _():
            act(i - lag)

        j = lax.div(i - first, ratio)

        @pl.when((i >= first) & (lax.rem(i - first, ratio) == 0))
        def _():
            @pl.when(j < all_tiles)
            def _():
                down(j)

            line.step(j)

            @pl.when(j >= n)
            def _():
                emit(j - n)

    @pl.loop(0, all_tiles)
    def _(j):
        line.drain(j)
        for q in range(n):

            @pl.when((q <= c) & (c < n - 1))
            def _():
                gather_copy(j, q, 1, r.gsr).wait_send()

            @pl.when((q >= c) & (c > 0))
            def _():
                gather_copy(j, q, n - 1, r.gsl).wait_send()


def layer(
    n, n_smp, ids, lengths, queries, prefix_cache, suffix_cache, w, residual, gain, gate, up, down
):
    samples, heads = queries.shape[0], queries.shape[1] // HD
    keys = prefix_cache.shape[2] // HD
    suffix_rows = suffix_cache.shape[1]
    features = queries.shape[1] // n
    rows, width = residual.shape
    sub = SUB if rows % SUB == 0 else rows
    subsets = rows // sub
    sub_rows = n * 2 * sub
    smp_rows = sub_rows // n_smp
    units = gate.shape[1]
    steps = units // UNITS
    tile = max(TILE, width // steps)
    tiles = width // tile
    all_steps, all_tiles = subsets * steps, subsets * tiles
    slots = min(SLOTS, all_steps)
    vmem = pl.BlockSpec(memory_space=pltpu.VMEM)
    hbm = pl.BlockSpec(memory_space=pl.ANY)
    dma = pltpu.SemaphoreType.DMA
    bf16, f32 = jnp.bfloat16, jnp.float32
    scratch = {
        "kv": pltpu.VMEM(prefix_cache.shape, bf16),
        "cache": pltpu.VMEM(suffix_cache.shape, bf16),
        "row_q": pltpu.VMEM((suffix_rows * heads, HD), f32),
        "row_out": pltpu.VMEM((suffix_rows * heads, HD), f32),
        "row_piece": pltpu.VMEM((suffix_rows, heads * HD), bf16),
        "placed": pltpu.VMEM((samples, heads * HD), bf16),
        "placed_lse": pltpu.VMEM((keys, samples, heads // keys), f32),
        "out_mine": pltpu.VMEM((n, samples, features), bf16),
        "lse_mine": pltpu.VMEM((n, 8, samples), f32),
        "out_in": pltpu.VMEM((n, samples, features), bf16),
        "lse_in": pltpu.VMEM((n, 8, samples), f32),
        "attn": pltpu.VMEM((n_smp, samples, features), bf16),
        "attn_rows": pltpu.VMEM((subsets, sub_rows, features), bf16),
        "state": pltpu.VMEM((n, 2, rows, width), bf16),
        "scaled": pltpu.VMEM((subsets, sub_rows, width), bf16),
        "squares": pltpu.VMEM((subsets, sub_rows, 128), f32),
        "squares_in": pltpu.VMEM((subsets, n_smp - 1, smp_rows, 128), f32),
        "gate_buf": pltpu.VMEM((slots, width, UNITS), bf16),
        "up_buf": pltpu.VMEM((slots, width, UNITS), bf16),
        "down_buf": pltpu.VMEM((tiles, units, tile), bf16),
        "part": pltpu.VMEM((all_steps, sub_rows, 2 * UNITS), bf16),
        "part_in": pltpu.VMEM((all_steps, n_smp - 1, smp_rows, 2 * UNITS), bf16),
        "hidden": pltpu.VMEM((subsets, sub_rows, units), bf16),
        "buf_a": pltpu.VMEM((all_tiles, 2, n, sub, tile), bf16),
        "recv_a": pltpu.VMEM((all_tiles, n, sub, tile), bf16),
        "buf_b": pltpu.VMEM((all_tiles, n, sub, tile), bf16),
        "from_left": pltpu.VMEM((all_tiles, n, sub, tile), bf16),
        "from_right": pltpu.VMEM((all_tiles, n, sub, tile), bf16),
        "kv_sem": dma,
        "cache_sem": dma((suffix_rows // min(8, suffix_rows),)),
        "w_sem": dma((tiles,)),
        "g_sem": dma((slots,)),
        "u_sem": dma((slots,)),
        "d_sem": dma((tiles,)),
    }
    scratch |= {name: dma((n,)) for name in ("os", "orr", "ls", "lr")}
    scratch |= {name: dma((n_smp - 1,)) for name in ("xs", "xr")}
    scratch |= {name: dma((subsets, n_smp - 1)) for name in ("qs", "qr")}
    scratch |= {name: dma((all_steps, n_smp - 1)) for name in ("ps", "pr", "hs", "hr")}
    scratch |= {name: dma((all_tiles,)) for name in ("sa", "ra")}
    scratch |= {
        name: dma((all_tiles, n)) for name in ("ss", "rl", "rr", "gsr", "gsl", "gr", "fs", "fr")
    }
    operands = {
        "ids": (ids, vmem),
        "lengths": (lengths, vmem),
        "q": (queries, vmem),
        "kv_hbm": (prefix_cache, hbm),
        "cache_hbm": (suffix_cache, hbm),
        "w_hbm": (w, hbm),
        "res": (residual, vmem),
        "gain": (gain, vmem),
        "gate_hbm": (gate, hbm),
        "up_hbm": (up, hbm),
        "down_hbm": (down, hbm),
    }
    names = (*operands, "mixed", *scratch)
    return pl.pallas_call(
        functools.partial(layer_kernel, n, n_smp, names),
        out_shape=jax.ShapeDtypeStruct((rows, width), bf16),
        in_specs=[spec for _, spec in operands.values()],
        out_specs=vmem,
        scratch_shapes=list(scratch.values()),
        compiler_params=pltpu.CompilerParams(
            collective_id=0, has_side_effects=True, vmem_limit_bytes=VMEM_BYTES
        ),
    )(*[value for value, _ in operands.values()])


def on_device(
    queries,
    prefix_cache,
    suffix_cache,
    suffix_length,
    cache_sample,
    residual,
    w_out,
    norm_gain,
    gate_matrix,
    w_up,
    w_down,
):
    group_rows = queries.shape[0]
    n, n_smp = lax.axis_size("ctx"), lax.axis_size("smp")
    rows_here = suffix_cache.shape[1]
    flat_index = lax.axis_index("ctx") * n_smp + lax.axis_index("smp")
    row_ids = lax.dynamic_slice_in_dim(cache_sample, flat_index * rows_here, rows_here, 0)
    local_ids = row_ids - lax.axis_index("smp") * group_rows
    local_ids = jnp.pad(local_ids, (0, 128 - rows_here), constant_values=-1)
    return layer(
        n,
        n_smp,
        local_ids[None, :],
        suffix_length[None, :],
        queries[:, 0],
        prefix_cache[:, :, 0],
        suffix_cache[:, :, :, 0],
        w_out[0],
        residual,
        norm_gain[None, :],
        gate_matrix,
        w_up,
        w_down,
    )


def solution(mesh):
    in_specs = (
        P(("group", "smp"), "head", None),
        P(None, ("group", "ctx"), "head", None),
        P(None, ("group", "ctx", "smp"), None, "head", None),
        P(("group", "smp")),
        P("group"),
        P(("group", "ctx", "head"), "smp"),
        P("head", "ctx", "smp"),
        P("smp"),
        P("smp", ("ctx", "head")),
        P("smp", ("ctx", "head")),
        P(("ctx", "head"), "smp"),
    )
    out_specs = P(("group", "ctx", "head"), "smp")
    return jax.shard_map(
        on_device, mesh=mesh, in_specs=in_specs, out_specs=out_specs, check_vma=False
    )
```

```python
import functools
import types

import jax
import jax.numpy as jnp
from jax import lax
from jax.experimental import pallas as pl
from jax.experimental.pallas import tpu as pltpu
from jax.sharding import PartitionSpec as P

D = 8192
QUERY_HEADS = 64
KEY_VALUE_HEADS = 8
HD = 128


EPSILON = 1e-05


MESH = pl.DeviceIdType.MESH
TILE = 1024
UNITS = 256
SLOTS = 3
SUB = 16
VMEM_BYTES = 67043328


def remote(src, dst, send_sem, recv_sem, where):
    return pltpu.make_async_remote_copy(
        src_ref=src,
        dst_ref=dst,
        send_sem=send_sem,
        recv_sem=recv_sem,
        device_id=where,
        device_id_type=MESH,
    )


def announce(n, n_smp, c, s, h):
    barrier = pltpu.get_barrier_semaphore()
    for k in range(1, n):
        pl.semaphore_signal(barrier, inc=1, device_id={"ctx": lax.rem(c + k, n)}, device_id_type=MESH)
    for k in range(1, n_smp):
        pl.semaphore_signal(
            barrier, inc=1, device_id={"smp": lax.rem(s + k, n_smp)}, device_id_type=MESH
        )
    pl.semaphore_signal(barrier, inc=1, device_id={"head": 1 - h}, device_id_type=MESH)


def gather_round(n, n_smp):
    pl.semaphore_wait(pltpu.get_barrier_semaphore(), (n - 1) + (n_smp - 1) + 1)


class Line:
    def __init__(self, n, c, h, buf_a, recv_a, buf_b, from_left, from_right, sa, ra, ss, rl, rr):
        self.n, self.c, self.h = n, c, h
        self.buf_a, self.recv_a, self.buf_b = buf_a, recv_a, buf_b
        self.from_left, self.from_right = from_left, from_right
        self.sa, self.ra, self.ss, self.rl, self.rr = sa, ra, ss, rl, rr
        self.tiles = buf_a.shape[0]

        @pl.when(c == 0)
        def _():
            from_left[:, 0] = jnp.zeros(from_left.shape[:1] + from_left.shape[2:], from_left.dtype)

        @pl.when(c == n - 1)
        def _():
            from_right[:, n - 1] = jnp.zeros(
                from_right.shape[:1] + from_right.shape[2:], from_right.dtype
            )

    def pair_copy(self, t):
        return remote(
            self.buf_a.at[t, 1 - self.h],
            self.recv_a.at[t],
            self.sa.at[t],
            self.ra.at[t],
            {"head": 1 - self.h},
        )

    def to_right(self, t, d):
        return remote(
            self.buf_b.at[t, d],
            self.from_left.at[t, d],
            self.ss.at[t, d],
            self.rl.at[t, d],
            {"ctx": lax.rem(self.c + 1, self.n)},
        )

    def to_left(self, t, d):
        return remote(
            self.buf_b.at[t, d],
            self.from_right.at[t, d],
            self.ss.at[t, d],
            self.rr.at[t, d],
            {"ctx": lax.rem(self.c + self.n - 1, self.n)},
        )

    def give(self, t, value):
        _, _, n, rows, width = self.buf_a.shape
        parts = value.reshape(n, 2, rows, width).astype(jnp.bfloat16)
        self.buf_a[t, 0] = parts[:, 0]
        self.buf_a[t, 1] = parts[:, 1]
        self.pair_copy(t).start()

    def middle(self, t):
        self.pair_copy(t).wait()
        both = self.buf_a[t, self.h].astype(jnp.float32) + self.recv_a[t].astype(jnp.float32)
        self.buf_b[t] = both.astype(jnp.bfloat16)

    def hop(self, t, inside, d, copy_of, arrived, first):
        @pl.when(inside)
        def _():
            @pl.when(jnp.logical_not(first))
            def _():
                copy_of(t, d).wait_recv()
                both = self.buf_b[t, d].astype(jnp.float32) + arrived[t, d].astype(jnp.float32)
                self.buf_b[t, d] = both.astype(jnp.bfloat16)

            copy_of(t, d).start()

    def step(self, i, tile_at):
        n, c = self.n, self.c
        live, t = tile_at(i - 1)

        @pl.when(live)
        def _():
            self.middle(t)

        live_r, t_r = tile_at(i - 1 - c)
        live_l, t_l = tile_at(i - n + c)
        for e in range(n - 1):
            right, left = n - 1 - e, e
            self.hop(t_r, live_r & (right > c), right, self.to_right, self.from_left, c == 0)
            self.hop(t_l, live_l & (left < c), left, self.to_left, self.from_right, c == n - 1)

    def finish(self, t):
        n, c = self.n, self.c

        @pl.when(c > 0)
        def _():
            self.to_right(t, c).wait_recv()

        @pl.when(c < n - 1)
        def _():
            self.to_left(t, c).wait_recv()

        return (
            self.buf_b[t, c].astype(jnp.float32)
            + self.from_left[t, c].astype(jnp.float32)
            + self.from_right[t, c].astype(jnp.float32)
        )

    def drain(self, t):
        for d in range(self.n):

            @pl.when(d > self.c)
            def _():
                self.to_right(t, d).wait_send()

            @pl.when(d < self.c)
            def _():
                self.to_left(t, d).wait_send()


def columns(t, width):
    return pl.ds(pl.multiple_of(t * width, width), width)


def suffix_pieces(
    ids_ref, lengths_ref, sub, q_ref, block_copy, cache, row_q, row_out, row_piece, placed, placed_lse
):
    _, rows, positions_here, width = cache.shape
    subsets, part_samples, features = q_ref.shape
    samples = subsets * part_samples
    keys, _, _, per_key = placed_lse.shape
    heads = features // HD
    block = min(8, rows)
    ids = ids_ref[...]
    sample_at = lax.broadcasted_iota(jnp.int32, (samples, ids.shape[1]), 0)
    picked = (sample_at == ids).astype(jnp.float32).T[:rows]
    lengths = jnp.sum(picked * lengths_ref[...].astype(jnp.float32), axis=1, keepdims=True)
    lengths = lengths.astype(jnp.int32)
    spot = ids // sub % subsets * part_samples + ids // (sub * subsets) * sub + ids % sub
    chosen = (sample_at == jnp.where(ids < 0, -1, spot)).astype(jnp.float32)
    picked = chosen.T[:rows].astype(jnp.bfloat16)
    all_q = q_ref[...].reshape(samples, features)
    for j in range(keys):
        lanes = slice(j * per_key * HD, (j + 1) * per_key * HD)
        own = jnp.dot(picked, all_q[:, lanes], preferred_element_type=jnp.float32)
        for g in range(per_key):
            row_q[pl.ds(j * per_key + g, rows, stride=heads), :] = own[:, g * HD : (g + 1) * HD]

    same = (
        lax.broadcasted_iota(jnp.int32, (heads, width), 0) // per_key
        == lax.broadcasted_iota(jnp.int32, (heads, width), 1) // HD
    )
    positions = lax.broadcasted_iota(jnp.int32, (heads, positions_here), 1)
    lanes_at = lax.broadcasted_iota(jnp.int32, (heads, ids.shape[1]), 1)
    table = jnp.zeros((heads, ids.shape[1]), jnp.float32)
    for r0 in range(0, rows, block):
        block_copy(r0 // block).wait()
        scores = []
        for r in range(r0, r0 + block):
            q = row_q[r * heads : (r + 1) * heads]
            spread = jnp.concatenate([q] * keys, axis=1)
            spread = jnp.where(same, spread, 0.0).astype(jnp.bfloat16)
            one = lax.dot_general(
                spread, cache[0, r], (((1,), (1,)), ((), ())), preferred_element_type=jnp.float32
            )
            live = positions < lengths[r : r + 1]
            scores.append(jnp.where(live, one * HD ** (-0.5), -jnp.inf))
        scores = jnp.concatenate(scores, axis=0)
        high = jnp.max(scores, axis=1, keepdims=True)
        weights = jnp.exp(scores - high)
        total = jnp.sum(weights, axis=1, keepdims=True)
        lse = high + jnp.log(total)
        weights = weights.astype(jnp.bfloat16)
        for r in range(r0, r0 + block):
            part = slice((r - r0) * heads, (r - r0 + 1) * heads)
            summed = jnp.dot(weights[part], cache[1, r], preferred_element_type=jnp.float32)
            own = jnp.concatenate(
                [
                    summed[j * per_key : (j + 1) * per_key, j * HD : (j + 1) * HD]
                    for j in range(keys)
                ],
                axis=0,
            )
            piece = (own / total[part]).astype(jnp.bfloat16)
            row_out[r * heads : (r + 1) * heads] = piece.astype(jnp.float32)
            table = jnp.where(lanes_at == r, lse[part], table)

    found = jnp.sum(chosen, axis=1, keepdims=True) > 0.0
    for k in range(heads):
        row_piece[:, k * HD : (k + 1) * HD] = row_out[pl.ds(k, rows, stride=heads), :].astype(
            jnp.bfloat16
        )
    to_sample = chosen[:, :rows].astype(jnp.bfloat16)
    for j in range(keys):
        lanes = slice(j * per_key * HD, (j + 1) * per_key * HD)
        one = jnp.dot(to_sample, row_piece[:, lanes], preferred_element_type=jnp.float32)
        placed[:, :, lanes] = one.astype(jnp.bfloat16).reshape(subsets, part_samples, -1)
        one = lax.dot_general(
            chosen,
            table[j * per_key : (j + 1) * per_key],
            (((1,), (1,)), ((), ())),
            precision=lax.Precision.HIGHEST,
            preferred_element_type=jnp.float32,
        )
        one = jnp.where(found, one, -1e30)
        placed_lse[j] = one.reshape(subsets, part_samples, per_key)


def layer_kernel(n, n_smp, names, *refs):
    r = types.SimpleNamespace(**dict(zip(names, refs, strict=True)))
    c, s, h = lax.axis_index("ctx"), lax.axis_index("smp"), lax.axis_index("head")
    kv_ref, state = r.kv, r.state
    out_mine, lse_mine, out_in, lse_in = r.out_mine, r.lse_mine, r.out_in, r.lse_in
    keys, _, samples, per_key = r.placed_lse.shape
    per_dest = out_mine.shape[3] // HD
    dests = per_key // per_dest
    together = max(1, min(per_key, 512 // samples))
    stat_lanes = lse_mine.shape[3]
    slots, width, _ = r.gate_buf.shape
    tiles, units, tile = r.down_buf.shape
    subsets, sub_rows, _ = r.scaled.shape
    sub = state.shape[2] // subsets
    smp_rows = sub_rows // n_smp
    steps = units // UNITS
    all_steps, all_tiles = subsets * steps, subsets * tiles
    ratio = max(1, steps // tiles)
    w_rows = r.w_hbm.shape[0]
    per_slot = units // w_rows
    w_slots = -(-tiles // per_slot)
    block = min(8, r.cache.shape[1])

    def block_copy(i):
        rows_at = pl.ds(i * block, block)
        return pltpu.make_async_copy(
            r.cache_hbm.at[:, rows_at], r.cache.at[:, rows_at], r.cache_sem.at[i]
        )

    def w_block(t):
        first_row = pl.multiple_of(lax.rem(t, per_slot) * w_rows, w_rows)
        return r.down_buf.at[lax.div(t, per_slot), pl.ds(first_row, w_rows)]

    def w_copy(t):
        return pltpu.make_async_copy(r.w_hbm.at[:, columns(t, tile)], w_block(t), r.w_sem.at[t])

    def weight_copies(i):
        slot, t = lax.rem(i, slots), lax.rem(i, steps)
        return (
            pltpu.make_async_copy(
                r.gate_hbm.at[:, columns(t, UNITS)], r.gate_buf.at[slot], r.g_sem.at[slot]
            ),
            pltpu.make_async_copy(
                r.up_hbm.at[:, columns(t, UNITS)], r.up_buf.at[slot], r.u_sem.at[slot]
            ),
        )

    def down_copy(t):
        return pltpu.make_async_copy(
            r.down_hbm.at[:, columns(t, tile)], r.down_buf.at[t], r.d_sem.at[t]
        )

    for i in range(r.cache.shape[1] // block):
        block_copy(i).start()
    kv_copy = pltpu.make_async_copy(r.kv_hbm, kv_ref, r.kv_sem)
    kv_copy.start()
    announce(n, n_smp, c, s, h)

    by_owner = r.q[...].reshape(samples // sub, subsets, sub, r.q.shape[1])
    for k in range(subsets):
        r.q_rows[k] = by_owner[:, k].reshape(samples, r.q.shape[1])

    suffix_pieces(
        r.ids,
        r.lengths,
        sub,
        r.q_rows,
        block_copy,
        r.cache,
        r.row_q,
        r.row_out,
        r.row_piece,
        r.placed,
        r.placed_lse,
    )
    kv_copy.wait()

    @pl.loop(0, tiles)
    def _(t):
        w_copy(t).start()

    @pl.loop(0, min(slots, all_steps))
    def _(t):
        for copy in weight_copies(t):
            copy.start()

    for t in range(w_slots, tiles):
        down_copy(t).start()
    gather_round(n, n_smp)

    lanes_at = lax.broadcasted_iota(jnp.int32, (samples, 128), 1)

    def piece_copies(k, at, d):
        return (
            remote(
                out_mine.at[k, d], out_in.at[k, at], r.os.at[k, d], r.orr.at[k, at], {"ctx": d}
            ),
            remote(
                lse_mine.at[k, d], lse_in.at[k, at], r.ls.at[k, d], r.lr.at[k, at], {"ctx": d}
            ),
        )

    def prefix_piece(k, i):
        j = lax.rem(lax.div(c, dests) + 1 + i, keys)
        key = kv_ref[0, :, columns(j, HD)]
        value = kv_ref[1, :, columns(j, HD)]
        own = r.q_rows[k, :, columns(j, per_key * HD)]
        placed = r.placed[k, :, columns(j, per_key * HD)]
        placed_lse = r.placed_lse[j, k]
        tables = [jnp.zeros((samples, 128), jnp.float32) for _ in range(dests)]
        for g0 in range(0, per_key, together):
            rows = jnp.concatenate(
                [own[:, g * HD : (g + 1) * HD] for g in range(g0, g0 + together)], axis=0
            )
            scores = lax.dot_general(
                rows, key, (((1,), (1,)), ((), ())), preferred_element_type=jnp.float32
            ) * HD ** (-0.5)
            high = jnp.max(scores, axis=1, keepdims=True)
            weights = jnp.exp(scores - high)
            total = jnp.sum(weights, axis=1, keepdims=True)
            summed = (
                jnp.dot(weights.astype(jnp.bfloat16), value, preferred_element_type=jnp.float32)
                / total
            )
            lse = high + jnp.log(total)
            for g in range(g0, g0 + together):
                part = slice((g - g0) * samples, (g - g0 + 1) * samples)
                own_lse, other_lse = lse[part], placed_lse[:, g : g + 1]
                top = jnp.maximum(own_lse, other_lse)
                own_weight = jnp.exp(own_lse - top)
                other_weight = jnp.exp(other_lse - top)
                both = own_weight + other_weight
                merged = (
                    own_weight * summed[part]
                    + other_weight * placed[:, g * HD : (g + 1) * HD].astype(jnp.float32)
                ) / both
                at = g % per_dest
                out_mine[k, j * dests + g // per_dest, :, at * HD : (at + 1) * HD] = merged.astype(
                    jnp.bfloat16
                )
                q = g // per_dest
                tables[q] = jnp.where(lanes_at == at, top + jnp.log(both), tables[q])
        for q in range(dests):
            d = j * dests + q
            table = tables[q]
            if stat_lanes > samples:
                rest_of = jnp.zeros((stat_lanes - samples, 128), jnp.float32)
                table = jnp.concatenate([table, rest_of], axis=0)
            lse_mine[k, d] = table.T[:8]

            @pl.when(d != c)
            def _():
                for copy in piece_copies(k, c, d):
                    copy.start()

    def attn_copy(k, m):
        at = r.attn_rows.at[k, pl.ds(pl.multiple_of(s * samples, samples), samples)]
        return remote(
            at, at, r.xs.at[k, m - 1], r.xr.at[k, m - 1], {"smp": lax.rem(s + m, n_smp)}
        )

    def merge_pieces(k):
        for m in range(1, n):
            d = lax.rem(c + m, n)
            for copy in piece_copies(k, d, d):
                copy.wait_recv()
        lses = [lse_mine[k, c]] + [lse_in[k, lax.rem(c + m, n)] for m in range(1, n)]
        peak = functools.reduce(jnp.maximum, lses)
        scales = [jnp.exp(value - peak) for value in lses]
        denom = functools.reduce(jnp.add, scales)
        blank = jnp.zeros((120, stat_lanes), jnp.float32)
        scales = [
            jnp.concatenate([value / denom, blank], axis=0).T[:samples] for value in scales
        ]
        for j in range(per_dest):
            lanes = slice(j * HD, (j + 1) * HD)
            total = scales[0][:, j : j + 1] * out_mine[k, c, :, lanes].astype(jnp.float32)
            for m in range(1, n):
                piece = out_in[k, lax.rem(c + m, n), :, lanes].astype(jnp.float32)
                total = total + scales[m][:, j : j + 1] * piece
            at = pl.ds(pl.multiple_of(s * samples, samples), samples)
            r.attn_rows[k, at, lanes] = total.astype(jnp.bfloat16)
        for m in range(1, n_smp):
            attn_copy(k, m).start()

    def finish_attn(k):
        for m in range(1, n_smp):
            attn_copy(k, m).wait()
        for m in range(1, n):
            d = lax.rem(c + m, n)
            for copy in piece_copies(k, c, d):
                copy.wait_send()

    @pl.loop(0, keys)
    def _(i):
        prefix_piece(0, i)

    early = keys // 2 if subsets > 1 else 0
    gap = max(0, steps - tiles) if subsets > 1 else 0
    period = tiles + gap
    if subsets > 1:

        @pl.loop(0, early)
        def _(i):
            prefix_piece(1, i)

    merge_pieces(0)
    finish_attn(0)

    line = Line(
        n,
        c,
        h,
        r.buf_a,
        r.recv_a,
        r.buf_b,
        r.from_left,
        r.from_right,
        r.sa,
        r.ra,
        r.ss,
        r.rl,
        r.rr,
    )

    def rows_of(k):
        return pl.ds(pl.multiple_of(k * sub, sub), sub)

    def gather_copy(j, q, way, sems):
        k, t = lax.div(j, tiles), lax.rem(j, tiles)
        at = state.at[q, h, rows_of(k), columns(t, tile)]
        return remote(at, at, sems.at[j, q], r.gr.at[j, q], {"ctx": lax.rem(c + way, n)})

    def pass_copy(j, q):
        k, t = lax.div(j, tiles), lax.rem(j, tiles)
        at = state.at[q, h, rows_of(k), columns(t, tile)]
        return remote(at, at, r.fs.at[j, q], r.fr.at[j, q], {"head": 1 - h})

    def spread(j, q, right, left):
        @pl.when(right & (c < n - 1))
        def _():
            gather_copy(j, q, 1, r.gsr).start()

        @pl.when(left & (c > 0))
        def _():
            gather_copy(j, q, n - 1, r.gsl).start()

        pass_copy(j, q).start()

    def state_tile(i):
        at = lax.max(i, 0)
        k, t = lax.div(at, period), lax.rem(at, period)
        return (i >= 0) & (k < subsets) & (t < tiles), k * tiles + t

    def mixed_tile(i):
        return (i >= 0) & (i < all_tiles), i

    def project(i):
        live, j = state_tile(i)

        @pl.when(live)
        def _():
            k, t = lax.div(j, tiles), lax.rem(j, tiles)

            @pl.when(k == 0)
            def _():
                w_copy(t).wait()

            line.give(
                j, jnp.dot(r.attn_rows[k], w_block(t)[...], preferred_element_type=jnp.float32)
            )

        line.step(i, state_tile)
        ready, done = state_tile(i - n)

        @pl.when(ready)
        def _():
            j = done
            k, t = lax.div(j, tiles), lax.rem(j, tiles)
            own = line.finish(j) + r.res[rows_of(k), columns(t, tile)].astype(jnp.float32)
            state[c, h, rows_of(k), columns(t, tile)] = own.astype(jnp.bfloat16)
            spread(j, c, c >= 0, c >= 0)

        for q in range(n):
            here, moved = state_tile(i - n - lax.max(c - q, q - c))

            @pl.when((q != c) & here)
            def _():
                gather_copy(moved, q, 1, r.gsr).wait_recv()
                spread(moved, q, q < c, q > c)

    def smp_rows_of(p):
        return pl.ds(pl.multiple_of(p * smp_rows, smp_rows), smp_rows)

    def square_copy(k, m):
        p = lax.rem(s + m, n_smp)
        return remote(
            r.squares.at[k, smp_rows_of(p)],
            r.squares_in.at[k, m - 1],
            r.qs.at[k, m - 1],
            r.qr.at[k, m - 1],
            {"smp": p},
        )

    def prepare(k):
        @pl.loop(k * tiles, (k + 1) * tiles)
        def _(j):
            for q in range(n):
                pass_copy(j, q).wait()

        for owner in range(n):
            for core in range(2):
                wide = state[owner, core, rows_of(k)].astype(jnp.float32)
                first_row = (2 * owner + core) * sub
                rows = slice(first_row, first_row + sub)
                r.scaled[k, rows] = (wide * r.gain[...]).astype(jnp.bfloat16)
                sums = jnp.sum(wide * wide, axis=1, keepdims=True)
                r.squares[k, rows] = jnp.broadcast_to(sums, (sub, 128))
        for m in range(1, n_smp):
            square_copy(k, m).start()

    def part_copy(i, m):
        p = lax.rem(s + m, n_smp)
        return remote(
            r.part.at[i, smp_rows_of(p)],
            r.part_in.at[i, m - 1],
            r.ps.at[i, m - 1],
            r.pr.at[i, m - 1],
            {"smp": p},
        )

    def hidden_copy(i, m):
        k, t = lax.div(i, steps), lax.rem(i, steps)
        at = r.hidden.at[k, smp_rows_of(s), columns(t, UNITS)]
        return remote(
            at, at, r.hs.at[i, m - 1], r.hr.at[i, m - 1], {"smp": lax.rem(s + m, n_smp)}
        )

    def act(i):
        k, t = lax.div(i, steps), lax.rem(i, steps)

        @pl.when(t == 0)
        def _():
            for m in range(1, n_smp):
                square_copy(k, m).wait()

        both = r.part[i, smp_rows_of(s)].astype(jnp.float32)
        for m in range(1, n_smp):
            part_copy(i, m).wait()
            both = both + r.part_in[i, m - 1].astype(jnp.float32)
        total = r.squares[k, smp_rows_of(s)]
        for m in range(1, n_smp):
            total = total + r.squares_in[k, m - 1]
        factor = lax.rsqrt(total / (width * n_smp) + EPSILON)[:, :1]
        gate = factor * both[:, :UNITS]
        up = factor * both[:, UNITS:]
        value = gate / (1.0 + jnp.exp(-gate)) * up
        r.hidden[k, smp_rows_of(s), columns(t, UNITS)] = value.astype(jnp.bfloat16)
        for m in range(1, n_smp):
            hidden_copy(i, m).start()

    def gate_up(i):
        k, t = lax.div(i, steps), lax.rem(i, steps)

        @pl.when(t == 0)
        def _():
            prepare(k)

        for copy in weight_copies(i):
            copy.wait()
        slot = lax.rem(i, slots)
        r.part[i, :, :UNITS] = jnp.dot(
            r.scaled[k], r.gate_buf[slot], preferred_element_type=jnp.float32
        ).astype(jnp.bfloat16)
        r.part[i, :, UNITS:] = jnp.dot(
            r.scaled[k], r.up_buf[slot], preferred_element_type=jnp.float32
        ).astype(jnp.bfloat16)
        for m in range(1, n_smp):
            part_copy(i, m).start()

        @pl.when(i + slots < all_steps)
        def _():
            for copy in weight_copies(i + slots):
                copy.start()

    def down(j):
        k, t = lax.div(j, tiles), lax.rem(j, tiles)

        @pl.when(t == 0)
        def _():
            @pl.loop(0, steps)
            def _(u):
                for m in range(1, n_smp):
                    hidden_copy(k * steps + u, m).wait()

        @pl.when(k == 0)
        def _():
            down_copy(t).wait()

        line.drain(j)
        line.give(j, jnp.dot(r.hidden[k], r.down_buf[t], preferred_element_type=jnp.float32))

    def emit(j):
        k, t = lax.div(j, tiles), lax.rem(j, tiles)
        value = line.finish(j) + state[c, h, rows_of(k), columns(t, tile)].astype(jnp.float32)
        r.mixed[rows_of(k), columns(t, tile)] = value.astype(jnp.bfloat16)

    ahead = tiles + 2 * n - 1
    rest = period * (subsets - 1)
    free_at = max(0, period * (subsets - 1) + tiles - ahead)
    merge_at = max(keys - early, period - 2)

    @pl.loop(0, ahead)
    def _(i):
        if subsets > 1:

            @pl.when(i == period)
            def _():
                finish_attn(1)

        project(i)
        if subsets > 1:

            @pl.when(i < keys - early)
            def _():
                prefix_piece(1, i + early)

            @pl.when(i == merge_at)
            def _():
                merge_pieces(1)

    lag = min(2, all_steps)
    first = max(steps + lag + 1, rest)

    @pl.loop(0, first + (all_tiles + n) * ratio)
    def _(i):
        @pl.when(i < all_steps)
        def _():
            gate_up(i)

        @pl.when(i < rest)
        def _():
            project(i + ahead)

        @pl.when(i == free_at)
        def _():
            for t in range(w_slots):
                down_copy(t).start()

        @pl.when((i >= lag) & (i < all_steps + lag))
        def _():
            act(i - lag)

        j = lax.div(i - first, ratio)

        @pl.when((i >= first) & (lax.rem(i - first, ratio) == 0))
        def _():
            @pl.when(j < all_tiles)
            def _():
                down(j)

            line.step(j, mixed_tile)

            @pl.when(j >= n)
            def _():
                emit(j - n)

    @pl.loop(0, all_tiles)
    def _(j):
        line.drain(j)
        for q in range(n):

            @pl.when((q <= c) & (c < n - 1))
            def _():
                gather_copy(j, q, 1, r.gsr).wait_send()

            @pl.when((q >= c) & (c > 0))
            def _():
                gather_copy(j, q, n - 1, r.gsl).wait_send()


def layer(
    n, n_smp, ids, lengths, queries, prefix_cache, suffix_cache, w, residual, gain, gate, up, down
):
    samples, heads = queries.shape[0], queries.shape[1] // HD
    keys = prefix_cache.shape[2] // HD
    suffix_rows = suffix_cache.shape[1]
    features = queries.shape[1] // n
    rows, width = residual.shape
    sub = SUB if rows % SUB == 0 else rows
    subsets = rows // sub
    part_samples = samples // subsets
    stat_lanes = -(-part_samples // 128) * 128
    sub_rows = n * 2 * sub
    smp_rows = sub_rows // n_smp
    units = gate.shape[1]
    steps = units // UNITS
    tile = max(TILE, width // steps)
    tiles = width // tile
    all_steps, all_tiles = subsets * steps, subsets * tiles
    slots = min(SLOTS, all_steps)
    vmem = pl.BlockSpec(memory_space=pltpu.VMEM)
    hbm = pl.BlockSpec(memory_space=pl.ANY)
    dma = pltpu.SemaphoreType.DMA
    bf16, f32 = jnp.bfloat16, jnp.float32
    scratch = {
        "kv": pltpu.VMEM(prefix_cache.shape, bf16),
        "cache": pltpu.VMEM(suffix_cache.shape, bf16),
        "row_q": pltpu.VMEM((suffix_rows * heads, HD), f32),
        "row_out": pltpu.VMEM((suffix_rows * heads, HD), f32),
        "row_piece": pltpu.VMEM((suffix_rows, heads * HD), bf16),
        "q_rows": pltpu.VMEM((subsets, part_samples, heads * HD), bf16),
        "placed": pltpu.VMEM((subsets, part_samples, heads * HD), bf16),
        "placed_lse": pltpu.VMEM((keys, subsets, part_samples, heads // keys), f32),
        "out_mine": pltpu.VMEM((subsets, n, part_samples, features), bf16),
        "lse_mine": pltpu.VMEM((subsets, n, 8, stat_lanes), f32),
        "out_in": pltpu.VMEM((subsets, n, part_samples, features), bf16),
        "lse_in": pltpu.VMEM((subsets, n, 8, stat_lanes), f32),
        "attn_rows": pltpu.VMEM((subsets, sub_rows, features), bf16),
        "state": pltpu.VMEM((n, 2, rows, width), bf16),
        "scaled": pltpu.VMEM((subsets, sub_rows, width), bf16),
        "squares": pltpu.VMEM((subsets, sub_rows, 128), f32),
        "squares_in": pltpu.VMEM((subsets, n_smp - 1, smp_rows, 128), f32),
        "gate_buf": pltpu.VMEM((slots, width, UNITS), bf16),
        "up_buf": pltpu.VMEM((slots, width, UNITS), bf16),
        "down_buf": pltpu.VMEM((tiles, units, tile), bf16),
        "part": pltpu.VMEM((all_steps, sub_rows, 2 * UNITS), bf16),
        "part_in": pltpu.VMEM((all_steps, n_smp - 1, smp_rows, 2 * UNITS), bf16),
        "hidden": pltpu.VMEM((subsets, sub_rows, units), bf16),
        "buf_a": pltpu.VMEM((all_tiles, 2, n, sub, tile), bf16),
        "recv_a": pltpu.VMEM((all_tiles, n, sub, tile), bf16),
        "buf_b": pltpu.VMEM((all_tiles, n, sub, tile), bf16),
        "from_left": pltpu.VMEM((all_tiles, n, sub, tile), bf16),
        "from_right": pltpu.VMEM((all_tiles, n, sub, tile), bf16),
        "kv_sem": dma,
        "cache_sem": dma((suffix_rows // min(8, suffix_rows),)),
        "w_sem": dma((tiles,)),
        "g_sem": dma((slots,)),
        "u_sem": dma((slots,)),
        "d_sem": dma((tiles,)),
    }
    scratch |= {name: dma((subsets, n)) for name in ("os", "orr", "ls", "lr")}
    scratch |= {name: dma((subsets, n_smp - 1)) for name in ("xs", "xr", "qs", "qr")}
    scratch |= {name: dma((all_steps, n_smp - 1)) for name in ("ps", "pr", "hs", "hr")}
    scratch |= {name: dma((all_tiles,)) for name in ("sa", "ra")}
    scratch |= {
        name: dma((all_tiles, n)) for name in ("ss", "rl", "rr", "gsr", "gsl", "gr", "fs", "fr")
    }
    operands = {
        "ids": (ids, vmem),
        "lengths": (lengths, vmem),
        "q": (queries, vmem),
        "kv_hbm": (prefix_cache, hbm),
        "cache_hbm": (suffix_cache, hbm),
        "w_hbm": (w, hbm),
        "res": (residual, vmem),
        "gain": (gain, vmem),
        "gate_hbm": (gate, hbm),
        "up_hbm": (up, hbm),
        "down_hbm": (down, hbm),
    }
    names = (*operands, "mixed", *scratch)
    return pl.pallas_call(
        functools.partial(layer_kernel, n, n_smp, names),
        out_shape=jax.ShapeDtypeStruct((rows, width), bf16),
        in_specs=[spec for _, spec in operands.values()],
        out_specs=vmem,
        scratch_shapes=list(scratch.values()),
        compiler_params=pltpu.CompilerParams(
            collective_id=0, has_side_effects=True, vmem_limit_bytes=VMEM_BYTES
        ),
    )(*[value for value, _ in operands.values()])


def on_device(
    queries,
    prefix_cache,
    suffix_cache,
    suffix_length,
    cache_sample,
    residual,
    w_out,
    norm_gain,
    gate_matrix,
    w_up,
    w_down,
):
    group_rows = queries.shape[0]
    n, n_smp = lax.axis_size("ctx"), lax.axis_size("smp")
    rows_here = suffix_cache.shape[1]
    flat_index = lax.axis_index("ctx") * n_smp + lax.axis_index("smp")
    row_ids = lax.dynamic_slice_in_dim(cache_sample, flat_index * rows_here, rows_here, 0)
    local_ids = row_ids - lax.axis_index("smp") * group_rows
    local_ids = jnp.pad(local_ids, (0, 128 - rows_here), constant_values=-1)
    return layer(
        n,
        n_smp,
        local_ids[None, :],
        suffix_length[None, :],
        queries[:, 0],
        prefix_cache[:, :, 0],
        suffix_cache[:, :, :, 0],
        w_out[0],
        residual,
        norm_gain[None, :],
        gate_matrix,
        w_up,
        w_down,
    )


def solution(mesh):
    in_specs = (
        P(("group", "smp"), "head", None),
        P(None, ("group", "ctx"), "head", None),
        P(None, ("group", "ctx", "smp"), None, "head", None),
        P(("group", "smp")),
        P("group"),
        P(("group", "ctx", "head"), "smp"),
        P("head", "ctx", "smp"),
        P("smp"),
        P("smp", ("ctx", "head")),
        P("smp", ("ctx", "head")),
        P(("ctx", "head"), "smp"),
    )
    out_specs = P(("group", "ctx", "head"), "smp")
    return jax.shard_map(
        on_device, mesh=mesh, in_specs=in_specs, out_specs=out_specs, check_vma=False
    )
```

```python
import functools
import types

import jax
import jax.numpy as jnp
from jax import lax
from jax.experimental import pallas as pl
from jax.experimental.pallas import tpu as pltpu
from jax.sharding import PartitionSpec as P

D = 8192
QUERY_HEADS = 64
KEY_VALUE_HEADS = 8
HD = 128


EPSILON = 1e-05


MESH = pl.DeviceIdType.MESH
TILE = 1024
UNITS = 256
SLOTS = 3
SUB = 16
VMEM_BYTES = 67043328


def remote(src, dst, send_sem, recv_sem, where):
    return pltpu.make_async_remote_copy(
        src_ref=src,
        dst_ref=dst,
        send_sem=send_sem,
        recv_sem=recv_sem,
        device_id=where,
        device_id_type=MESH,
    )


def announce(n, n_smp, c, s, h):
    barrier = pltpu.get_barrier_semaphore()
    for k in range(1, n):
        pl.semaphore_signal(barrier, inc=1, device_id={"ctx": lax.rem(c + k, n)}, device_id_type=MESH)
    for k in range(1, n_smp):
        pl.semaphore_signal(
            barrier, inc=1, device_id={"smp": lax.rem(s + k, n_smp)}, device_id_type=MESH
        )
    pl.semaphore_signal(barrier, inc=1, device_id={"head": 1 - h}, device_id_type=MESH)


def gather_round(n, n_smp):
    pl.semaphore_wait(pltpu.get_barrier_semaphore(), (n - 1) + (n_smp - 1) + 1)


class Line:
    def __init__(self, n, c, h, buf_a, recv_a, buf_b, from_left, from_right, sa, ra, ss, rl, rr):
        self.n, self.c, self.h = n, c, h
        self.buf_a, self.recv_a, self.buf_b = buf_a, recv_a, buf_b
        self.from_left, self.from_right = from_left, from_right
        self.sa, self.ra, self.ss, self.rl, self.rr = sa, ra, ss, rl, rr
        self.tiles = buf_a.shape[0]

        @pl.when(c == 0)
        def _():
            from_left[:, 0] = jnp.zeros(from_left.shape[:1] + from_left.shape[2:], from_left.dtype)

        @pl.when(c == n - 1)
        def _():
            from_right[:, n - 1] = jnp.zeros(
                from_right.shape[:1] + from_right.shape[2:], from_right.dtype
            )

    def pair_copy(self, t):
        return remote(
            self.buf_a.at[t, 1 - self.h],
            self.recv_a.at[t],
            self.sa.at[t],
            self.ra.at[t],
            {"head": 1 - self.h},
        )

    def to_right(self, t, d):
        return remote(
            self.buf_b.at[t, d],
            self.from_left.at[t, d],
            self.ss.at[t, d],
            self.rl.at[t, d],
            {"ctx": lax.rem(self.c + 1, self.n)},
        )

    def to_left(self, t, d):
        return remote(
            self.buf_b.at[t, d],
            self.from_right.at[t, d],
            self.ss.at[t, d],
            self.rr.at[t, d],
            {"ctx": lax.rem(self.c + self.n - 1, self.n)},
        )

    def give(self, t, value):
        _, _, n, rows, width = self.buf_a.shape
        parts = value.reshape(n, 2, rows, width).astype(jnp.bfloat16)
        self.buf_a[t, 0] = parts[:, 0]
        self.buf_a[t, 1] = parts[:, 1]
        self.pair_copy(t).start()

    def middle(self, t):
        self.pair_copy(t).wait()
        both = self.buf_a[t, self.h].astype(jnp.float32) + self.recv_a[t].astype(jnp.float32)
        self.buf_b[t] = both.astype(jnp.bfloat16)

    def hop(self, t, inside, d, copy_of, arrived, first):
        @pl.when(inside)
        def _():
            @pl.when(jnp.logical_not(first))
            def _():
                copy_of(t, d).wait_recv()
                both = self.buf_b[t, d].astype(jnp.float32) + arrived[t, d].astype(jnp.float32)
                self.buf_b[t, d] = both.astype(jnp.bfloat16)

            copy_of(t, d).start()

    def step(self, i, tile_at):
        n, c = self.n, self.c
        live, t = tile_at(i - 1)

        @pl.when(live)
        def _():
            self.middle(t)

        live_r, t_r = tile_at(i - 1 - c)
        live_l, t_l = tile_at(i - n + c)
        for e in range(n - 1):
            right, left = n - 1 - e, e
            self.hop(t_r, live_r & (right > c), right, self.to_right, self.from_left, c == 0)
            self.hop(t_l, live_l & (left < c), left, self.to_left, self.from_right, c == n - 1)

    def finish(self, t):
        n, c = self.n, self.c

        @pl.when(c > 0)
        def _():
            self.to_right(t, c).wait_recv()

        @pl.when(c < n - 1)
        def _():
            self.to_left(t, c).wait_recv()

        return (
            self.buf_b[t, c].astype(jnp.float32)
            + self.from_left[t, c].astype(jnp.float32)
            + self.from_right[t, c].astype(jnp.float32)
        )

    def drain(self, t):
        for d in range(self.n):

            @pl.when(d > self.c)
            def _():
                self.to_right(t, d).wait_send()

            @pl.when(d < self.c)
            def _():
                self.to_left(t, d).wait_send()


def columns(t, width):
    return pl.ds(pl.multiple_of(t * width, width), width)


def suffix_pieces(
    ids_ref, lengths_ref, sub, q_ref, block_copy, cache, row_q, row_out, row_piece, placed, placed_lse
):
    _, rows, positions_here, width = cache.shape
    subsets, part_samples, features = q_ref.shape
    samples = subsets * part_samples
    keys, _, _, per_key = placed_lse.shape
    heads = features // HD
    block = min(8, rows)
    ids = ids_ref[...]
    sample_at = lax.broadcasted_iota(jnp.int32, (samples, ids.shape[1]), 0)
    picked = (sample_at == ids).astype(jnp.float32).T[:rows]
    lengths = jnp.sum(picked * lengths_ref[...].astype(jnp.float32), axis=1, keepdims=True)
    lengths = lengths.astype(jnp.int32)
    spot = ids // sub % subsets * part_samples + ids // (sub * subsets) * sub + ids % sub
    chosen = (sample_at == jnp.where(ids < 0, -1, spot)).astype(jnp.float32)
    picked = chosen.T[:rows].astype(jnp.bfloat16)
    all_q = q_ref[...].reshape(samples, features)
    for j in range(keys):
        lanes = slice(j * per_key * HD, (j + 1) * per_key * HD)
        own = jnp.dot(picked, all_q[:, lanes], preferred_element_type=jnp.float32)
        for g in range(per_key):
            row_q[pl.ds(j * per_key + g, rows, stride=heads), :] = own[:, g * HD : (g + 1) * HD]

    same = (
        lax.broadcasted_iota(jnp.int32, (heads, width), 0) // per_key
        == lax.broadcasted_iota(jnp.int32, (heads, width), 1) // HD
    )
    positions = lax.broadcasted_iota(jnp.int32, (heads, positions_here), 1)
    lanes_at = lax.broadcasted_iota(jnp.int32, (heads, ids.shape[1]), 1)
    table = jnp.zeros((heads, ids.shape[1]), jnp.float32)
    for r0 in range(0, rows, block):
        block_copy(r0 // block).wait()
        scores = []
        for r in range(r0, r0 + block):
            q = row_q[r * heads : (r + 1) * heads]
            spread = jnp.concatenate([q] * keys, axis=1)
            spread = jnp.where(same, spread, 0.0).astype(jnp.bfloat16)
            one = lax.dot_general(
                spread, cache[0, r], (((1,), (1,)), ((), ())), preferred_element_type=jnp.float32
            )
            live = positions < lengths[r : r + 1]
            scores.append(jnp.where(live, one * HD ** (-0.5), -jnp.inf))
        scores = jnp.concatenate(scores, axis=0)
        high = jnp.max(scores, axis=1, keepdims=True)
        weights = jnp.exp(scores - high)
        total = jnp.sum(weights, axis=1, keepdims=True)
        lse = high + jnp.log(total)
        weights = weights.astype(jnp.bfloat16)
        for r in range(r0, r0 + block):
            part = slice((r - r0) * heads, (r - r0 + 1) * heads)
            summed = jnp.dot(weights[part], cache[1, r], preferred_element_type=jnp.float32)
            own = jnp.concatenate(
                [
                    summed[j * per_key : (j + 1) * per_key, j * HD : (j + 1) * HD]
                    for j in range(keys)
                ],
                axis=0,
            )
            piece = (own / total[part]).astype(jnp.bfloat16)
            row_out[r * heads : (r + 1) * heads] = piece.astype(jnp.float32)
            table = jnp.where(lanes_at == r, lse[part], table)

    found = jnp.sum(chosen, axis=1, keepdims=True) > 0.0
    for k in range(heads):
        row_piece[:, k * HD : (k + 1) * HD] = row_out[pl.ds(k, rows, stride=heads), :].astype(
            jnp.bfloat16
        )
    to_sample = chosen[:, :rows].astype(jnp.bfloat16)
    for j in range(keys):
        lanes = slice(j * per_key * HD, (j + 1) * per_key * HD)
        one = jnp.dot(to_sample, row_piece[:, lanes], preferred_element_type=jnp.float32)
        placed[:, :, lanes] = one.astype(jnp.bfloat16).reshape(subsets, part_samples, -1)
        one = lax.dot_general(
            chosen,
            table[j * per_key : (j + 1) * per_key],
            (((1,), (1,)), ((), ())),
            precision=lax.Precision.HIGHEST,
            preferred_element_type=jnp.float32,
        )
        one = jnp.where(found, one, -1e30)
        placed_lse[j] = one.reshape(subsets, part_samples, per_key)


def layer_kernel(n, n_smp, names, *refs):
    r = types.SimpleNamespace(**dict(zip(names, refs, strict=True)))
    c, s, h = lax.axis_index("ctx"), lax.axis_index("smp"), lax.axis_index("head")
    kv_ref, state = r.kv, r.state
    out_mine, lse_mine, out_in, lse_in = r.out_mine, r.lse_mine, r.out_in, r.lse_in
    keys, _, samples, per_key = r.placed_lse.shape
    per_dest = out_mine.shape[3] // HD
    dests = per_key // per_dest
    together = max(1, min(per_key, 512 // samples))
    stat_lanes = lse_mine.shape[3]
    slots, width, _ = r.gate_buf.shape
    tiles, units, tile = r.down_buf.shape
    subsets, sub_rows, _ = r.scaled.shape
    sub = state.shape[2] // subsets
    smp_rows = sub_rows // n_smp
    steps = units // UNITS
    all_steps, all_tiles = subsets * steps, subsets * tiles
    ratio = max(1, steps // tiles)
    w_rows = r.w_hbm.shape[0]
    per_slot = units // w_rows
    w_slots = -(-tiles // per_slot)
    block = min(8, r.cache.shape[1])

    def block_copy(i):
        rows_at = pl.ds(i * block, block)
        return pltpu.make_async_copy(
            r.cache_hbm.at[:, rows_at], r.cache.at[:, rows_at], r.cache_sem.at[i]
        )

    def w_block(t):
        first_row = pl.multiple_of(lax.rem(t, per_slot) * w_rows, w_rows)
        return r.down_buf.at[lax.div(t, per_slot), pl.ds(first_row, w_rows)]

    def w_copy(t):
        return pltpu.make_async_copy(r.w_hbm.at[:, columns(t, tile)], w_block(t), r.w_sem.at[t])

    def weight_copies(i):
        slot, t = lax.rem(i, slots), lax.rem(i, steps)
        return (
            pltpu.make_async_copy(
                r.gate_hbm.at[:, columns(t, UNITS)], r.gate_buf.at[slot], r.g_sem.at[slot]
            ),
            pltpu.make_async_copy(
                r.up_hbm.at[:, columns(t, UNITS)], r.up_buf.at[slot], r.u_sem.at[slot]
            ),
        )

    def down_copy(t):
        return pltpu.make_async_copy(
            r.down_hbm.at[:, columns(t, tile)], r.down_buf.at[t], r.d_sem.at[t]
        )

    for i in range(r.cache.shape[1] // block):
        block_copy(i).start()
    kv_copy = pltpu.make_async_copy(r.kv_hbm, kv_ref, r.kv_sem)
    kv_copy.start()
    announce(n, n_smp, c, s, h)

    by_owner = r.q[...].reshape(samples // sub, subsets, sub, r.q.shape[1])
    for k in range(subsets):
        r.q_rows[k] = by_owner[:, k].reshape(samples, r.q.shape[1])

    suffix_pieces(
        r.ids,
        r.lengths,
        sub,
        r.q_rows,
        block_copy,
        r.cache,
        r.row_q,
        r.row_out,
        r.row_piece,
        r.placed,
        r.placed_lse,
    )
    kv_copy.wait()

    @pl.loop(0, tiles)
    def _(t):
        w_copy(t).start()

    @pl.loop(0, min(slots, all_steps))
    def _(t):
        for copy in weight_copies(t):
            copy.start()

    for t in range(w_slots, tiles):
        down_copy(t).start()
    gather_round(n, n_smp)

    lanes_at = lax.broadcasted_iota(jnp.int32, (samples, 128), 1)

    def piece_copies(k, at, d):
        return (
            remote(
                out_mine.at[k, d], out_in.at[k, at], r.os.at[k, d], r.orr.at[k, at], {"ctx": d}
            ),
            remote(
                lse_mine.at[k, d], lse_in.at[k, at], r.ls.at[k, d], r.lr.at[k, at], {"ctx": d}
            ),
        )

    def prefix_piece(k, i):
        j = lax.rem(lax.div(c, dests) + 1 + i, keys)
        key = kv_ref[0, :, columns(j, HD)]
        value = kv_ref[1, :, columns(j, HD)]
        own = r.q_rows[k, :, columns(j, per_key * HD)]
        placed = r.placed[k, :, columns(j, per_key * HD)]
        placed_lse = r.placed_lse[j, k]
        tables = [jnp.zeros((samples, 128), jnp.float32) for _ in range(dests)]
        for g0 in range(0, per_key, together):
            rows = jnp.concatenate(
                [own[:, g * HD : (g + 1) * HD] for g in range(g0, g0 + together)], axis=0
            )
            scores = lax.dot_general(
                rows, key, (((1,), (1,)), ((), ())), preferred_element_type=jnp.float32
            ) * HD ** (-0.5)
            high = jnp.max(scores, axis=1, keepdims=True)
            weights = jnp.exp(scores - high)
            total = jnp.sum(weights, axis=1, keepdims=True)
            summed = (
                jnp.dot(weights.astype(jnp.bfloat16), value, preferred_element_type=jnp.float32)
                / total
            )
            lse = high + jnp.log(total)
            for g in range(g0, g0 + together):
                part = slice((g - g0) * samples, (g - g0 + 1) * samples)
                own_lse, other_lse = lse[part], placed_lse[:, g : g + 1]
                top = jnp.maximum(own_lse, other_lse)
                own_weight = jnp.exp(own_lse - top)
                other_weight = jnp.exp(other_lse - top)
                both = own_weight + other_weight
                merged = (
                    own_weight * summed[part]
                    + other_weight * placed[:, g * HD : (g + 1) * HD].astype(jnp.float32)
                ) / both
                at = g % per_dest
                out_mine[k, j * dests + g // per_dest, :, at * HD : (at + 1) * HD] = merged.astype(
                    jnp.bfloat16
                )
                q = g // per_dest
                tables[q] = jnp.where(lanes_at == at, top + jnp.log(both), tables[q])
        for q in range(dests):
            d = j * dests + q
            table = tables[q]
            if stat_lanes > samples:
                rest_of = jnp.zeros((stat_lanes - samples, 128), jnp.float32)
                table = jnp.concatenate([table, rest_of], axis=0)
            lse_mine[k, d] = table.T[:8]

            @pl.when(d != c)
            def _():
                for copy in piece_copies(k, c, d):
                    copy.start()

    def attn_copy(k, m):
        at = r.attn_rows.at[k, pl.ds(pl.multiple_of(s * samples, samples), samples)]
        return remote(
            at, at, r.xs.at[k, m - 1], r.xr.at[k, m - 1], {"smp": lax.rem(s + m, n_smp)}
        )

    def merge_pieces(k):
        for m in range(1, n):
            d = lax.rem(c + m, n)
            for copy in piece_copies(k, d, d):
                copy.wait_recv()
        lses = [lse_mine[k, c]] + [lse_in[k, lax.rem(c + m, n)] for m in range(1, n)]
        peak = functools.reduce(jnp.maximum, lses)
        scales = [jnp.exp(value - peak) for value in lses]
        denom = functools.reduce(jnp.add, scales)
        blank = jnp.zeros((120, stat_lanes), jnp.float32)
        scales = [
            jnp.concatenate([value / denom, blank], axis=0).T[:samples] for value in scales
        ]
        for j in range(per_dest):
            lanes = slice(j * HD, (j + 1) * HD)
            total = scales[0][:, j : j + 1] * out_mine[k, c, :, lanes].astype(jnp.float32)
            for m in range(1, n):
                piece = out_in[k, lax.rem(c + m, n), :, lanes].astype(jnp.float32)
                total = total + scales[m][:, j : j + 1] * piece
            at = pl.ds(pl.multiple_of(s * samples, samples), samples)
            r.attn_rows[k, at, lanes] = total.astype(jnp.bfloat16)
        for m in range(1, n_smp):
            attn_copy(k, m).start()

    def finish_attn(k):
        for m in range(1, n_smp):
            attn_copy(k, m).wait()
        for m in range(1, n):
            d = lax.rem(c + m, n)
            for copy in piece_copies(k, c, d):
                copy.wait_send()

    @pl.loop(0, keys)
    def _(i):
        prefix_piece(0, i)

    early = keys // 2 if subsets > 1 else 0
    gap = max(0, steps - tiles) // 2 if subsets > 1 else 0
    period = tiles + gap
    if subsets > 1:

        @pl.loop(0, early)
        def _(i):
            prefix_piece(1, i)

    merge_pieces(0)
    if subsets > 1:

        @pl.loop(early, keys)
        def _(i):
            prefix_piece(1, i)

    finish_attn(0)

    line = Line(
        n,
        c,
        h,
        r.buf_a,
        r.recv_a,
        r.buf_b,
        r.from_left,
        r.from_right,
        r.sa,
        r.ra,
        r.ss,
        r.rl,
        r.rr,
    )

    def rows_of(k):
        return pl.ds(pl.multiple_of(k * sub, sub), sub)

    def gather_copy(j, q, way, sems):
        k, t = lax.div(j, tiles), lax.rem(j, tiles)
        at = state.at[q, h, rows_of(k), columns(t, tile)]
        return remote(at, at, sems.at[j, q], r.gr.at[j, q], {"ctx": lax.rem(c + way, n)})

    def pass_copy(j, q):
        k, t = lax.div(j, tiles), lax.rem(j, tiles)
        at = state.at[q, h, rows_of(k), columns(t, tile)]
        return remote(at, at, r.fs.at[j, q], r.fr.at[j, q], {"head": 1 - h})

    def spread(j, q, right, left):
        @pl.when(right & (c < n - 1))
        def _():
            gather_copy(j, q, 1, r.gsr).start()

        @pl.when(left & (c > 0))
        def _():
            gather_copy(j, q, n - 1, r.gsl).start()

        pass_copy(j, q).start()

    def state_tile(i):
        at = lax.max(i, 0)
        k, t = lax.div(at, period), lax.rem(at, period)
        return (i >= 0) & (k < subsets) & (t < tiles), k * tiles + t

    def mixed_tile(i):
        return (i >= 0) & (i < all_tiles), i

    def project(i):
        live, j = state_tile(i)

        @pl.when(live)
        def _():
            k, t = lax.div(j, tiles), lax.rem(j, tiles)

            @pl.when(k == 0)
            def _():
                w_copy(t).wait()

            line.give(
                j, jnp.dot(r.attn_rows[k], w_block(t)[...], preferred_element_type=jnp.float32)
            )

        line.step(i, state_tile)
        ready, done = state_tile(i - n)

        @pl.when(ready)
        def _():
            j = done
            k, t = lax.div(j, tiles), lax.rem(j, tiles)
            own = line.finish(j) + r.res[rows_of(k), columns(t, tile)].astype(jnp.float32)
            state[c, h, rows_of(k), columns(t, tile)] = own.astype(jnp.bfloat16)
            spread(j, c, c >= 0, c >= 0)

        for q in range(n):
            here, moved = state_tile(i - n - lax.max(c - q, q - c))

            @pl.when((q != c) & here)
            def _():
                gather_copy(moved, q, 1, r.gsr).wait_recv()
                spread(moved, q, q < c, q > c)

    def smp_rows_of(p):
        return pl.ds(pl.multiple_of(p * smp_rows, smp_rows), smp_rows)

    def square_copy(k, m):
        p = lax.rem(s + m, n_smp)
        return remote(
            r.squares.at[k, smp_rows_of(p)],
            r.squares_in.at[k, m - 1],
            r.qs.at[k, m - 1],
            r.qr.at[k, m - 1],
            {"smp": p},
        )

    def prepare(k):
        @pl.loop(k * tiles, (k + 1) * tiles)
        def _(j):
            for q in range(n):
                pass_copy(j, q).wait()

        for owner in range(n):
            for core in range(2):
                wide = state[owner, core, rows_of(k)].astype(jnp.float32)
                first_row = (2 * owner + core) * sub
                rows = slice(first_row, first_row + sub)
                r.scaled[k, rows] = (wide * r.gain[...]).astype(jnp.bfloat16)
                sums = jnp.sum(wide * wide, axis=1, keepdims=True)
                r.squares[k, rows] = jnp.broadcast_to(sums, (sub, 128))
        for m in range(1, n_smp):
            square_copy(k, m).start()

    def part_copy(i, m):
        p = lax.rem(s + m, n_smp)
        return remote(
            r.part.at[i, smp_rows_of(p)],
            r.part_in.at[i, m - 1],
            r.ps.at[i, m - 1],
            r.pr.at[i, m - 1],
            {"smp": p},
        )

    def hidden_copy(i, m):
        k, t = lax.div(i, steps), lax.rem(i, steps)
        at = r.hidden.at[k, smp_rows_of(s), columns(t, UNITS)]
        return remote(
            at, at, r.hs.at[i, m - 1], r.hr.at[i, m - 1], {"smp": lax.rem(s + m, n_smp)}
        )

    def act(i):
        k, t = lax.div(i, steps), lax.rem(i, steps)

        @pl.when(t == 0)
        def _():
            for m in range(1, n_smp):
                square_copy(k, m).wait()

        both = r.part[i, smp_rows_of(s)].astype(jnp.float32)
        for m in range(1, n_smp):
            part_copy(i, m).wait()
            both = both + r.part_in[i, m - 1].astype(jnp.float32)
        total = r.squares[k, smp_rows_of(s)]
        for m in range(1, n_smp):
            total = total + r.squares_in[k, m - 1]
        factor = lax.rsqrt(total / (width * n_smp) + EPSILON)[:, :1]
        gate = factor * both[:, :UNITS]
        up = factor * both[:, UNITS:]
        value = gate / (1.0 + jnp.exp(-gate)) * up
        r.hidden[k, smp_rows_of(s), columns(t, UNITS)] = value.astype(jnp.bfloat16)
        for m in range(1, n_smp):
            hidden_copy(i, m).start()

    def gate_up(i):
        k, t = lax.div(i, steps), lax.rem(i, steps)

        @pl.when(t == 0)
        def _():
            prepare(k)

        for copy in weight_copies(i):
            copy.wait()
        slot = lax.rem(i, slots)
        r.part[i, :, :UNITS] = jnp.dot(
            r.scaled[k], r.gate_buf[slot], preferred_element_type=jnp.float32
        ).astype(jnp.bfloat16)
        r.part[i, :, UNITS:] = jnp.dot(
            r.scaled[k], r.up_buf[slot], preferred_element_type=jnp.float32
        ).astype(jnp.bfloat16)
        for m in range(1, n_smp):
            part_copy(i, m).start()

        @pl.when(i + slots < all_steps)
        def _():
            for copy in weight_copies(i + slots):
                copy.start()

    def down(j):
        k, t = lax.div(j, tiles), lax.rem(j, tiles)

        @pl.when(t == 0)
        def _():
            @pl.loop(0, steps)
            def _(u):
                for m in range(1, n_smp):
                    hidden_copy(k * steps + u, m).wait()

        @pl.when(k == 0)
        def _():
            down_copy(t).wait()

        line.drain(j)
        line.give(j, jnp.dot(r.hidden[k], r.down_buf[t], preferred_element_type=jnp.float32))

    def emit(j):
        k, t = lax.div(j, tiles), lax.rem(j, tiles)
        value = line.finish(j) + state[c, h, rows_of(k), columns(t, tile)].astype(jnp.float32)
        r.mixed[rows_of(k), columns(t, tile)] = value.astype(jnp.bfloat16)

    ahead = tiles + 2 * n - 1
    rest = period * (subsets - 1)
    free_at = max(0, period * (subsets - 1) + tiles - ahead)
    merge_at = max(0, period - 2)

    @pl.loop(0, ahead)
    def _(i):
        if subsets > 1:

            @pl.when(i == period)
            def _():
                finish_attn(1)

        project(i)
        if subsets > 1:

            @pl.when(i == merge_at)
            def _():
                merge_pieces(1)

    lag = min(2, all_steps)
    first = max(steps + lag + 1, rest)

    @pl.loop(0, first + (all_tiles + n) * ratio)
    def _(i):
        @pl.when(i < all_steps)
        def _():
            gate_up(i)

        @pl.when(i < rest)
        def _():
            project(i + ahead)

        @pl.when(i == free_at)
        def _():
            for t in range(w_slots):
                down_copy(t).start()

        @pl.when((i >= lag) & (i < all_steps + lag))
        def _():
            act(i - lag)

        j = lax.div(i - first, ratio)

        @pl.when((i >= first) & (lax.rem(i - first, ratio) == 0))
        def _():
            @pl.when(j < all_tiles)
            def _():
                down(j)

            line.step(j, mixed_tile)

            @pl.when(j >= n)
            def _():
                emit(j - n)

    @pl.loop(0, all_tiles)
    def _(j):
        line.drain(j)
        for q in range(n):

            @pl.when((q <= c) & (c < n - 1))
            def _():
                gather_copy(j, q, 1, r.gsr).wait_send()

            @pl.when((q >= c) & (c > 0))
            def _():
                gather_copy(j, q, n - 1, r.gsl).wait_send()


def layer(
    n, n_smp, ids, lengths, queries, prefix_cache, suffix_cache, w, residual, gain, gate, up, down
):
    samples, heads = queries.shape[0], queries.shape[1] // HD
    keys = prefix_cache.shape[2] // HD
    suffix_rows = suffix_cache.shape[1]
    features = queries.shape[1] // n
    rows, width = residual.shape
    sub = SUB if rows % SUB == 0 else rows
    subsets = rows // sub
    part_samples = samples // subsets
    stat_lanes = -(-part_samples // 128) * 128
    sub_rows = n * 2 * sub
    smp_rows = sub_rows // n_smp
    units = gate.shape[1]
    steps = units // UNITS
    tile = max(TILE, width // steps)
    tiles = width // tile
    all_steps, all_tiles = subsets * steps, subsets * tiles
    slots = min(SLOTS, all_steps)
    vmem = pl.BlockSpec(memory_space=pltpu.VMEM)
    hbm = pl.BlockSpec(memory_space=pl.ANY)
    dma = pltpu.SemaphoreType.DMA
    bf16, f32 = jnp.bfloat16, jnp.float32
    scratch = {
        "kv": pltpu.VMEM(prefix_cache.shape, bf16),
        "cache": pltpu.VMEM(suffix_cache.shape, bf16),
        "row_q": pltpu.VMEM((suffix_rows * heads, HD), f32),
        "row_out": pltpu.VMEM((suffix_rows * heads, HD), f32),
        "row_piece": pltpu.VMEM((suffix_rows, heads * HD), bf16),
        "q_rows": pltpu.VMEM((subsets, part_samples, heads * HD), bf16),
        "placed": pltpu.VMEM((subsets, part_samples, heads * HD), bf16),
        "placed_lse": pltpu.VMEM((keys, subsets, part_samples, heads // keys), f32),
        "out_mine": pltpu.VMEM((subsets, n, part_samples, features), bf16),
        "lse_mine": pltpu.VMEM((subsets, n, 8, stat_lanes), f32),
        "out_in": pltpu.VMEM((subsets, n, part_samples, features), bf16),
        "lse_in": pltpu.VMEM((subsets, n, 8, stat_lanes), f32),
        "attn_rows": pltpu.VMEM((subsets, sub_rows, features), bf16),
        "state": pltpu.VMEM((n, 2, rows, width), bf16),
        "scaled": pltpu.VMEM((subsets, sub_rows, width), bf16),
        "squares": pltpu.VMEM((subsets, sub_rows, 128), f32),
        "squares_in": pltpu.VMEM((subsets, n_smp - 1, smp_rows, 128), f32),
        "gate_buf": pltpu.VMEM((slots, width, UNITS), bf16),
        "up_buf": pltpu.VMEM((slots, width, UNITS), bf16),
        "down_buf": pltpu.VMEM((tiles, units, tile), bf16),
        "part": pltpu.VMEM((all_steps, sub_rows, 2 * UNITS), bf16),
        "part_in": pltpu.VMEM((all_steps, n_smp - 1, smp_rows, 2 * UNITS), bf16),
        "hidden": pltpu.VMEM((subsets, sub_rows, units), bf16),
        "buf_a": pltpu.VMEM((all_tiles, 2, n, sub, tile), bf16),
        "recv_a": pltpu.VMEM((all_tiles, n, sub, tile), bf16),
        "buf_b": pltpu.VMEM((all_tiles, n, sub, tile), bf16),
        "from_left": pltpu.VMEM((all_tiles, n, sub, tile), bf16),
        "from_right": pltpu.VMEM((all_tiles, n, sub, tile), bf16),
        "kv_sem": dma,
        "cache_sem": dma((suffix_rows // min(8, suffix_rows),)),
        "w_sem": dma((tiles,)),
        "g_sem": dma((slots,)),
        "u_sem": dma((slots,)),
        "d_sem": dma((tiles,)),
    }
    scratch |= {name: dma((subsets, n)) for name in ("os", "orr", "ls", "lr")}
    scratch |= {name: dma((subsets, n_smp - 1)) for name in ("xs", "xr", "qs", "qr")}
    scratch |= {name: dma((all_steps, n_smp - 1)) for name in ("ps", "pr", "hs", "hr")}
    scratch |= {name: dma((all_tiles,)) for name in ("sa", "ra")}
    scratch |= {
        name: dma((all_tiles, n)) for name in ("ss", "rl", "rr", "gsr", "gsl", "gr", "fs", "fr")
    }
    operands = {
        "ids": (ids, vmem),
        "lengths": (lengths, vmem),
        "q": (queries, vmem),
        "kv_hbm": (prefix_cache, hbm),
        "cache_hbm": (suffix_cache, hbm),
        "w_hbm": (w, hbm),
        "res": (residual, vmem),
        "gain": (gain, vmem),
        "gate_hbm": (gate, hbm),
        "up_hbm": (up, hbm),
        "down_hbm": (down, hbm),
    }
    names = (*operands, "mixed", *scratch)
    return pl.pallas_call(
        functools.partial(layer_kernel, n, n_smp, names),
        out_shape=jax.ShapeDtypeStruct((rows, width), bf16),
        in_specs=[spec for _, spec in operands.values()],
        out_specs=vmem,
        scratch_shapes=list(scratch.values()),
        compiler_params=pltpu.CompilerParams(
            collective_id=0, has_side_effects=True, vmem_limit_bytes=VMEM_BYTES
        ),
    )(*[value for value, _ in operands.values()])


def on_device(
    queries,
    prefix_cache,
    suffix_cache,
    suffix_length,
    cache_sample,
    residual,
    w_out,
    norm_gain,
    gate_matrix,
    w_up,
    w_down,
):
    group_rows = queries.shape[0]
    n, n_smp = lax.axis_size("ctx"), lax.axis_size("smp")
    rows_here = suffix_cache.shape[1]
    flat_index = lax.axis_index("ctx") * n_smp + lax.axis_index("smp")
    row_ids = lax.dynamic_slice_in_dim(cache_sample, flat_index * rows_here, rows_here, 0)
    local_ids = row_ids - lax.axis_index("smp") * group_rows
    local_ids = jnp.pad(local_ids, (0, 128 - rows_here), constant_values=-1)
    return layer(
        n,
        n_smp,
        local_ids[None, :],
        suffix_length[None, :],
        queries[:, 0],
        prefix_cache[:, :, 0],
        suffix_cache[:, :, :, 0],
        w_out[0],
        residual,
        norm_gain[None, :],
        gate_matrix,
        w_up,
        w_down,
    )


def solution(mesh):
    in_specs = (
        P(("group", "smp"), "head", None),
        P(None, ("group", "ctx"), "head", None),
        P(None, ("group", "ctx", "smp"), None, "head", None),
        P(("group", "smp")),
        P("group"),
        P(("group", "ctx", "head"), "smp"),
        P("head", "ctx", "smp"),
        P("smp"),
        P("smp", ("ctx", "head")),
        P("smp", ("ctx", "head")),
        P(("ctx", "head"), "smp"),
    )
    out_specs = P(("group", "ctx", "head"), "smp")
    return jax.shard_map(
        on_device, mesh=mesh, in_specs=in_specs, out_specs=out_specs, check_vma=False
    )
```

```python
import functools
import types

import jax
import jax.numpy as jnp
from jax import lax
from jax.experimental import pallas as pl
from jax.experimental.pallas import tpu as pltpu
from jax.sharding import PartitionSpec as P

D = 8192
QUERY_HEADS = 64
KEY_VALUE_HEADS = 8
HD = 128


EPSILON = 1e-05


MESH = pl.DeviceIdType.MESH
TILE = 1024
UNITS = 256
SLOTS = 3
SUB = 16
VMEM_BYTES = 67043328


def remote(src, dst, send_sem, recv_sem, where):
    return pltpu.make_async_remote_copy(
        src_ref=src,
        dst_ref=dst,
        send_sem=send_sem,
        recv_sem=recv_sem,
        device_id=where,
        device_id_type=MESH,
    )


def announce(n, n_smp, c, s, h):
    barrier = pltpu.get_barrier_semaphore()
    for k in range(1, n):
        pl.semaphore_signal(barrier, inc=1, device_id={"ctx": lax.rem(c + k, n)}, device_id_type=MESH)
    for k in range(1, n_smp):
        pl.semaphore_signal(
            barrier, inc=1, device_id={"smp": lax.rem(s + k, n_smp)}, device_id_type=MESH
        )
    pl.semaphore_signal(barrier, inc=1, device_id={"head": 1 - h}, device_id_type=MESH)


def gather_round(n, n_smp):
    pl.semaphore_wait(pltpu.get_barrier_semaphore(), (n - 1) + (n_smp - 1) + 1)


class Line:
    def __init__(self, n, c, h, buf_a, recv_a, buf_b, from_left, from_right, sa, ra, ss, rl, rr):
        self.n, self.c, self.h = n, c, h
        self.buf_a, self.recv_a, self.buf_b = buf_a, recv_a, buf_b
        self.from_left, self.from_right = from_left, from_right
        self.sa, self.ra, self.ss, self.rl, self.rr = sa, ra, ss, rl, rr
        self.tiles = buf_a.shape[0]

        @pl.when(c == 0)
        def _():
            from_left[:, 0] = jnp.zeros(from_left.shape[:1] + from_left.shape[2:], from_left.dtype)

        @pl.when(c == n - 1)
        def _():
            from_right[:, n - 1] = jnp.zeros(
                from_right.shape[:1] + from_right.shape[2:], from_right.dtype
            )

    def pair_copy(self, t):
        return remote(
            self.buf_a.at[t, 1 - self.h],
            self.recv_a.at[t],
            self.sa.at[t],
            self.ra.at[t],
            {"head": 1 - self.h},
        )

    def to_right(self, t, d):
        return remote(
            self.buf_b.at[t, d],
            self.from_left.at[t, d],
            self.ss.at[t, d],
            self.rl.at[t, d],
            {"ctx": lax.rem(self.c + 1, self.n)},
        )

    def to_left(self, t, d):
        return remote(
            self.buf_b.at[t, d],
            self.from_right.at[t, d],
            self.ss.at[t, d],
            self.rr.at[t, d],
            {"ctx": lax.rem(self.c + self.n - 1, self.n)},
        )

    def give(self, t, value):
        _, _, n, rows, width = self.buf_a.shape
        parts = value.reshape(n, 2, rows, width).astype(jnp.bfloat16)
        self.buf_a[t, 0] = parts[:, 0]
        self.buf_a[t, 1] = parts[:, 1]
        self.pair_copy(t).start()

    def middle(self, t):
        self.pair_copy(t).wait()
        both = self.buf_a[t, self.h].astype(jnp.float32) + self.recv_a[t].astype(jnp.float32)
        self.buf_b[t] = both.astype(jnp.bfloat16)

    def hop(self, t, inside, d, copy_of, arrived, first):
        @pl.when(inside)
        def _():
            @pl.when(jnp.logical_not(first))
            def _():
                copy_of(t, d).wait_recv()
                both = self.buf_b[t, d].astype(jnp.float32) + arrived[t, d].astype(jnp.float32)
                self.buf_b[t, d] = both.astype(jnp.bfloat16)

            copy_of(t, d).start()

    def step(self, i, tile_at):
        n, c = self.n, self.c
        live, t = tile_at(i - 1)

        @pl.when(live)
        def _():
            self.middle(t)

        live_r, t_r = tile_at(i - 1 - c)
        live_l, t_l = tile_at(i - n + c)
        for e in range(n - 1):
            right, left = n - 1 - e, e
            self.hop(t_r, live_r & (right > c), right, self.to_right, self.from_left, c == 0)
            self.hop(t_l, live_l & (left < c), left, self.to_left, self.from_right, c == n - 1)

    def finish(self, t):
        n, c = self.n, self.c

        @pl.when(c > 0)
        def _():
            self.to_right(t, c).wait_recv()

        @pl.when(c < n - 1)
        def _():
            self.to_left(t, c).wait_recv()

        return (
            self.buf_b[t, c].astype(jnp.float32)
            + self.from_left[t, c].astype(jnp.float32)
            + self.from_right[t, c].astype(jnp.float32)
        )

    def drain(self, t):
        for d in range(self.n):

            @pl.when(d > self.c)
            def _():
                self.to_right(t, d).wait_send()

            @pl.when(d < self.c)
            def _():
                self.to_left(t, d).wait_send()


def columns(t, width):
    return pl.ds(pl.multiple_of(t * width, width), width)


def suffix_pieces(
    ids_ref, lengths_ref, sub, q_ref, block_copy, cache, row_q, row_out, row_piece, placed, placed_lse
):
    _, rows, positions_here, width = cache.shape
    subsets, part_samples, features = q_ref.shape
    samples = subsets * part_samples
    keys, _, _, per_key = placed_lse.shape
    heads = features // HD
    block = min(8, rows)
    ids = ids_ref[...]
    sample_at = lax.broadcasted_iota(jnp.int32, (samples, ids.shape[1]), 0)
    picked = (sample_at == ids).astype(jnp.float32).T[:rows]
    lengths = jnp.sum(picked * lengths_ref[...].astype(jnp.float32), axis=1, keepdims=True)
    lengths = lengths.astype(jnp.int32)
    spot = ids // sub % subsets * part_samples + ids // (sub * subsets) * sub + ids % sub
    chosen = (sample_at == jnp.where(ids < 0, -1, spot)).astype(jnp.float32)
    picked = chosen.T[:rows].astype(jnp.bfloat16)
    all_q = q_ref[...].reshape(samples, features)
    for j in range(keys):
        lanes = slice(j * per_key * HD, (j + 1) * per_key * HD)
        own = jnp.dot(picked, all_q[:, lanes], preferred_element_type=jnp.float32)
        for g in range(per_key):
            row_q[pl.ds(j * per_key + g, rows, stride=heads), :] = own[:, g * HD : (g + 1) * HD]

    same = (
        lax.broadcasted_iota(jnp.int32, (heads, width), 0) // per_key
        == lax.broadcasted_iota(jnp.int32, (heads, width), 1) // HD
    )
    positions = lax.broadcasted_iota(jnp.int32, (heads, positions_here), 1)
    lanes_at = lax.broadcasted_iota(jnp.int32, (heads, ids.shape[1]), 1)
    table = jnp.zeros((heads, ids.shape[1]), jnp.float32)
    scores = []
    for r0 in range(0, rows, block):
        block_copy(r0 // block).wait()
        for r in range(r0, r0 + block):
            q = row_q[r * heads : (r + 1) * heads]
            spread = jnp.concatenate([q] * keys, axis=1)
            spread = jnp.where(same, spread, 0.0).astype(jnp.bfloat16)
            one = lax.dot_general(
                spread, cache[0, r], (((1,), (1,)), ((), ())), preferred_element_type=jnp.float32
            )
            live = positions < lengths[r : r + 1]
            scores.append(jnp.where(live, one * HD ** (-0.5), -jnp.inf))
    for r0 in range(0, rows, block):
        group = jnp.concatenate(scores[r0 : r0 + block], axis=0)
        high = jnp.max(group, axis=1, keepdims=True)
        weights = jnp.exp(group - high)
        total = jnp.sum(weights, axis=1, keepdims=True)
        lse = high + jnp.log(total)
        weights = weights.astype(jnp.bfloat16)
        for r in range(r0, r0 + block):
            part = slice((r - r0) * heads, (r - r0 + 1) * heads)
            summed = jnp.dot(weights[part], cache[1, r], preferred_element_type=jnp.float32)
            own = jnp.concatenate(
                [
                    summed[j * per_key : (j + 1) * per_key, j * HD : (j + 1) * HD]
                    for j in range(keys)
                ],
                axis=0,
            )
            piece = (own / total[part]).astype(jnp.bfloat16)
            row_out[r * heads : (r + 1) * heads] = piece.astype(jnp.float32)
            table = jnp.where(lanes_at == r, lse[part], table)

    found = jnp.sum(chosen, axis=1, keepdims=True) > 0.0
    for k in range(heads):
        row_piece[:, k * HD : (k + 1) * HD] = row_out[pl.ds(k, rows, stride=heads), :].astype(
            jnp.bfloat16
        )
    to_sample = chosen[:, :rows].astype(jnp.bfloat16)
    for j in range(keys):
        lanes = slice(j * per_key * HD, (j + 1) * per_key * HD)
        one = jnp.dot(to_sample, row_piece[:, lanes], preferred_element_type=jnp.float32)
        placed[:, :, lanes] = one.astype(jnp.bfloat16).reshape(subsets, part_samples, -1)
        one = lax.dot_general(
            chosen,
            table[j * per_key : (j + 1) * per_key],
            (((1,), (1,)), ((), ())),
            precision=lax.Precision.HIGHEST,
            preferred_element_type=jnp.float32,
        )
        one = jnp.where(found, one, -1e30)
        placed_lse[j] = one.reshape(subsets, part_samples, per_key)


def layer_kernel(n, n_smp, names, *refs):
    r = types.SimpleNamespace(**dict(zip(names, refs, strict=True)))
    c, s, h = lax.axis_index("ctx"), lax.axis_index("smp"), lax.axis_index("head")
    kv_ref, state = r.kv, r.state
    out_mine, lse_mine, out_in, lse_in = r.out_mine, r.lse_mine, r.out_in, r.lse_in
    keys, _, samples, per_key = r.placed_lse.shape
    per_dest = out_mine.shape[3] // HD
    dests = per_key // per_dest
    together = max(1, min(per_key, 512 // samples))
    stat_lanes = lse_mine.shape[3]
    slots, width, _ = r.gate_buf.shape
    tiles, units, tile = r.down_buf.shape
    subsets, sub_rows, _ = r.scaled.shape
    sub = state.shape[2] // subsets
    smp_rows = sub_rows // n_smp
    steps = units // UNITS
    all_steps, all_tiles = subsets * steps, subsets * tiles
    ratio = max(1, steps // tiles)
    w_rows = r.w_hbm.shape[0]
    per_slot = units // w_rows
    w_slots = -(-tiles // per_slot)
    block = min(8, r.cache.shape[1])

    def block_copy(i):
        rows_at = pl.ds(i * block, block)
        return pltpu.make_async_copy(
            r.cache_hbm.at[:, rows_at], r.cache.at[:, rows_at], r.cache_sem.at[i]
        )

    def w_block(t):
        first_row = pl.multiple_of(lax.rem(t, per_slot) * w_rows, w_rows)
        return r.down_buf.at[lax.div(t, per_slot), pl.ds(first_row, w_rows)]

    def w_copy(t):
        return pltpu.make_async_copy(r.w_hbm.at[:, columns(t, tile)], w_block(t), r.w_sem.at[t])

    def weight_copies(i):
        slot, t = lax.rem(i, slots), lax.rem(i, steps)
        return (
            pltpu.make_async_copy(
                r.gate_hbm.at[:, columns(t, UNITS)], r.gate_buf.at[slot], r.g_sem.at[slot]
            ),
            pltpu.make_async_copy(
                r.up_hbm.at[:, columns(t, UNITS)], r.up_buf.at[slot], r.u_sem.at[slot]
            ),
        )

    def down_copy(t):
        return pltpu.make_async_copy(
            r.down_hbm.at[:, columns(t, tile)], r.down_buf.at[t], r.d_sem.at[t]
        )

    for i in range(r.cache.shape[1] // block):
        block_copy(i).start()
    kv_copy = pltpu.make_async_copy(r.kv_hbm, kv_ref, r.kv_sem)
    kv_copy.start()
    announce(n, n_smp, c, s, h)

    by_owner = r.q[...].reshape(samples // sub, subsets, sub, r.q.shape[1])
    for k in range(subsets):
        r.q_rows[k] = by_owner[:, k].reshape(samples, r.q.shape[1])

    suffix_pieces(
        r.ids,
        r.lengths,
        sub,
        r.q_rows,
        block_copy,
        r.cache,
        r.row_q,
        r.row_out,
        r.row_piece,
        r.placed,
        r.placed_lse,
    )
    kv_copy.wait()

    @pl.loop(0, tiles)
    def _(t):
        w_copy(t).start()

    @pl.loop(0, min(slots, all_steps))
    def _(t):
        for copy in weight_copies(t):
            copy.start()

    for t in range(w_slots, tiles):
        down_copy(t).start()
    gather_round(n, n_smp)

    lanes_at = lax.broadcasted_iota(jnp.int32, (samples, 128), 1)

    def piece_copies(k, at, d):
        return (
            remote(
                out_mine.at[k, d], out_in.at[k, at], r.os.at[k, d], r.orr.at[k, at], {"ctx": d}
            ),
            remote(
                lse_mine.at[k, d], lse_in.at[k, at], r.ls.at[k, d], r.lr.at[k, at], {"ctx": d}
            ),
        )

    def prefix_piece(k, i):
        j = lax.rem(lax.div(c, dests) + 1 + i, keys)
        key = kv_ref[0, :, columns(j, HD)]
        value = kv_ref[1, :, columns(j, HD)]
        own = r.q_rows[k, :, columns(j, per_key * HD)]
        placed = r.placed[k, :, columns(j, per_key * HD)]
        placed_lse = r.placed_lse[j, k]
        tables = [jnp.zeros((samples, 128), jnp.float32) for _ in range(dests)]
        for g0 in range(0, per_key, together):
            rows = jnp.concatenate(
                [own[:, g * HD : (g + 1) * HD] for g in range(g0, g0 + together)], axis=0
            )
            scores = lax.dot_general(
                rows, key, (((1,), (1,)), ((), ())), preferred_element_type=jnp.float32
            ) * HD ** (-0.5)
            high = jnp.max(scores, axis=1, keepdims=True)
            weights = jnp.exp(scores - high)
            total = jnp.sum(weights, axis=1, keepdims=True)
            summed = (
                jnp.dot(weights.astype(jnp.bfloat16), value, preferred_element_type=jnp.float32)
                / total
            )
            lse = high + jnp.log(total)
            for g in range(g0, g0 + together):
                part = slice((g - g0) * samples, (g - g0 + 1) * samples)
                own_lse, other_lse = lse[part], placed_lse[:, g : g + 1]
                top = jnp.maximum(own_lse, other_lse)
                own_weight = jnp.exp(own_lse - top)
                other_weight = jnp.exp(other_lse - top)
                both = own_weight + other_weight
                merged = (
                    own_weight * summed[part]
                    + other_weight * placed[:, g * HD : (g + 1) * HD].astype(jnp.float32)
                ) / both
                at = g % per_dest
                out_mine[k, j * dests + g // per_dest, :, at * HD : (at + 1) * HD] = merged.astype(
                    jnp.bfloat16
                )
                q = g // per_dest
                tables[q] = jnp.where(lanes_at == at, top + jnp.log(both), tables[q])
        for q in range(dests):
            d = j * dests + q
            table = tables[q]
            if stat_lanes > samples:
                rest_of = jnp.zeros((stat_lanes - samples, 128), jnp.float32)
                table = jnp.concatenate([table, rest_of], axis=0)
            lse_mine[k, d] = table.T[:8]

            @pl.when(d != c)
            def _():
                for copy in piece_copies(k, c, d):
                    copy.start()

    def attn_copy(k, m):
        at = r.attn_rows.at[k, pl.ds(pl.multiple_of(s * samples, samples), samples)]
        return remote(
            at, at, r.xs.at[k, m - 1], r.xr.at[k, m - 1], {"smp": lax.rem(s + m, n_smp)}
        )

    def merge_pieces(k):
        for m in range(1, n):
            d = lax.rem(c + m, n)
            for copy in piece_copies(k, d, d):
                copy.wait_recv()
        lses = [lse_mine[k, c]] + [lse_in[k, lax.rem(c + m, n)] for m in range(1, n)]
        peak = functools.reduce(jnp.maximum, lses)
        scales = [jnp.exp(value - peak) for value in lses]
        denom = functools.reduce(jnp.add, scales)
        blank = jnp.zeros((120, stat_lanes), jnp.float32)
        scales = [
            jnp.concatenate([value / denom, blank], axis=0).T[:samples] for value in scales
        ]
        for j in range(per_dest):
            lanes = slice(j * HD, (j + 1) * HD)
            total = scales[0][:, j : j + 1] * out_mine[k, c, :, lanes].astype(jnp.float32)
            for m in range(1, n):
                piece = out_in[k, lax.rem(c + m, n), :, lanes].astype(jnp.float32)
                total = total + scales[m][:, j : j + 1] * piece
            at = pl.ds(pl.multiple_of(s * samples, samples), samples)
            r.attn_rows[k, at, lanes] = total.astype(jnp.bfloat16)
        for m in range(1, n_smp):
            attn_copy(k, m).start()

    def finish_attn(k):
        for m in range(1, n_smp):
            attn_copy(k, m).wait()
        for m in range(1, n):
            d = lax.rem(c + m, n)
            for copy in piece_copies(k, c, d):
                copy.wait_send()

    @pl.loop(0, keys)
    def _(i):
        prefix_piece(0, i)

    early = keys // 2 if subsets > 1 else 0
    gap = max(0, steps - tiles) // 4 if subsets > 1 else 0
    period = tiles + gap
    if subsets > 1:

        @pl.loop(0, early)
        def _(i):
            prefix_piece(1, i)

    merge_pieces(0)
    if subsets > 1:

        @pl.loop(early, keys)
        def _(i):
            prefix_piece(1, i)

    finish_attn(0)

    line = Line(
        n,
        c,
        h,
        r.buf_a,
        r.recv_a,
        r.buf_b,
        r.from_left,
        r.from_right,
        r.sa,
        r.ra,
        r.ss,
        r.rl,
        r.rr,
    )

    def rows_of(k):
        return pl.ds(pl.multiple_of(k * sub, sub), sub)

    def gather_copy(j, q, way, sems):
        k, t = lax.div(j, tiles), lax.rem(j, tiles)
        at = state.at[q, h, rows_of(k), columns(t, tile)]
        return remote(at, at, sems.at[j, q], r.gr.at[j, q], {"ctx": lax.rem(c + way, n)})

    def pass_copy(j, q):
        k, t = lax.div(j, tiles), lax.rem(j, tiles)
        at = state.at[q, h, rows_of(k), columns(t, tile)]
        return remote(at, at, r.fs.at[j, q], r.fr.at[j, q], {"head": 1 - h})

    def spread(j, q, right, left):
        @pl.when(right & (c < n - 1))
        def _():
            gather_copy(j, q, 1, r.gsr).start()

        @pl.when(left & (c > 0))
        def _():
            gather_copy(j, q, n - 1, r.gsl).start()

        pass_copy(j, q).start()

    def state_tile(i):
        at = lax.max(i, 0)
        k, t = lax.div(at, period), lax.rem(at, period)
        return (i >= 0) & (k < subsets) & (t < tiles), k * tiles + t

    def mixed_tile(i):
        return (i >= 0) & (i < all_tiles), i

    def project(i):
        live, j = state_tile(i)

        @pl.when(live)
        def _():
            k, t = lax.div(j, tiles), lax.rem(j, tiles)

            @pl.when(k == 0)
            def _():
                w_copy(t).wait()

            line.give(
                j, jnp.dot(r.attn_rows[k], w_block(t)[...], preferred_element_type=jnp.float32)
            )

        line.step(i, state_tile)
        ready, done = state_tile(i - n)

        @pl.when(ready)
        def _():
            j = done
            k, t = lax.div(j, tiles), lax.rem(j, tiles)
            own = line.finish(j) + r.res[rows_of(k), columns(t, tile)].astype(jnp.float32)
            state[c, h, rows_of(k), columns(t, tile)] = own.astype(jnp.bfloat16)
            spread(j, c, c >= 0, c >= 0)

        for q in range(n):
            here, moved = state_tile(i - n - lax.max(c - q, q - c))

            @pl.when((q != c) & here)
            def _():
                gather_copy(moved, q, 1, r.gsr).wait_recv()
                spread(moved, q, q < c, q > c)

    def smp_rows_of(p):
        return pl.ds(pl.multiple_of(p * smp_rows, smp_rows), smp_rows)

    def square_copy(k, m):
        p = lax.rem(s + m, n_smp)
        return remote(
            r.squares.at[k, smp_rows_of(p)],
            r.squares_in.at[k, m - 1],
            r.qs.at[k, m - 1],
            r.qr.at[k, m - 1],
            {"smp": p},
        )

    def prepare(k):
        @pl.loop(k * tiles, (k + 1) * tiles)
        def _(j):
            for q in range(n):
                pass_copy(j, q).wait()

        for owner in range(n):
            for core in range(2):
                wide = state[owner, core, rows_of(k)].astype(jnp.float32)
                first_row = (2 * owner + core) * sub
                rows = slice(first_row, first_row + sub)
                r.scaled[k, rows] = (wide * r.gain[...]).astype(jnp.bfloat16)
                sums = jnp.sum(wide * wide, axis=1, keepdims=True)
                r.squares[k, rows] = jnp.broadcast_to(sums, (sub, 128))
        for m in range(1, n_smp):
            square_copy(k, m).start()

    def part_copy(i, m):
        p = lax.rem(s + m, n_smp)
        return remote(
            r.part.at[i, smp_rows_of(p)],
            r.part_in.at[i, m - 1],
            r.ps.at[i, m - 1],
            r.pr.at[i, m - 1],
            {"smp": p},
        )

    def hidden_copy(i, m):
        k, t = lax.div(i, steps), lax.rem(i, steps)
        at = r.hidden.at[k, smp_rows_of(s), columns(t, UNITS)]
        return remote(
            at, at, r.hs.at[i, m - 1], r.hr.at[i, m - 1], {"smp": lax.rem(s + m, n_smp)}
        )

    def act(i):
        k, t = lax.div(i, steps), lax.rem(i, steps)

        @pl.when(t == 0)
        def _():
            for m in range(1, n_smp):
                square_copy(k, m).wait()

        both = r.part[i, smp_rows_of(s)].astype(jnp.float32)
        for m in range(1, n_smp):
            part_copy(i, m).wait()
            both = both + r.part_in[i, m - 1].astype(jnp.float32)
        total = r.squares[k, smp_rows_of(s)]
        for m in range(1, n_smp):
            total = total + r.squares_in[k, m - 1]
        factor = lax.rsqrt(total / (width * n_smp) + EPSILON)[:, :1]
        gate = factor * both[:, :UNITS]
        up = factor * both[:, UNITS:]
        value = gate / (1.0 + jnp.exp(-gate)) * up
        r.hidden[k, smp_rows_of(s), columns(t, UNITS)] = value.astype(jnp.bfloat16)
        for m in range(1, n_smp):
            hidden_copy(i, m).start()

    def gate_up(i):
        k, t = lax.div(i, steps), lax.rem(i, steps)

        @pl.when(t == 0)
        def _():
            prepare(k)

        for copy in weight_copies(i):
            copy.wait()
        slot = lax.rem(i, slots)
        r.part[i, :, :UNITS] = jnp.dot(
            r.scaled[k], r.gate_buf[slot], preferred_element_type=jnp.float32
        ).astype(jnp.bfloat16)
        r.part[i, :, UNITS:] = jnp.dot(
            r.scaled[k], r.up_buf[slot], preferred_element_type=jnp.float32
        ).astype(jnp.bfloat16)
        for m in range(1, n_smp):
            part_copy(i, m).start()

        @pl.when(i + slots < all_steps)
        def _():
            for copy in weight_copies(i + slots):
                copy.start()

    def down(j):
        k, t = lax.div(j, tiles), lax.rem(j, tiles)

        @pl.when(t == 0)
        def _():
            @pl.loop(0, steps)
            def _(u):
                for m in range(1, n_smp):
                    hidden_copy(k * steps + u, m).wait()

        @pl.when(k == 0)
        def _():
            down_copy(t).wait()

        line.drain(j)
        line.give(j, jnp.dot(r.hidden[k], r.down_buf[t], preferred_element_type=jnp.float32))

    def emit(j):
        k, t = lax.div(j, tiles), lax.rem(j, tiles)
        value = line.finish(j) + state[c, h, rows_of(k), columns(t, tile)].astype(jnp.float32)
        r.mixed[rows_of(k), columns(t, tile)] = value.astype(jnp.bfloat16)

    ahead = tiles + 2 * n - 1
    rest = period * (subsets - 1)
    free_at = max(0, period * (subsets - 1) + tiles - ahead)
    merge_at = max(0, period - 2)

    @pl.loop(0, ahead)
    def _(i):
        if subsets > 1:

            @pl.when(i == period)
            def _():
                finish_attn(1)

        project(i)
        if subsets > 1:

            @pl.when(i == merge_at)
            def _():
                merge_pieces(1)

    lag = min(2, all_steps)
    first = max(steps + lag + 1, rest)

    @pl.loop(0, first + (all_tiles + n) * ratio)
    def _(i):
        @pl.when(i < all_steps)
        def _():
            gate_up(i)

        @pl.when(i < rest)
        def _():
            project(i + ahead)

        @pl.when(i == free_at)
        def _():
            for t in range(w_slots):
                down_copy(t).start()

        @pl.when((i >= lag) & (i < all_steps + lag))
        def _():
            act(i - lag)

        j = lax.div(i - first, ratio)

        @pl.when((i >= first) & (lax.rem(i - first, ratio) == 0))
        def _():
            @pl.when(j < all_tiles)
            def _():
                down(j)

            line.step(j, mixed_tile)

            @pl.when(j >= n)
            def _():
                emit(j - n)

    @pl.loop(0, all_tiles)
    def _(j):
        line.drain(j)
        for q in range(n):

            @pl.when((q <= c) & (c < n - 1))
            def _():
                gather_copy(j, q, 1, r.gsr).wait_send()

            @pl.when((q >= c) & (c > 0))
            def _():
                gather_copy(j, q, n - 1, r.gsl).wait_send()


def layer(
    n, n_smp, ids, lengths, queries, prefix_cache, suffix_cache, w, residual, gain, gate, up, down
):
    samples, heads = queries.shape[0], queries.shape[1] // HD
    keys = prefix_cache.shape[2] // HD
    suffix_rows = suffix_cache.shape[1]
    features = queries.shape[1] // n
    rows, width = residual.shape
    sub = SUB if rows % SUB == 0 else rows
    subsets = rows // sub
    part_samples = samples // subsets
    stat_lanes = -(-part_samples // 128) * 128
    sub_rows = n * 2 * sub
    smp_rows = sub_rows // n_smp
    units = gate.shape[1]
    steps = units // UNITS
    tile = max(TILE, width // steps)
    tiles = width // tile
    all_steps, all_tiles = subsets * steps, subsets * tiles
    slots = min(SLOTS, all_steps)
    vmem = pl.BlockSpec(memory_space=pltpu.VMEM)
    hbm = pl.BlockSpec(memory_space=pl.ANY)
    dma = pltpu.SemaphoreType.DMA
    bf16, f32 = jnp.bfloat16, jnp.float32
    scratch = {
        "kv": pltpu.VMEM(prefix_cache.shape, bf16),
        "cache": pltpu.VMEM(suffix_cache.shape, bf16),
        "row_q": pltpu.VMEM((suffix_rows * heads, HD), f32),
        "row_out": pltpu.VMEM((suffix_rows * heads, HD), f32),
        "row_piece": pltpu.VMEM((suffix_rows, heads * HD), bf16),
        "q_rows": pltpu.VMEM((subsets, part_samples, heads * HD), bf16),
        "placed": pltpu.VMEM((subsets, part_samples, heads * HD), bf16),
        "placed_lse": pltpu.VMEM((keys, subsets, part_samples, heads // keys), f32),
        "out_mine": pltpu.VMEM((subsets, n, part_samples, features), bf16),
        "lse_mine": pltpu.VMEM((subsets, n, 8, stat_lanes), f32),
        "out_in": pltpu.VMEM((subsets, n, part_samples, features), bf16),
        "lse_in": pltpu.VMEM((subsets, n, 8, stat_lanes), f32),
        "attn_rows": pltpu.VMEM((subsets, sub_rows, features), bf16),
        "state": pltpu.VMEM((n, 2, rows, width), bf16),
        "scaled": pltpu.VMEM((subsets, sub_rows, width), bf16),
        "squares": pltpu.VMEM((subsets, sub_rows, 128), f32),
        "squares_in": pltpu.VMEM((subsets, n_smp - 1, smp_rows, 128), f32),
        "gate_buf": pltpu.VMEM((slots, width, UNITS), bf16),
        "up_buf": pltpu.VMEM((slots, width, UNITS), bf16),
        "down_buf": pltpu.VMEM((tiles, units, tile), bf16),
        "part": pltpu.VMEM((all_steps, sub_rows, 2 * UNITS), bf16),
        "part_in": pltpu.VMEM((all_steps, n_smp - 1, smp_rows, 2 * UNITS), bf16),
        "hidden": pltpu.VMEM((subsets, sub_rows, units), bf16),
        "buf_a": pltpu.VMEM((all_tiles, 2, n, sub, tile), bf16),
        "recv_a": pltpu.VMEM((all_tiles, n, sub, tile), bf16),
        "buf_b": pltpu.VMEM((all_tiles, n, sub, tile), bf16),
        "from_left": pltpu.VMEM((all_tiles, n, sub, tile), bf16),
        "from_right": pltpu.VMEM((all_tiles, n, sub, tile), bf16),
        "kv_sem": dma,
        "cache_sem": dma((suffix_rows // min(8, suffix_rows),)),
        "w_sem": dma((tiles,)),
        "g_sem": dma((slots,)),
        "u_sem": dma((slots,)),
        "d_sem": dma((tiles,)),
    }
    scratch |= {name: dma((subsets, n)) for name in ("os", "orr", "ls", "lr")}
    scratch |= {name: dma((subsets, n_smp - 1)) for name in ("xs", "xr", "qs", "qr")}
    scratch |= {name: dma((all_steps, n_smp - 1)) for name in ("ps", "pr", "hs", "hr")}
    scratch |= {name: dma((all_tiles,)) for name in ("sa", "ra")}
    scratch |= {
        name: dma((all_tiles, n)) for name in ("ss", "rl", "rr", "gsr", "gsl", "gr", "fs", "fr")
    }
    operands = {
        "ids": (ids, vmem),
        "lengths": (lengths, vmem),
        "q": (queries, vmem),
        "kv_hbm": (prefix_cache, hbm),
        "cache_hbm": (suffix_cache, hbm),
        "w_hbm": (w, hbm),
        "res": (residual, vmem),
        "gain": (gain, vmem),
        "gate_hbm": (gate, hbm),
        "up_hbm": (up, hbm),
        "down_hbm": (down, hbm),
    }
    names = (*operands, "mixed", *scratch)
    return pl.pallas_call(
        functools.partial(layer_kernel, n, n_smp, names),
        out_shape=jax.ShapeDtypeStruct((rows, width), bf16),
        in_specs=[spec for _, spec in operands.values()],
        out_specs=vmem,
        scratch_shapes=list(scratch.values()),
        compiler_params=pltpu.CompilerParams(
            collective_id=0, has_side_effects=True, vmem_limit_bytes=VMEM_BYTES
        ),
    )(*[value for value, _ in operands.values()])


def on_device(
    queries,
    prefix_cache,
    suffix_cache,
    suffix_length,
    cache_sample,
    residual,
    w_out,
    norm_gain,
    gate_matrix,
    w_up,
    w_down,
):
    group_rows = queries.shape[0]
    n, n_smp = lax.axis_size("ctx"), lax.axis_size("smp")
    rows_here = suffix_cache.shape[1]
    flat_index = lax.axis_index("ctx") * n_smp + lax.axis_index("smp")
    row_ids = lax.dynamic_slice_in_dim(cache_sample, flat_index * rows_here, rows_here, 0)
    local_ids = row_ids - lax.axis_index("smp") * group_rows
    local_ids = jnp.pad(local_ids, (0, 128 - rows_here), constant_values=-1)
    return layer(
        n,
        n_smp,
        local_ids[None, :],
        suffix_length[None, :],
        queries[:, 0],
        prefix_cache[:, :, 0],
        suffix_cache[:, :, :, 0],
        w_out[0],
        residual,
        norm_gain[None, :],
        gate_matrix,
        w_up,
        w_down,
    )


def solution(mesh):
    in_specs = (
        P(("group", "smp"), "head", None),
        P(None, ("group", "ctx"), "head", None),
        P(None, ("group", "ctx", "smp"), None, "head", None),
        P(("group", "smp")),
        P("group"),
        P(("group", "ctx", "head"), "smp"),
        P("head", "ctx", "smp"),
        P("smp"),
        P("smp", ("ctx", "head")),
        P("smp", ("ctx", "head")),
        P(("ctx", "head"), "smp"),
    )
    out_specs = P(("group", "ctx", "head"), "smp")
    return jax.shard_map(
        on_device, mesh=mesh, in_specs=in_specs, out_specs=out_specs, check_vma=False
    )
```

```python
import functools
import types

import jax
import jax.numpy as jnp
from jax import lax
from jax.experimental import pallas as pl
from jax.experimental.pallas import tpu as pltpu
from jax.sharding import PartitionSpec as P

D = 8192
QUERY_HEADS = 64
KEY_VALUE_HEADS = 8
HD = 128


EPSILON = 1e-05


MESH = pl.DeviceIdType.MESH
TILE = 1024
UNITS = 256
SLOTS = 3
SUB = 16
VMEM_BYTES = 67043328


def remote(src, dst, send_sem, recv_sem, where):
    return pltpu.make_async_remote_copy(
        src_ref=src,
        dst_ref=dst,
        send_sem=send_sem,
        recv_sem=recv_sem,
        device_id=where,
        device_id_type=MESH,
    )


def announce(n, n_smp, c, s, h):
    barrier = pltpu.get_barrier_semaphore()
    for k in range(1, n):
        pl.semaphore_signal(barrier, inc=1, device_id={"ctx": lax.rem(c + k, n)}, device_id_type=MESH)
    for k in range(1, n_smp):
        pl.semaphore_signal(
            barrier, inc=1, device_id={"smp": lax.rem(s + k, n_smp)}, device_id_type=MESH
        )
    pl.semaphore_signal(barrier, inc=1, device_id={"head": 1 - h}, device_id_type=MESH)


def gather_round(n, n_smp):
    pl.semaphore_wait(pltpu.get_barrier_semaphore(), (n - 1) + (n_smp - 1) + 1)


class Line:
    def __init__(self, n, c, h, buf_a, recv_a, buf_b, from_left, from_right, sa, ra, ss, rl, rr):
        self.n, self.c, self.h = n, c, h
        self.buf_a, self.recv_a, self.buf_b = buf_a, recv_a, buf_b
        self.from_left, self.from_right = from_left, from_right
        self.sa, self.ra, self.ss, self.rl, self.rr = sa, ra, ss, rl, rr
        self.tiles = buf_a.shape[0]

        @pl.when(c == 0)
        def _():
            from_left[:, 0] = jnp.zeros(from_left.shape[:1] + from_left.shape[2:], from_left.dtype)

        @pl.when(c == n - 1)
        def _():
            from_right[:, n - 1] = jnp.zeros(
                from_right.shape[:1] + from_right.shape[2:], from_right.dtype
            )

    def pair_copy(self, t):
        return remote(
            self.buf_a.at[t, 1 - self.h],
            self.recv_a.at[t],
            self.sa.at[t],
            self.ra.at[t],
            {"head": 1 - self.h},
        )

    def to_right(self, t, d):
        return remote(
            self.buf_b.at[t, d],
            self.from_left.at[t, d],
            self.ss.at[t, d],
            self.rl.at[t, d],
            {"ctx": lax.rem(self.c + 1, self.n)},
        )

    def to_left(self, t, d):
        return remote(
            self.buf_b.at[t, d],
            self.from_right.at[t, d],
            self.ss.at[t, d],
            self.rr.at[t, d],
            {"ctx": lax.rem(self.c + self.n - 1, self.n)},
        )

    def give(self, t, value):
        _, _, n, rows, width = self.buf_a.shape
        parts = value.reshape(n, 2, rows, width).astype(jnp.bfloat16)
        self.buf_a[t, 0] = parts[:, 0]
        self.buf_a[t, 1] = parts[:, 1]
        self.pair_copy(t).start()

    def middle(self, t):
        self.pair_copy(t).wait()
        both = self.buf_a[t, self.h].astype(jnp.float32) + self.recv_a[t].astype(jnp.float32)
        self.buf_b[t] = both.astype(jnp.bfloat16)

    def hop(self, t, inside, d, copy_of, arrived, first):
        @pl.when(inside)
        def _():
            @pl.when(jnp.logical_not(first))
            def _():
                copy_of(t, d).wait_recv()
                both = self.buf_b[t, d].astype(jnp.float32) + arrived[t, d].astype(jnp.float32)
                self.buf_b[t, d] = both.astype(jnp.bfloat16)

            copy_of(t, d).start()

    def step(self, i, tile_at):
        n, c = self.n, self.c
        live, t = tile_at(i - 1)

        @pl.when(live)
        def _():
            self.middle(t)

        live_r, t_r = tile_at(i - 1 - c)
        live_l, t_l = tile_at(i - n + c)
        for e in range(n - 1):
            right, left = n - 1 - e, e
            self.hop(t_r, live_r & (right > c), right, self.to_right, self.from_left, c == 0)
            self.hop(t_l, live_l & (left < c), left, self.to_left, self.from_right, c == n - 1)

    def finish(self, t):
        n, c = self.n, self.c

        @pl.when(c > 0)
        def _():
            self.to_right(t, c).wait_recv()

        @pl.when(c < n - 1)
        def _():
            self.to_left(t, c).wait_recv()

        return (
            self.buf_b[t, c].astype(jnp.float32)
            + self.from_left[t, c].astype(jnp.float32)
            + self.from_right[t, c].astype(jnp.float32)
        )

    def drain(self, t):
        for d in range(self.n):

            @pl.when(d > self.c)
            def _():
                self.to_right(t, d).wait_send()

            @pl.when(d < self.c)
            def _():
                self.to_left(t, d).wait_send()


def columns(t, width):
    return pl.ds(pl.multiple_of(t * width, width), width)


def suffix_pieces(
    ids_ref, lengths_ref, sub, q_ref, block_copy, cache, row_q, row_out, row_piece, placed, placed_lse
):
    _, rows, positions_here, width = cache.shape
    subsets, part_samples, features = q_ref.shape
    samples = subsets * part_samples
    keys, _, _, per_key = placed_lse.shape
    heads = features // HD
    block = min(8, rows)
    all_ids = ids_ref[...]
    group_rows = all_ids.shape[1]
    n_smp = lax.axis_size("smp")
    own_first = (lax.axis_index("ctx") * n_smp + lax.axis_index("smp")) * rows
    turned = pltpu.roll(all_ids, lax.rem(group_rows - own_first, group_rows), 1)
    ids = turned[:, :128] - lax.axis_index("smp") * samples
    ids = jnp.where(lax.broadcasted_iota(jnp.int32, ids.shape, 1) < rows, ids, -1)
    sample_at = lax.broadcasted_iota(jnp.int32, (samples, ids.shape[1]), 0)
    picked = (sample_at == ids).astype(jnp.float32).T[:rows]
    lengths = jnp.sum(picked * lengths_ref[...].astype(jnp.float32), axis=1, keepdims=True)
    lengths = lengths.astype(jnp.int32)
    spot = ids // sub % subsets * part_samples + ids // (sub * subsets) * sub + ids % sub
    chosen = (sample_at == jnp.where(ids < 0, -1, spot)).astype(jnp.float32)
    picked = chosen.T[:rows].astype(jnp.bfloat16)
    all_q = q_ref[...].reshape(samples, features)
    for j in range(keys):
        lanes = slice(j * per_key * HD, (j + 1) * per_key * HD)
        own = jnp.dot(picked, all_q[:, lanes], preferred_element_type=jnp.float32)
        for g in range(per_key):
            row_q[pl.ds(j * per_key + g, rows, stride=heads), :] = own[:, g * HD : (g + 1) * HD]

    same = (
        lax.broadcasted_iota(jnp.int32, (heads, width), 0) // per_key
        == lax.broadcasted_iota(jnp.int32, (heads, width), 1) // HD
    )
    positions = lax.broadcasted_iota(jnp.int32, (heads, positions_here), 1)
    lanes_at = lax.broadcasted_iota(jnp.int32, (heads, ids.shape[1]), 1)
    table = jnp.zeros((heads, ids.shape[1]), jnp.float32)
    scores = []
    for r0 in range(0, rows, block):
        block_copy(r0 // block).wait()
        for r in range(r0, r0 + block):
            q = row_q[r * heads : (r + 1) * heads]
            spread = jnp.concatenate([q] * keys, axis=1)
            spread = jnp.where(same, spread, 0.0).astype(jnp.bfloat16)
            one = lax.dot_general(
                spread, cache[0, r], (((1,), (1,)), ((), ())), preferred_element_type=jnp.float32
            )
            live = positions < lengths[r : r + 1]
            scores.append(jnp.where(live, one * HD ** (-0.5), -jnp.inf))
    for r0 in range(0, rows, block):
        group = jnp.concatenate(scores[r0 : r0 + block], axis=0)
        high = jnp.max(group, axis=1, keepdims=True)
        weights = jnp.exp(group - high)
        total = jnp.sum(weights, axis=1, keepdims=True)
        lse = high + jnp.log(total)
        weights = weights.astype(jnp.bfloat16)
        for r in range(r0, r0 + block):
            part = slice((r - r0) * heads, (r - r0 + 1) * heads)
            summed = jnp.dot(weights[part], cache[1, r], preferred_element_type=jnp.float32)
            own = jnp.concatenate(
                [
                    summed[j * per_key : (j + 1) * per_key, j * HD : (j + 1) * HD]
                    for j in range(keys)
                ],
                axis=0,
            )
            piece = (own / total[part]).astype(jnp.bfloat16)
            row_out[r * heads : (r + 1) * heads] = piece.astype(jnp.float32)
            table = jnp.where(lanes_at == r, lse[part], table)

    found = jnp.sum(chosen, axis=1, keepdims=True) > 0.0
    for k in range(heads):
        row_piece[:, k * HD : (k + 1) * HD] = row_out[pl.ds(k, rows, stride=heads), :].astype(
            jnp.bfloat16
        )
    to_sample = chosen[:, :rows].astype(jnp.bfloat16)
    for j in range(keys):
        lanes = slice(j * per_key * HD, (j + 1) * per_key * HD)
        one = jnp.dot(to_sample, row_piece[:, lanes], preferred_element_type=jnp.float32)
        placed[:, :, lanes] = one.astype(jnp.bfloat16).reshape(subsets, part_samples, -1)
        one = lax.dot_general(
            chosen,
            table[j * per_key : (j + 1) * per_key],
            (((1,), (1,)), ((), ())),
            precision=lax.Precision.HIGHEST,
            preferred_element_type=jnp.float32,
        )
        one = jnp.where(found, one, -1e30)
        placed_lse[j] = one.reshape(subsets, part_samples, per_key)


def layer_kernel(n, n_smp, names, *refs):
    r = types.SimpleNamespace(**dict(zip(names, refs, strict=True)))
    c, s, h = lax.axis_index("ctx"), lax.axis_index("smp"), lax.axis_index("head")
    kv_ref, state = r.kv, r.state
    out_mine, lse_mine, out_in, lse_in = r.out_mine, r.lse_mine, r.out_in, r.lse_in
    keys, _, samples, per_key = r.placed_lse.shape
    per_dest = out_mine.shape[3] // HD
    dests = per_key // per_dest
    together = max(1, min(per_key, 512 // samples))
    stat_lanes = lse_mine.shape[3]
    slots, width, _ = r.gate_buf.shape
    tiles, units, tile = r.down_buf.shape
    subsets, sub_rows, _ = r.scaled.shape
    sub = state.shape[2] // subsets
    smp_rows = sub_rows // n_smp
    steps = units // UNITS
    all_steps, all_tiles = subsets * steps, subsets * tiles
    ratio = max(1, steps // tiles)
    w_rows = r.w_hbm.shape[0]
    per_slot = units // w_rows
    w_slots = -(-tiles // per_slot)
    block = min(8, r.cache.shape[1])

    def block_copy(i):
        rows_at = pl.ds(i * block, block)
        return pltpu.make_async_copy(
            r.cache_hbm.at[:, rows_at], r.cache.at[:, rows_at], r.cache_sem.at[i]
        )

    def w_block(t):
        first_row = pl.multiple_of(lax.rem(t, per_slot) * w_rows, w_rows)
        return r.down_buf.at[lax.div(t, per_slot), pl.ds(first_row, w_rows)]

    def w_copy(t):
        return pltpu.make_async_copy(r.w_hbm.at[:, columns(t, tile)], w_block(t), r.w_sem.at[t])

    def weight_copies(i):
        slot, t = lax.rem(i, slots), lax.rem(i, steps)
        return (
            pltpu.make_async_copy(
                r.gate_hbm.at[:, columns(t, UNITS)], r.gate_buf.at[slot], r.g_sem.at[slot]
            ),
            pltpu.make_async_copy(
                r.up_hbm.at[:, columns(t, UNITS)], r.up_buf.at[slot], r.u_sem.at[slot]
            ),
        )

    def down_copy(t):
        return pltpu.make_async_copy(
            r.down_hbm.at[:, columns(t, tile)], r.down_buf.at[t], r.d_sem.at[t]
        )

    for i in range(r.cache.shape[1] // block):
        block_copy(i).start()
    kv_copy = pltpu.make_async_copy(r.kv_hbm, kv_ref, r.kv_sem)
    kv_copy.start()
    announce(n, n_smp, c, s, h)

    by_owner = r.q[...].reshape(samples // sub, subsets, sub, r.q.shape[1])
    for k in range(subsets):
        r.q_rows[k] = by_owner[:, k].reshape(samples, r.q.shape[1])

    suffix_pieces(
        r.ids,
        r.lengths,
        sub,
        r.q_rows,
        block_copy,
        r.cache,
        r.row_q,
        r.row_out,
        r.row_piece,
        r.placed,
        r.placed_lse,
    )
    kv_copy.wait()

    @pl.loop(0, tiles)
    def _(t):
        w_copy(t).start()

    @pl.loop(0, min(slots, all_steps))
    def _(t):
        for copy in weight_copies(t):
            copy.start()

    for t in range(w_slots, tiles):
        down_copy(t).start()
    gather_round(n, n_smp)

    lanes_at = lax.broadcasted_iota(jnp.int32, (samples, 128), 1)

    def piece_copies(k, at, d):
        return (
            remote(
                out_mine.at[k, d], out_in.at[k, at], r.os.at[k, d], r.orr.at[k, at], {"ctx": d}
            ),
            remote(
                lse_mine.at[k, d], lse_in.at[k, at], r.ls.at[k, d], r.lr.at[k, at], {"ctx": d}
            ),
        )

    def prefix_piece(k, i):
        j = lax.rem(lax.div(c, dests) + 1 + i, keys)
        key = kv_ref[0, :, columns(j, HD)]
        value = kv_ref[1, :, columns(j, HD)]
        own = r.q_rows[k, :, columns(j, per_key * HD)]
        placed = r.placed[k, :, columns(j, per_key * HD)]
        placed_lse = r.placed_lse[j, k]
        tables = [jnp.zeros((samples, 128), jnp.float32) for _ in range(dests)]
        for g0 in range(0, per_key, together):
            rows = jnp.concatenate(
                [own[:, g * HD : (g + 1) * HD] for g in range(g0, g0 + together)], axis=0
            )
            scores = lax.dot_general(
                rows, key, (((1,), (1,)), ((), ())), preferred_element_type=jnp.float32
            ) * HD ** (-0.5)
            high = jnp.max(scores, axis=1, keepdims=True)
            weights = jnp.exp(scores - high)
            total = jnp.sum(weights, axis=1, keepdims=True)
            summed = (
                jnp.dot(weights.astype(jnp.bfloat16), value, preferred_element_type=jnp.float32)
                / total
            )
            lse = high + jnp.log(total)
            for g in range(g0, g0 + together):
                part = slice((g - g0) * samples, (g - g0 + 1) * samples)
                own_lse, other_lse = lse[part], placed_lse[:, g : g + 1]
                top = jnp.maximum(own_lse, other_lse)
                own_weight = jnp.exp(own_lse - top)
                other_weight = jnp.exp(other_lse - top)
                both = own_weight + other_weight
                merged = (
                    own_weight * summed[part]
                    + other_weight * placed[:, g * HD : (g + 1) * HD].astype(jnp.float32)
                ) / both
                at = g % per_dest
                out_mine[k, j * dests + g // per_dest, :, at * HD : (at + 1) * HD] = merged.astype(
                    jnp.bfloat16
                )
                q = g // per_dest
                tables[q] = jnp.where(lanes_at == at, top + jnp.log(both), tables[q])
        for q in range(dests):
            d = j * dests + q
            table = tables[q]
            if stat_lanes > samples:
                rest_of = jnp.zeros((stat_lanes - samples, 128), jnp.float32)
                table = jnp.concatenate([table, rest_of], axis=0)
            lse_mine[k, d] = table.T[:8]

            @pl.when(d != c)
            def _():
                for copy in piece_copies(k, c, d):
                    copy.start()

    def attn_copy(k, m):
        at = r.attn_rows.at[k, pl.ds(pl.multiple_of(s * samples, samples), samples)]
        return remote(
            at, at, r.xs.at[k, m - 1], r.xr.at[k, m - 1], {"smp": lax.rem(s + m, n_smp)}
        )

    def merge_pieces(k):
        for m in range(1, n):
            d = lax.rem(c + m, n)
            for copy in piece_copies(k, d, d):
                copy.wait_recv()
        lses = [lse_mine[k, c]] + [lse_in[k, lax.rem(c + m, n)] for m in range(1, n)]
        peak = functools.reduce(jnp.maximum, lses)
        scales = [jnp.exp(value - peak) for value in lses]
        denom = functools.reduce(jnp.add, scales)
        blank = jnp.zeros((120, stat_lanes), jnp.float32)
        scales = [
            jnp.concatenate([value / denom, blank], axis=0).T[:samples] for value in scales
        ]
        for j in range(per_dest):
            lanes = slice(j * HD, (j + 1) * HD)
            total = scales[0][:, j : j + 1] * out_mine[k, c, :, lanes].astype(jnp.float32)
            for m in range(1, n):
                piece = out_in[k, lax.rem(c + m, n), :, lanes].astype(jnp.float32)
                total = total + scales[m][:, j : j + 1] * piece
            at = pl.ds(pl.multiple_of(s * samples, samples), samples)
            r.attn_rows[k, at, lanes] = total.astype(jnp.bfloat16)
        for m in range(1, n_smp):
            attn_copy(k, m).start()

    def finish_attn(k):
        for m in range(1, n_smp):
            attn_copy(k, m).wait()
        for m in range(1, n):
            d = lax.rem(c + m, n)
            for copy in piece_copies(k, c, d):
                copy.wait_send()

    @pl.loop(0, keys)
    def _(i):
        prefix_piece(0, i)

    early = keys // 2 if subsets > 1 else 0
    gap = max(0, steps - tiles) // 4 if subsets > 1 else 0
    period = tiles + gap
    if subsets > 1:

        @pl.loop(0, early)
        def _(i):
            prefix_piece(1, i)

    merge_pieces(0)
    if subsets > 1:

        @pl.loop(early, keys)
        def _(i):
            prefix_piece(1, i)

    finish_attn(0)

    line = Line(
        n,
        c,
        h,
        r.buf_a,
        r.recv_a,
        r.buf_b,
        r.from_left,
        r.from_right,
        r.sa,
        r.ra,
        r.ss,
        r.rl,
        r.rr,
    )

    def rows_of(k):
        return pl.ds(pl.multiple_of(k * sub, sub), sub)

    def gather_copy(j, q, way, sems):
        k, t = lax.div(j, tiles), lax.rem(j, tiles)
        at = state.at[q, h, rows_of(k), columns(t, tile)]
        return remote(at, at, sems.at[j, q], r.gr.at[j, q], {"ctx": lax.rem(c + way, n)})

    def pass_copy(j, q):
        k, t = lax.div(j, tiles), lax.rem(j, tiles)
        at = state.at[q, h, rows_of(k), columns(t, tile)]
        return remote(at, at, r.fs.at[j, q], r.fr.at[j, q], {"head": 1 - h})

    def spread(j, q, right, left):
        @pl.when(right & (c < n - 1))
        def _():
            gather_copy(j, q, 1, r.gsr).start()

        @pl.when(left & (c > 0))
        def _():
            gather_copy(j, q, n - 1, r.gsl).start()

        pass_copy(j, q).start()

    def state_tile(i):
        at = lax.max(i, 0)
        k, t = lax.div(at, period), lax.rem(at, period)
        return (i >= 0) & (k < subsets) & (t < tiles), k * tiles + t

    def mixed_tile(i):
        return (i >= 0) & (i < all_tiles), i

    def project(i):
        live, j = state_tile(i)

        @pl.when(live)
        def _():
            k, t = lax.div(j, tiles), lax.rem(j, tiles)

            @pl.when(k == 0)
            def _():
                w_copy(t).wait()

            line.give(
                j, jnp.dot(r.attn_rows[k], w_block(t)[...], preferred_element_type=jnp.float32)
            )

        line.step(i, state_tile)
        ready, done = state_tile(i - n)

        @pl.when(ready)
        def _():
            j = done
            k, t = lax.div(j, tiles), lax.rem(j, tiles)
            own = line.finish(j) + r.res[rows_of(k), columns(t, tile)].astype(jnp.float32)
            state[c, h, rows_of(k), columns(t, tile)] = own.astype(jnp.bfloat16)
            spread(j, c, c >= 0, c >= 0)

        for q in range(n):
            here, moved = state_tile(i - n - lax.max(c - q, q - c))

            @pl.when((q != c) & here)
            def _():
                gather_copy(moved, q, 1, r.gsr).wait_recv()
                spread(moved, q, q < c, q > c)

    def smp_rows_of(p):
        return pl.ds(pl.multiple_of(p * smp_rows, smp_rows), smp_rows)

    def square_copy(k, m):
        p = lax.rem(s + m, n_smp)
        return remote(
            r.squares.at[k, smp_rows_of(p)],
            r.squares_in.at[k, m - 1],
            r.qs.at[k, m - 1],
            r.qr.at[k, m - 1],
            {"smp": p},
        )

    def prepare(k):
        @pl.loop(k * tiles, (k + 1) * tiles)
        def _(j):
            for q in range(n):
                pass_copy(j, q).wait()

        for owner in range(n):
            for core in range(2):
                wide = state[owner, core, rows_of(k)].astype(jnp.float32)
                first_row = (2 * owner + core) * sub
                rows = slice(first_row, first_row + sub)
                r.scaled[k, rows] = (wide * r.gain[...]).astype(jnp.bfloat16)
                sums = jnp.sum(wide * wide, axis=1, keepdims=True)
                r.squares[k, rows] = jnp.broadcast_to(sums, (sub, 128))
        for m in range(1, n_smp):
            square_copy(k, m).start()

    def part_copy(i, m):
        p = lax.rem(s + m, n_smp)
        return remote(
            r.part.at[i, smp_rows_of(p)],
            r.part_in.at[i, m - 1],
            r.ps.at[i, m - 1],
            r.pr.at[i, m - 1],
            {"smp": p},
        )

    def hidden_copy(i, m):
        k, t = lax.div(i, steps), lax.rem(i, steps)
        at = r.hidden.at[k, smp_rows_of(s), columns(t, UNITS)]
        return remote(
            at, at, r.hs.at[i, m - 1], r.hr.at[i, m - 1], {"smp": lax.rem(s + m, n_smp)}
        )

    def act(i):
        k, t = lax.div(i, steps), lax.rem(i, steps)

        @pl.when(t == 0)
        def _():
            for m in range(1, n_smp):
                square_copy(k, m).wait()

        both = r.part[i, smp_rows_of(s)].astype(jnp.float32)
        for m in range(1, n_smp):
            part_copy(i, m).wait()
            both = both + r.part_in[i, m - 1].astype(jnp.float32)
        total = r.squares[k, smp_rows_of(s)]
        for m in range(1, n_smp):
            total = total + r.squares_in[k, m - 1]
        factor = lax.rsqrt(total / (width * n_smp) + EPSILON)[:, :1]
        gate = factor * both[:, :UNITS]
        up = factor * both[:, UNITS:]
        value = gate / (1.0 + jnp.exp(-gate)) * up
        r.hidden[k, smp_rows_of(s), columns(t, UNITS)] = value.astype(jnp.bfloat16)
        for m in range(1, n_smp):
            hidden_copy(i, m).start()

    def gate_up(i):
        k, t = lax.div(i, steps), lax.rem(i, steps)

        @pl.when(t == 0)
        def _():
            prepare(k)

        for copy in weight_copies(i):
            copy.wait()
        slot = lax.rem(i, slots)
        r.part[i, :, :UNITS] = jnp.dot(
            r.scaled[k], r.gate_buf[slot], preferred_element_type=jnp.float32
        ).astype(jnp.bfloat16)
        r.part[i, :, UNITS:] = jnp.dot(
            r.scaled[k], r.up_buf[slot], preferred_element_type=jnp.float32
        ).astype(jnp.bfloat16)
        for m in range(1, n_smp):
            part_copy(i, m).start()

        @pl.when(i + slots < all_steps)
        def _():
            for copy in weight_copies(i + slots):
                copy.start()

    def down(j):
        k, t = lax.div(j, tiles), lax.rem(j, tiles)

        @pl.when(t == 0)
        def _():
            @pl.loop(0, steps)
            def _(u):
                for m in range(1, n_smp):
                    hidden_copy(k * steps + u, m).wait()

        @pl.when(k == 0)
        def _():
            down_copy(t).wait()

        line.drain(j)
        line.give(j, jnp.dot(r.hidden[k], r.down_buf[t], preferred_element_type=jnp.float32))

    def emit(j):
        k, t = lax.div(j, tiles), lax.rem(j, tiles)
        value = line.finish(j) + state[c, h, rows_of(k), columns(t, tile)].astype(jnp.float32)
        r.mixed[rows_of(k), columns(t, tile)] = value.astype(jnp.bfloat16)

    ahead = tiles + 2 * n - 1
    rest = period * (subsets - 1)
    free_at = max(0, period * (subsets - 1) + tiles - ahead)
    merge_at = max(0, period - 2)

    @pl.loop(0, ahead)
    def _(i):
        if subsets > 1:

            @pl.when(i == period)
            def _():
                finish_attn(1)

        project(i)
        if subsets > 1:

            @pl.when(i == merge_at)
            def _():
                merge_pieces(1)

    lag = min(2, all_steps)
    first = max(steps + lag + 1, rest)

    @pl.loop(0, first + (all_tiles + n) * ratio)
    def _(i):
        @pl.when(i < all_steps)
        def _():
            gate_up(i)

        @pl.when(i < rest)
        def _():
            project(i + ahead)

        @pl.when(i == free_at)
        def _():
            for t in range(w_slots):
                down_copy(t).start()

        @pl.when((i >= lag) & (i < all_steps + lag))
        def _():
            act(i - lag)

        j = lax.div(i - first, ratio)

        @pl.when((i >= first) & (lax.rem(i - first, ratio) == 0))
        def _():
            @pl.when(j < all_tiles)
            def _():
                down(j)

            line.step(j, mixed_tile)

            @pl.when(j >= n)
            def _():
                emit(j - n)

    @pl.loop(0, all_tiles)
    def _(j):
        line.drain(j)
        for q in range(n):

            @pl.when((q <= c) & (c < n - 1))
            def _():
                gather_copy(j, q, 1, r.gsr).wait_send()

            @pl.when((q >= c) & (c > 0))
            def _():
                gather_copy(j, q, n - 1, r.gsl).wait_send()


def layer(
    n, n_smp, ids, lengths, queries, prefix_cache, suffix_cache, w, residual, gain, gate, up, down
):
    samples, heads = queries.shape[0], queries.shape[1] // HD
    keys = prefix_cache.shape[2] // HD
    suffix_rows = suffix_cache.shape[1]
    features = queries.shape[1] // n
    rows, width = residual.shape
    sub = SUB if rows % SUB == 0 else rows
    subsets = rows // sub
    part_samples = samples // subsets
    stat_lanes = -(-part_samples // 128) * 128
    sub_rows = n * 2 * sub
    smp_rows = sub_rows // n_smp
    units = gate.shape[1]
    steps = units // UNITS
    tile = max(TILE, width // steps)
    tiles = width // tile
    all_steps, all_tiles = subsets * steps, subsets * tiles
    slots = min(SLOTS, all_steps)
    vmem = pl.BlockSpec(memory_space=pltpu.VMEM)
    hbm = pl.BlockSpec(memory_space=pl.ANY)
    dma = pltpu.SemaphoreType.DMA
    bf16, f32 = jnp.bfloat16, jnp.float32
    scratch = {
        "kv": pltpu.VMEM(prefix_cache.shape, bf16),
        "cache": pltpu.VMEM(suffix_cache.shape, bf16),
        "row_q": pltpu.VMEM((suffix_rows * heads, HD), f32),
        "row_out": pltpu.VMEM((suffix_rows * heads, HD), f32),
        "row_piece": pltpu.VMEM((suffix_rows, heads * HD), bf16),
        "q_rows": pltpu.VMEM((subsets, part_samples, heads * HD), bf16),
        "placed": pltpu.VMEM((subsets, part_samples, heads * HD), bf16),
        "placed_lse": pltpu.VMEM((keys, subsets, part_samples, heads // keys), f32),
        "out_mine": pltpu.VMEM((subsets, n, part_samples, features), bf16),
        "lse_mine": pltpu.VMEM((subsets, n, 8, stat_lanes), f32),
        "out_in": pltpu.VMEM((subsets, n, part_samples, features), bf16),
        "lse_in": pltpu.VMEM((subsets, n, 8, stat_lanes), f32),
        "attn_rows": pltpu.VMEM((subsets, sub_rows, features), bf16),
        "state": pltpu.VMEM((n, 2, rows, width), bf16),
        "scaled": pltpu.VMEM((subsets, sub_rows, width), bf16),
        "squares": pltpu.VMEM((subsets, sub_rows, 128), f32),
        "squares_in": pltpu.VMEM((subsets, n_smp - 1, smp_rows, 128), f32),
        "gate_buf": pltpu.VMEM((slots, width, UNITS), bf16),
        "up_buf": pltpu.VMEM((slots, width, UNITS), bf16),
        "down_buf": pltpu.VMEM((tiles, units, tile), bf16),
        "part": pltpu.VMEM((all_steps, sub_rows, 2 * UNITS), bf16),
        "part_in": pltpu.VMEM((all_steps, n_smp - 1, smp_rows, 2 * UNITS), bf16),
        "hidden": pltpu.VMEM((subsets, sub_rows, units), bf16),
        "buf_a": pltpu.VMEM((all_tiles, 2, n, sub, tile), bf16),
        "recv_a": pltpu.VMEM((all_tiles, n, sub, tile), bf16),
        "buf_b": pltpu.VMEM((all_tiles, n, sub, tile), bf16),
        "from_left": pltpu.VMEM((all_tiles, n, sub, tile), bf16),
        "from_right": pltpu.VMEM((all_tiles, n, sub, tile), bf16),
        "kv_sem": dma,
        "cache_sem": dma((suffix_rows // min(8, suffix_rows),)),
        "w_sem": dma((tiles,)),
        "g_sem": dma((slots,)),
        "u_sem": dma((slots,)),
        "d_sem": dma((tiles,)),
    }
    scratch |= {name: dma((subsets, n)) for name in ("os", "orr", "ls", "lr")}
    scratch |= {name: dma((subsets, n_smp - 1)) for name in ("xs", "xr", "qs", "qr")}
    scratch |= {name: dma((all_steps, n_smp - 1)) for name in ("ps", "pr", "hs", "hr")}
    scratch |= {name: dma((all_tiles,)) for name in ("sa", "ra")}
    scratch |= {
        name: dma((all_tiles, n)) for name in ("ss", "rl", "rr", "gsr", "gsl", "gr", "fs", "fr")
    }
    operands = {
        "ids": (ids, vmem),
        "lengths": (lengths, vmem),
        "q": (queries, vmem),
        "kv_hbm": (prefix_cache, hbm),
        "cache_hbm": (suffix_cache, hbm),
        "w_hbm": (w, hbm),
        "res": (residual, vmem),
        "gain": (gain, vmem),
        "gate_hbm": (gate, hbm),
        "up_hbm": (up, hbm),
        "down_hbm": (down, hbm),
    }
    names = (*operands, "mixed", *scratch)
    return pl.pallas_call(
        functools.partial(layer_kernel, n, n_smp, names),
        out_shape=jax.ShapeDtypeStruct((rows, width), bf16),
        in_specs=[spec for _, spec in operands.values()],
        out_specs=vmem,
        scratch_shapes=list(scratch.values()),
        compiler_params=pltpu.CompilerParams(
            collective_id=0, has_side_effects=True, vmem_limit_bytes=VMEM_BYTES
        ),
    )(*[value for value, _ in operands.values()])


def on_device(
    queries,
    prefix_cache,
    suffix_cache,
    suffix_length,
    cache_sample,
    residual,
    w_out,
    norm_gain,
    gate_matrix,
    w_up,
    w_down,
):
    n, n_smp = lax.axis_size("ctx"), lax.axis_size("smp")
    return layer(
        n,
        n_smp,
        cache_sample[None, :],
        suffix_length[None, :],
        queries[:, 0],
        prefix_cache[:, :, 0],
        suffix_cache[:, :, :, 0],
        w_out[0],
        residual,
        norm_gain[None, :],
        gate_matrix,
        w_up,
        w_down,
    )


def solution(mesh):
    in_specs = (
        P(("group", "smp"), "head", None),
        P(None, ("group", "ctx"), "head", None),
        P(None, ("group", "ctx", "smp"), None, "head", None),
        P(("group", "smp")),
        P("group"),
        P(("group", "ctx", "head"), "smp"),
        P("head", "ctx", "smp"),
        P("smp"),
        P("smp", ("ctx", "head")),
        P("smp", ("ctx", "head")),
        P(("ctx", "head"), "smp"),
    )
    out_specs = P(("group", "ctx", "head"), "smp")
    return jax.shard_map(
        on_device, mesh=mesh, in_specs=in_specs, out_specs=out_specs, check_vma=False
    )
```

```python
import functools
import types

import jax
import jax.numpy as jnp
from jax import lax
from jax.experimental import pallas as pl
from jax.experimental.pallas import tpu as pltpu
from jax.sharding import PartitionSpec as P

D = 8192
QUERY_HEADS = 64
KEY_VALUE_HEADS = 8
HD = 128


EPSILON = 1e-05


MESH = pl.DeviceIdType.MESH
TILE = 1024
UNITS = 256
SLOTS = 3
SUB = 16
VMEM_BYTES = 67043328


def remote(src, dst, send_sem, recv_sem, where):
    return pltpu.make_async_remote_copy(
        src_ref=src,
        dst_ref=dst,
        send_sem=send_sem,
        recv_sem=recv_sem,
        device_id=where,
        device_id_type=MESH,
    )


def announce(n, n_smp, c, s, h):
    barrier = pltpu.get_barrier_semaphore()
    for k in range(1, n):
        pl.semaphore_signal(barrier, inc=1, device_id={"ctx": lax.rem(c + k, n)}, device_id_type=MESH)
    for k in range(1, n_smp):
        pl.semaphore_signal(
            barrier, inc=1, device_id={"smp": lax.rem(s + k, n_smp)}, device_id_type=MESH
        )
    pl.semaphore_signal(barrier, inc=1, device_id={"head": 1 - h}, device_id_type=MESH)


def gather_round(n, n_smp):
    pl.semaphore_wait(pltpu.get_barrier_semaphore(), (n - 1) + (n_smp - 1) + 1)


class Line:
    def __init__(self, n, c, h, buf_a, recv_a, buf_b, from_left, from_right, sa, ra, ss, rl, rr):
        self.n, self.c, self.h = n, c, h
        self.buf_a, self.recv_a, self.buf_b = buf_a, recv_a, buf_b
        self.from_left, self.from_right = from_left, from_right
        self.sa, self.ra, self.ss, self.rl, self.rr = sa, ra, ss, rl, rr
        self.tiles = buf_a.shape[0]

        @pl.when(c == 0)
        def _():
            from_left[:, 0] = jnp.zeros(from_left.shape[:1] + from_left.shape[2:], from_left.dtype)

        @pl.when(c == n - 1)
        def _():
            from_right[:, n - 1] = jnp.zeros(
                from_right.shape[:1] + from_right.shape[2:], from_right.dtype
            )

    def pair_copy(self, t):
        return remote(
            self.buf_a.at[t, 1 - self.h],
            self.recv_a.at[t],
            self.sa.at[t],
            self.ra.at[t],
            {"head": 1 - self.h},
        )

    def to_right(self, t, d):
        return remote(
            self.buf_b.at[t, d],
            self.from_left.at[t, d],
            self.ss.at[t, d],
            self.rl.at[t, d],
            {"ctx": lax.rem(self.c + 1, self.n)},
        )

    def to_left(self, t, d):
        return remote(
            self.buf_b.at[t, d],
            self.from_right.at[t, d],
            self.ss.at[t, d],
            self.rr.at[t, d],
            {"ctx": lax.rem(self.c + self.n - 1, self.n)},
        )

    def give(self, t, value):
        _, _, n, rows, width = self.buf_a.shape
        parts = value.reshape(n, 2, rows, width).astype(jnp.bfloat16)
        self.buf_a[t, 0] = parts[:, 0]
        self.buf_a[t, 1] = parts[:, 1]
        self.pair_copy(t).start()

    def middle(self, t):
        self.pair_copy(t).wait()
        both = self.buf_a[t, self.h].astype(jnp.float32) + self.recv_a[t].astype(jnp.float32)
        self.buf_b[t] = both.astype(jnp.bfloat16)

    def hop(self, t, inside, d, copy_of, arrived, first):
        @pl.when(inside)
        def _():
            @pl.when(jnp.logical_not(first))
            def _():
                copy_of(t, d).wait_recv()
                both = self.buf_b[t, d].astype(jnp.float32) + arrived[t, d].astype(jnp.float32)
                self.buf_b[t, d] = both.astype(jnp.bfloat16)

            copy_of(t, d).start()

    def step(self, i, tile_at):
        n, c = self.n, self.c
        live, t = tile_at(i - 1)

        @pl.when(live)
        def _():
            self.middle(t)

        live_r, t_r = tile_at(i - 1 - c)
        live_l, t_l = tile_at(i - n + c)
        for e in range(n - 1):
            right, left = n - 1 - e, e
            self.hop(t_r, live_r & (right > c), right, self.to_right, self.from_left, c == 0)
            self.hop(t_l, live_l & (left < c), left, self.to_left, self.from_right, c == n - 1)

    def finish(self, t):
        n, c = self.n, self.c

        @pl.when(c > 0)
        def _():
            self.to_right(t, c).wait_recv()

        @pl.when(c < n - 1)
        def _():
            self.to_left(t, c).wait_recv()

        return (
            self.buf_b[t, c].astype(jnp.float32)
            + self.from_left[t, c].astype(jnp.float32)
            + self.from_right[t, c].astype(jnp.float32)
        )

    def drain(self, t):
        for d in range(self.n):

            @pl.when(d > self.c)
            def _():
                self.to_right(t, d).wait_send()

            @pl.when(d < self.c)
            def _():
                self.to_left(t, d).wait_send()


def columns(t, width):
    return pl.ds(pl.multiple_of(t * width, width), width)


def suffix_pieces(
    ids_ref, lengths_ref, sub, q_ref, block_copy, cache, row_q, row_out, row_piece, placed, placed_lse
):
    _, rows, positions_here, width = cache.shape
    subsets, part_samples, features = q_ref.shape
    samples = subsets * part_samples
    keys, _, _, per_key = placed_lse.shape
    heads = features // HD
    block = min(8, rows)
    all_ids = ids_ref[...]
    group_rows = all_ids.shape[1]
    n_smp = lax.axis_size("smp")
    own_first = (lax.axis_index("ctx") * n_smp + lax.axis_index("smp")) * rows
    turned = pltpu.roll(all_ids, lax.rem(group_rows - own_first, group_rows), 1)
    ids = turned[:, :128] - lax.axis_index("smp") * samples
    ids = jnp.where(lax.broadcasted_iota(jnp.int32, ids.shape, 1) < rows, ids, -1)
    sample_at = lax.broadcasted_iota(jnp.int32, (samples, ids.shape[1]), 0)
    picked = (sample_at == ids).astype(jnp.float32).T[:rows]
    lengths = jnp.sum(picked * lengths_ref[...].astype(jnp.float32), axis=1, keepdims=True)
    lengths = lengths.astype(jnp.int32)
    spot = ids // sub % subsets * part_samples + ids // (sub * subsets) * sub + ids % sub
    chosen = (sample_at == jnp.where(ids < 0, -1, spot)).astype(jnp.float32)
    picked = chosen.T[:rows].astype(jnp.bfloat16)
    all_q = q_ref[...].reshape(samples, features)
    for j in range(keys):
        lanes = slice(j * per_key * HD, (j + 1) * per_key * HD)
        own = jnp.dot(picked, all_q[:, lanes], preferred_element_type=jnp.float32)
        for g in range(per_key):
            row_q[pl.ds(j * per_key + g, rows, stride=heads), :] = own[:, g * HD : (g + 1) * HD]

    same = (
        lax.broadcasted_iota(jnp.int32, (heads, width), 0) // per_key
        == lax.broadcasted_iota(jnp.int32, (heads, width), 1) // HD
    )
    positions = lax.broadcasted_iota(jnp.int32, (heads, positions_here), 1)
    lanes_at = lax.broadcasted_iota(jnp.int32, (heads, ids.shape[1]), 1)
    table = jnp.zeros((heads, ids.shape[1]), jnp.float32)
    scores = []
    for r0 in range(0, rows, block):
        block_copy(r0 // block).wait()
        for r in range(r0, r0 + block):
            q = row_q[r * heads : (r + 1) * heads]
            spread = jnp.concatenate([q] * keys, axis=1)
            spread = jnp.where(same, spread, 0.0).astype(jnp.bfloat16)
            one = lax.dot_general(
                spread, cache[0, r], (((1,), (1,)), ((), ())), preferred_element_type=jnp.float32
            )
            live = positions < lengths[r : r + 1]
            scores.append(jnp.where(live, one * HD ** (-0.5), -jnp.inf))
    for r0 in range(0, rows, block):
        group = jnp.concatenate(scores[r0 : r0 + block], axis=0)
        high = jnp.max(group, axis=1, keepdims=True)
        weights = jnp.exp(group - high)
        total = jnp.sum(weights, axis=1, keepdims=True)
        lse = high + jnp.log(total)
        weights = weights.astype(jnp.bfloat16)
        for r in range(r0, r0 + block):
            part = slice((r - r0) * heads, (r - r0 + 1) * heads)
            summed = jnp.dot(weights[part], cache[1, r], preferred_element_type=jnp.float32)
            own = jnp.concatenate(
                [
                    summed[j * per_key : (j + 1) * per_key, j * HD : (j + 1) * HD]
                    for j in range(keys)
                ],
                axis=0,
            )
            piece = (own / total[part]).astype(jnp.bfloat16)
            row_out[r * heads : (r + 1) * heads] = piece.astype(jnp.float32)
            table = jnp.where(lanes_at == r, lse[part], table)

    found = jnp.sum(chosen, axis=1, keepdims=True) > 0.0
    for k in range(heads):
        row_piece[:, k * HD : (k + 1) * HD] = row_out[pl.ds(k, rows, stride=heads), :].astype(
            jnp.bfloat16
        )
    to_sample = chosen[:, :rows].astype(jnp.bfloat16)
    for j in range(keys):
        lanes = slice(j * per_key * HD, (j + 1) * per_key * HD)
        one = jnp.dot(to_sample, row_piece[:, lanes], preferred_element_type=jnp.float32)
        placed[:, :, lanes] = one.astype(jnp.bfloat16).reshape(subsets, part_samples, -1)
        one = lax.dot_general(
            chosen,
            table[j * per_key : (j + 1) * per_key],
            (((1,), (1,)), ((), ())),
            precision=lax.Precision.HIGHEST,
            preferred_element_type=jnp.float32,
        )
        one = jnp.where(found, one, -1e30)
        placed_lse[j] = one.reshape(subsets, part_samples, per_key)


def layer_kernel(n, n_smp, names, *refs):
    r = types.SimpleNamespace(**dict(zip(names, refs, strict=True)))
    c, s, h = lax.axis_index("ctx"), lax.axis_index("smp"), lax.axis_index("head")
    kv_ref, state = r.kv, r.state
    out_mine, lse_mine, out_in, lse_in = r.out_mine, r.lse_mine, r.out_in, r.lse_in
    keys, _, samples, per_key = r.placed_lse.shape
    per_dest = out_mine.shape[3] // HD
    dests = per_key // per_dest
    together = max(1, min(per_key, 512 // samples))
    stat_lanes = lse_mine.shape[3]
    slots, width, _ = r.gate_buf.shape
    tiles, units, tile = r.down_buf.shape
    subsets, sub_rows, _ = r.scaled.shape
    sub = state.shape[2] // subsets
    smp_rows = sub_rows // n_smp
    steps = units // UNITS
    all_steps, all_tiles = subsets * steps, subsets * tiles
    ratio = max(1, steps // tiles)
    w_rows = r.w_hbm.shape[0]
    per_slot = units // w_rows
    w_slots = -(-tiles // per_slot)
    block = min(8, r.cache.shape[1])

    def block_copy(i):
        rows_at = pl.ds(i * block, block)
        return pltpu.make_async_copy(
            r.cache_hbm.at[:, rows_at], r.cache.at[:, rows_at], r.cache_sem.at[i]
        )

    def w_block(t):
        first_row = pl.multiple_of(lax.rem(t, per_slot) * w_rows, w_rows)
        return r.down_buf.at[lax.div(t, per_slot), pl.ds(first_row, w_rows)]

    def w_copy(t):
        return pltpu.make_async_copy(r.w_hbm.at[:, columns(t, tile)], w_block(t), r.w_sem.at[t])

    def weight_copies(i):
        slot, t = lax.rem(i, slots), lax.rem(i, steps)
        return (
            pltpu.make_async_copy(
                r.gate_hbm.at[:, columns(t, UNITS)], r.gate_buf.at[slot], r.g_sem.at[slot]
            ),
            pltpu.make_async_copy(
                r.up_hbm.at[:, columns(t, UNITS)], r.up_buf.at[slot], r.u_sem.at[slot]
            ),
        )

    def down_copy(t):
        return pltpu.make_async_copy(
            r.down_hbm.at[:, columns(t, tile)], r.down_buf.at[t], r.d_sem.at[t]
        )

    for i in range(r.cache.shape[1] // block):
        block_copy(i).start()
    kv_copy = pltpu.make_async_copy(r.kv_hbm, kv_ref, r.kv_sem)
    kv_copy.start()
    announce(n, n_smp, c, s, h)

    by_owner = r.q[...].reshape(samples // sub, subsets, sub, r.q.shape[1])
    for k in range(subsets):
        r.q_rows[k] = by_owner[:, k].reshape(samples, r.q.shape[1])

    suffix_pieces(
        r.ids,
        r.lengths,
        sub,
        r.q_rows,
        block_copy,
        r.cache,
        r.row_q,
        r.row_out,
        r.row_piece,
        r.placed,
        r.placed_lse,
    )
    kv_copy.wait()

    @pl.loop(0, tiles)
    def _(t):
        w_copy(t).start()

    @pl.loop(0, min(slots, all_steps))
    def _(t):
        for copy in weight_copies(t):
            copy.start()

    for t in range(w_slots, tiles):
        down_copy(t).start()
    gather_round(n, n_smp)

    lanes_at = lax.broadcasted_iota(jnp.int32, (samples, 128), 1)

    def piece_copies(k, at, d):
        return (
            remote(
                out_mine.at[k, d], out_in.at[k, at], r.os.at[k, d], r.orr.at[k, at], {"ctx": d}
            ),
            remote(
                lse_mine.at[k, d], lse_in.at[k, at], r.ls.at[k, d], r.lr.at[k, at], {"ctx": d}
            ),
        )

    def prefix_piece(k, i):
        j = lax.rem(lax.div(c, dests) + 1 + i, keys)
        key = kv_ref[0, :, columns(j, HD)]
        value = kv_ref[1, :, columns(j, HD)]
        own = r.q_rows[k, :, columns(j, per_key * HD)]
        placed = r.placed[k, :, columns(j, per_key * HD)]
        placed_lse = r.placed_lse[j, k]
        tables = [jnp.zeros((samples, 128), jnp.float32) for _ in range(dests)]
        for g0 in range(0, per_key, together):
            rows = jnp.concatenate(
                [own[:, g * HD : (g + 1) * HD] for g in range(g0, g0 + together)], axis=0
            )
            scores = lax.dot_general(
                rows, key, (((1,), (1,)), ((), ())), preferred_element_type=jnp.float32
            ) * HD ** (-0.5)
            high = jnp.max(scores, axis=1, keepdims=True)
            weights = jnp.exp(scores - high)
            total = jnp.sum(weights, axis=1, keepdims=True)
            summed = (
                jnp.dot(weights.astype(jnp.bfloat16), value, preferred_element_type=jnp.float32)
                / total
            )
            lse = high + jnp.log(total)
            for g in range(g0, g0 + together):
                part = slice((g - g0) * samples, (g - g0 + 1) * samples)
                own_lse, other_lse = lse[part], placed_lse[:, g : g + 1]
                top = jnp.maximum(own_lse, other_lse)
                own_weight = jnp.exp(own_lse - top)
                other_weight = jnp.exp(other_lse - top)
                both = own_weight + other_weight
                merged = (
                    own_weight * summed[part]
                    + other_weight * placed[:, g * HD : (g + 1) * HD].astype(jnp.float32)
                ) / both
                at = g % per_dest
                out_mine[k, j * dests + g // per_dest, :, at * HD : (at + 1) * HD] = merged.astype(
                    jnp.bfloat16
                )
                q = g // per_dest
                tables[q] = jnp.where(lanes_at == at, top + jnp.log(both), tables[q])
        for q in range(dests):
            d = j * dests + q
            table = tables[q]
            if stat_lanes > samples:
                rest_of = jnp.zeros((stat_lanes - samples, 128), jnp.float32)
                table = jnp.concatenate([table, rest_of], axis=0)
            lse_mine[k, d] = table.T[:8]

            @pl.when(d != c)
            def _():
                for copy in piece_copies(k, c, d):
                    copy.start()

    def attn_copy(k, m):
        at = r.attn_rows.at[k, pl.ds(pl.multiple_of(s * samples, samples), samples)]
        return remote(
            at, at, r.xs.at[k, m - 1], r.xr.at[k, m - 1], {"smp": lax.rem(s + m, n_smp)}
        )

    def merge_pieces(k):
        for m in range(1, n):
            d = lax.rem(c + m, n)
            for copy in piece_copies(k, d, d):
                copy.wait_recv()
        lses = [lse_mine[k, c]] + [lse_in[k, lax.rem(c + m, n)] for m in range(1, n)]
        peak = functools.reduce(jnp.maximum, lses)
        scales = [jnp.exp(value - peak) for value in lses]
        denom = functools.reduce(jnp.add, scales)
        blank = jnp.zeros((120, stat_lanes), jnp.float32)
        scales = [
            jnp.concatenate([value / denom, blank], axis=0).T[:samples] for value in scales
        ]
        for j in range(per_dest):
            lanes = slice(j * HD, (j + 1) * HD)
            total = scales[0][:, j : j + 1] * out_mine[k, c, :, lanes].astype(jnp.float32)
            for m in range(1, n):
                piece = out_in[k, lax.rem(c + m, n), :, lanes].astype(jnp.float32)
                total = total + scales[m][:, j : j + 1] * piece
            at = pl.ds(pl.multiple_of(s * samples, samples), samples)
            r.attn_rows[k, at, lanes] = total.astype(jnp.bfloat16)
        for m in range(1, n_smp):
            attn_copy(k, m).start()

    def finish_attn(k):
        for m in range(1, n_smp):
            attn_copy(k, m).wait()
        for m in range(1, n):
            d = lax.rem(c + m, n)
            for copy in piece_copies(k, c, d):
                copy.wait_send()

    @pl.loop(0, keys)
    def _(i):
        prefix_piece(0, i)

    early = keys // 2 if subsets > 1 else 0
    gap = 0
    period = tiles + gap
    if subsets > 1:

        @pl.loop(0, early)
        def _(i):
            prefix_piece(1, i)

    merge_pieces(0)
    if subsets > 1:

        @pl.loop(early, keys)
        def _(i):
            prefix_piece(1, i)

    finish_attn(0)

    line = Line(
        n,
        c,
        h,
        r.buf_a,
        r.recv_a,
        r.buf_b,
        r.from_left,
        r.from_right,
        r.sa,
        r.ra,
        r.ss,
        r.rl,
        r.rr,
    )

    def rows_of(k):
        return pl.ds(pl.multiple_of(k * sub, sub), sub)

    def gather_copy(j, q, way, sems):
        k, t = lax.div(j, tiles), lax.rem(j, tiles)
        at = state.at[q, h, rows_of(k), columns(t, tile)]
        return remote(at, at, sems.at[j, q], r.gr.at[j, q], {"ctx": lax.rem(c + way, n)})

    def pass_copy(j, q):
        k, t = lax.div(j, tiles), lax.rem(j, tiles)
        at = state.at[q, h, rows_of(k), columns(t, tile)]
        return remote(at, at, r.fs.at[j, q], r.fr.at[j, q], {"head": 1 - h})

    def spread(j, q, right, left):
        @pl.when(right & (c < n - 1))
        def _():
            gather_copy(j, q, 1, r.gsr).start()

        @pl.when(left & (c > 0))
        def _():
            gather_copy(j, q, n - 1, r.gsl).start()

        pass_copy(j, q).start()

    def state_tile(i):
        at = lax.max(i, 0)
        k, t = lax.div(at, period), lax.rem(at, period)
        return (i >= 0) & (k < subsets) & (t < tiles), k * tiles + t

    def mixed_tile(i):
        return (i >= 0) & (i < all_tiles), i

    def project(i):
        live, j = state_tile(i)

        @pl.when(live)
        def _():
            k, t = lax.div(j, tiles), lax.rem(j, tiles)

            @pl.when(k == 0)
            def _():
                w_copy(t).wait()

            line.give(
                j, jnp.dot(r.attn_rows[k], w_block(t)[...], preferred_element_type=jnp.float32)
            )

        line.step(i, state_tile)
        ready, done = state_tile(i - n)

        @pl.when(ready)
        def _():
            j = done
            k, t = lax.div(j, tiles), lax.rem(j, tiles)
            own = line.finish(j) + r.res[rows_of(k), columns(t, tile)].astype(jnp.float32)
            state[c, h, rows_of(k), columns(t, tile)] = own.astype(jnp.bfloat16)
            spread(j, c, c >= 0, c >= 0)

        for q in range(n):
            here, moved = state_tile(i - n - lax.max(c - q, q - c))

            @pl.when((q != c) & here)
            def _():
                gather_copy(moved, q, 1, r.gsr).wait_recv()
                spread(moved, q, q < c, q > c)

    def smp_rows_of(p):
        return pl.ds(pl.multiple_of(p * smp_rows, smp_rows), smp_rows)

    def square_copy(k, m):
        p = lax.rem(s + m, n_smp)
        return remote(
            r.squares.at[k, smp_rows_of(p)],
            r.squares_in.at[k, m - 1],
            r.qs.at[k, m - 1],
            r.qr.at[k, m - 1],
            {"smp": p},
        )

    def prepare(k):
        @pl.loop(k * tiles, (k + 1) * tiles)
        def _(j):
            for q in range(n):
                pass_copy(j, q).wait()

        for owner in range(n):
            for core in range(2):
                wide = state[owner, core, rows_of(k)].astype(jnp.float32)
                first_row = (2 * owner + core) * sub
                rows = slice(first_row, first_row + sub)
                r.scaled[k, rows] = (wide * r.gain[...]).astype(jnp.bfloat16)
                sums = jnp.sum(wide * wide, axis=1, keepdims=True)
                r.squares[k, rows] = jnp.broadcast_to(sums, (sub, 128))
        for m in range(1, n_smp):
            square_copy(k, m).start()

    def part_copy(i, m):
        p = lax.rem(s + m, n_smp)
        return remote(
            r.part.at[i, smp_rows_of(p)],
            r.part_in.at[i, m - 1],
            r.ps.at[i, m - 1],
            r.pr.at[i, m - 1],
            {"smp": p},
        )

    def hidden_copy(i, m):
        k, t = lax.div(i, steps), lax.rem(i, steps)
        at = r.hidden.at[k, smp_rows_of(s), columns(t, UNITS)]
        return remote(
            at, at, r.hs.at[i, m - 1], r.hr.at[i, m - 1], {"smp": lax.rem(s + m, n_smp)}
        )

    def act(i):
        k, t = lax.div(i, steps), lax.rem(i, steps)

        @pl.when(t == 0)
        def _():
            for m in range(1, n_smp):
                square_copy(k, m).wait()

        both = r.part[i, smp_rows_of(s)].astype(jnp.float32)
        for m in range(1, n_smp):
            part_copy(i, m).wait()
            both = both + r.part_in[i, m - 1].astype(jnp.float32)
        total = r.squares[k, smp_rows_of(s)]
        for m in range(1, n_smp):
            total = total + r.squares_in[k, m - 1]
        factor = lax.rsqrt(total / (width * n_smp) + EPSILON)[:, :1]
        gate = factor * both[:, :UNITS]
        up = factor * both[:, UNITS:]
        value = gate / (1.0 + jnp.exp(-gate)) * up
        r.hidden[k, smp_rows_of(s), columns(t, UNITS)] = value.astype(jnp.bfloat16)
        for m in range(1, n_smp):
            hidden_copy(i, m).start()

    def gate_up(i):
        k, t = lax.div(i, steps), lax.rem(i, steps)

        @pl.when(t == 0)
        def _():
            prepare(k)

        for copy in weight_copies(i):
            copy.wait()
        slot = lax.rem(i, slots)
        r.part[i, :, :UNITS] = jnp.dot(
            r.scaled[k], r.gate_buf[slot], preferred_element_type=jnp.float32
        ).astype(jnp.bfloat16)
        r.part[i, :, UNITS:] = jnp.dot(
            r.scaled[k], r.up_buf[slot], preferred_element_type=jnp.float32
        ).astype(jnp.bfloat16)
        for m in range(1, n_smp):
            part_copy(i, m).start()

        @pl.when(i + slots < all_steps)
        def _():
            for copy in weight_copies(i + slots):
                copy.start()

    def down(j):
        k, t = lax.div(j, tiles), lax.rem(j, tiles)

        @pl.when(t == 0)
        def _():
            @pl.loop(0, steps)
            def _(u):
                for m in range(1, n_smp):
                    hidden_copy(k * steps + u, m).wait()

        @pl.when(k == 0)
        def _():
            down_copy(t).wait()

        line.drain(j)
        line.give(j, jnp.dot(r.hidden[k], r.down_buf[t], preferred_element_type=jnp.float32))

    def emit(j):
        k, t = lax.div(j, tiles), lax.rem(j, tiles)
        value = line.finish(j) + state[c, h, rows_of(k), columns(t, tile)].astype(jnp.float32)
        r.mixed[rows_of(k), columns(t, tile)] = value.astype(jnp.bfloat16)

    ahead = tiles + 2 * n - 1
    rest = period * (subsets - 1)
    free_at = max(0, period * (subsets - 1) + tiles - ahead)
    merge_at = max(0, period - 2)

    @pl.loop(0, ahead)
    def _(i):
        if subsets > 1:

            @pl.when(i == period)
            def _():
                finish_attn(1)

        project(i)
        if subsets > 1:

            @pl.when(i == merge_at)
            def _():
                merge_pieces(1)

    lag = min(2, all_steps)
    first = max(steps + lag + 1, rest)

    @pl.loop(0, first + (all_tiles + n) * ratio)
    def _(i):
        @pl.when(i < all_steps)
        def _():
            gate_up(i)

        @pl.when(i < rest)
        def _():
            project(i + ahead)

        @pl.when(i == free_at)
        def _():
            for t in range(w_slots):
                down_copy(t).start()

        @pl.when((i >= lag) & (i < all_steps + lag))
        def _():
            act(i - lag)

        j = lax.div(i - first, ratio)

        @pl.when((i >= first) & (lax.rem(i - first, ratio) == 0))
        def _():
            @pl.when(j < all_tiles)
            def _():
                down(j)

            line.step(j, mixed_tile)

            @pl.when(j >= n)
            def _():
                emit(j - n)

    @pl.loop(0, all_tiles)
    def _(j):
        line.drain(j)
        for q in range(n):

            @pl.when((q <= c) & (c < n - 1))
            def _():
                gather_copy(j, q, 1, r.gsr).wait_send()

            @pl.when((q >= c) & (c > 0))
            def _():
                gather_copy(j, q, n - 1, r.gsl).wait_send()


def layer(
    n, n_smp, ids, lengths, queries, prefix_cache, suffix_cache, w, residual, gain, gate, up, down
):
    samples, heads = queries.shape[0], queries.shape[1] // HD
    keys = prefix_cache.shape[2] // HD
    suffix_rows = suffix_cache.shape[1]
    features = queries.shape[1] // n
    rows, width = residual.shape
    sub = SUB if rows % SUB == 0 else rows
    subsets = rows // sub
    part_samples = samples // subsets
    stat_lanes = -(-part_samples // 128) * 128
    sub_rows = n * 2 * sub
    smp_rows = sub_rows // n_smp
    units = gate.shape[1]
    steps = units // UNITS
    tile = max(TILE, width // steps)
    tiles = width // tile
    all_steps, all_tiles = subsets * steps, subsets * tiles
    slots = min(SLOTS, all_steps)
    vmem = pl.BlockSpec(memory_space=pltpu.VMEM)
    hbm = pl.BlockSpec(memory_space=pl.ANY)
    dma = pltpu.SemaphoreType.DMA
    bf16, f32 = jnp.bfloat16, jnp.float32
    scratch = {
        "kv": pltpu.VMEM(prefix_cache.shape, bf16),
        "cache": pltpu.VMEM(suffix_cache.shape, bf16),
        "row_q": pltpu.VMEM((suffix_rows * heads, HD), f32),
        "row_out": pltpu.VMEM((suffix_rows * heads, HD), f32),
        "row_piece": pltpu.VMEM((suffix_rows, heads * HD), bf16),
        "q_rows": pltpu.VMEM((subsets, part_samples, heads * HD), bf16),
        "placed": pltpu.VMEM((subsets, part_samples, heads * HD), bf16),
        "placed_lse": pltpu.VMEM((keys, subsets, part_samples, heads // keys), f32),
        "out_mine": pltpu.VMEM((subsets, n, part_samples, features), bf16),
        "lse_mine": pltpu.VMEM((subsets, n, 8, stat_lanes), f32),
        "out_in": pltpu.VMEM((subsets, n, part_samples, features), bf16),
        "lse_in": pltpu.VMEM((subsets, n, 8, stat_lanes), f32),
        "attn_rows": pltpu.VMEM((subsets, sub_rows, features), bf16),
        "state": pltpu.VMEM((n, 2, rows, width), bf16),
        "scaled": pltpu.VMEM((subsets, sub_rows, width), bf16),
        "squares": pltpu.VMEM((subsets, sub_rows, 128), f32),
        "squares_in": pltpu.VMEM((subsets, n_smp - 1, smp_rows, 128), f32),
        "gate_buf": pltpu.VMEM((slots, width, UNITS), bf16),
        "up_buf": pltpu.VMEM((slots, width, UNITS), bf16),
        "down_buf": pltpu.VMEM((tiles, units, tile), bf16),
        "part": pltpu.VMEM((all_steps, sub_rows, 2 * UNITS), bf16),
        "part_in": pltpu.VMEM((all_steps, n_smp - 1, smp_rows, 2 * UNITS), bf16),
        "hidden": pltpu.VMEM((subsets, sub_rows, units), bf16),
        "buf_a": pltpu.VMEM((all_tiles, 2, n, sub, tile), bf16),
        "recv_a": pltpu.VMEM((all_tiles, n, sub, tile), bf16),
        "buf_b": pltpu.VMEM((all_tiles, n, sub, tile), bf16),
        "from_left": pltpu.VMEM((all_tiles, n, sub, tile), bf16),
        "from_right": pltpu.VMEM((all_tiles, n, sub, tile), bf16),
        "kv_sem": dma,
        "cache_sem": dma((suffix_rows // min(8, suffix_rows),)),
        "w_sem": dma((tiles,)),
        "g_sem": dma((slots,)),
        "u_sem": dma((slots,)),
        "d_sem": dma((tiles,)),
    }
    scratch |= {name: dma((subsets, n)) for name in ("os", "orr", "ls", "lr")}
    scratch |= {name: dma((subsets, n_smp - 1)) for name in ("xs", "xr", "qs", "qr")}
    scratch |= {name: dma((all_steps, n_smp - 1)) for name in ("ps", "pr", "hs", "hr")}
    scratch |= {name: dma((all_tiles,)) for name in ("sa", "ra")}
    scratch |= {
        name: dma((all_tiles, n)) for name in ("ss", "rl", "rr", "gsr", "gsl", "gr", "fs", "fr")
    }
    operands = {
        "ids": (ids, vmem),
        "lengths": (lengths, vmem),
        "q": (queries, vmem),
        "kv_hbm": (prefix_cache, hbm),
        "cache_hbm": (suffix_cache, hbm),
        "w_hbm": (w, hbm),
        "res": (residual, vmem),
        "gain": (gain, vmem),
        "gate_hbm": (gate, hbm),
        "up_hbm": (up, hbm),
        "down_hbm": (down, hbm),
    }
    names = (*operands, "mixed", *scratch)
    return pl.pallas_call(
        functools.partial(layer_kernel, n, n_smp, names),
        out_shape=jax.ShapeDtypeStruct((rows, width), bf16),
        in_specs=[spec for _, spec in operands.values()],
        out_specs=vmem,
        scratch_shapes=list(scratch.values()),
        compiler_params=pltpu.CompilerParams(
            collective_id=0, has_side_effects=True, vmem_limit_bytes=VMEM_BYTES
        ),
    )(*[value for value, _ in operands.values()])


def on_device(
    queries,
    prefix_cache,
    suffix_cache,
    suffix_length,
    cache_sample,
    residual,
    w_out,
    norm_gain,
    gate_matrix,
    w_up,
    w_down,
):
    n, n_smp = lax.axis_size("ctx"), lax.axis_size("smp")
    return layer(
        n,
        n_smp,
        cache_sample[None, :],
        suffix_length[None, :],
        queries[:, 0],
        prefix_cache[:, :, 0],
        suffix_cache[:, :, :, 0],
        w_out[0],
        residual,
        norm_gain[None, :],
        gate_matrix,
        w_up,
        w_down,
    )


def solution(mesh):
    in_specs = (
        P(("group", "smp"), "head", None),
        P(None, ("group", "ctx"), "head", None),
        P(None, ("group", "ctx", "smp"), None, "head", None),
        P(("group", "smp")),
        P("group"),
        P(("group", "ctx", "head"), "smp"),
        P("head", "ctx", "smp"),
        P("smp"),
        P("smp", ("ctx", "head")),
        P("smp", ("ctx", "head")),
        P(("ctx", "head"), "smp"),
    )
    out_specs = P(("group", "ctx", "head"), "smp")
    return jax.shard_map(
        on_device, mesh=mesh, in_specs=in_specs, out_specs=out_specs, check_vma=False
    )
```
